512 devices in a mesh: gx: 4 (over x), rest: 128 (over y, z, core).
Axes of the slice: x: 4, y: 8, z: 8, core: 2. Of those that a mesh axis runs over, the one named last changes fastest.
Arguments:
- tensor: float32 [512, 672, 672], P('rest', 'gx'), as said below
- basis: float32 [672, 128], P('gx'), may hold values from -0.25 to 0.25
Outputs:
- gram_one: float32 [672, 672], P('gx')
- core: float32 [128, 512, 672], P('gx', 'rest')
- gram_two: float32 [672, 672], replicated
The draws below stay inside these ranges and needn't reach their ends.
Inputs may be any that keep to these rules, and one draw needn't show every extreme that they name: `tensor`: Real-valued field samples.
All inputs are finite; a program needn't handle non-finite values.
Results may differ from the reference program's by a relative error of at most 0.000073.
Values sent between devices are 32-bit elements; how exact they have to be, the bound alone decides.
No kernel may reach another device: no remote copies, remote signals or barrier semaphores. Data moves between devices by JAX's collectives and lax.ppermute only.
A program may use at most 64 MiB of HBM per device.

```python
import jax
import jax.numpy as jnp
from jax import lax

I1 = 672
I2 = 672
RANK = 128
SLICES = 512


def draw_tensor(key, part):
    keys = jax.random.split(key, 5)
    low = jnp.log(0.3)
    high = jnp.log(3.0)
    slice_scale = jnp.sqrt(jnp.exp(jax.random.uniform(keys[0], (SLICES, 1, 1), jnp.float32, low, high)))
    row_scale = jnp.sqrt(jnp.exp(jax.random.uniform(keys[1], (1, I1, 1), jnp.float32, low, high)))
    column_scale = jnp.sqrt(jnp.exp(jax.random.uniform(keys[2], (1, 1, I2), jnp.float32, low, high)))
    noise = jax.random.normal(keys[3], (SLICES, I1, I2), jnp.float32)
    shared = 0.5 * jax.random.normal(keys[4], (SLICES, 1, I2), jnp.float32)
    return slice_scale * row_scale * column_scale * (noise + shared)


def levels(own_key, dims, pieces, smallest, top_value):
    level, own = 1.0, jax.random.fold_in(own_key, 6)
    for position, shards_of in pieces:
        heights = jnp.exp(jax.random.uniform(jax.random.fold_in(own, position), (shards_of,), jnp.float32, smallest / len(pieces), top_value / len(pieces)))
        level = level * jnp.repeat(heights, dims[position] // shards_of).reshape([-1 if axis == position else 1 for axis in range(len(dims))])
    return level


def scatter_about(rng, extent, deviation, bound, shards=(), dtype=jnp.bfloat16):
    values = deviation * jax.random.normal(rng, extent, jnp.float32)
    if shards:
        values = values * levels(rng, extent, shards, -0.22, 0.18)
    return jnp.clip(values, -bound, bound).astype(dtype)


def setup_inputs(seed: int = 0) -> dict:
    streams_of = jax.random.split(jax.random.key(seed), 3)
    return {
        "tensor": draw_tensor(jax.random.fold_in(streams_of[2], 71), 0),
        "basis": scatter_about(streams_of[1], (I1, RANK), I1 ** -0.5, 0.25, ((0, 4),), jnp.float32),
    }


def reference(tensor, basis):
    highest = lax.Precision.HIGHEST
    slices_all = tensor.shape[0]
    first_width = tensor.shape[1]
    second_width = tensor.shape[2]
    flatten = jnp.transpose(tensor, (1, 0, 2)).reshape(first_width, -1)
    gram_one = jnp.dot(flatten, flatten.T, precision=highest, preferred_element_type=jnp.float32) / (slices_all * second_width)
    core = jnp.einsum("ir,kij->rkj", basis, tensor, precision=highest)
    core_flat = core.reshape(-1, second_width)
    gram_two = jnp.dot(core_flat.T, core_flat, precision=highest, preferred_element_type=jnp.float32) / (slices_all * basis.shape[1])
    return gram_one, core, gram_two
```

```python
import functools

import jax
import jax.numpy as jnp
from jax import lax
from jax.experimental import pallas as pl
from jax.experimental.pallas import tpu as pltpu
from jax.sharding import Mesh, PartitionSpec as P

LANES = 128


def triangle(width):
    full = width // LANES
    left = width - full * LANES
    offsets, row = [], 0
    for block in range(full):
        offsets.append(row)
        row += (block + 1) * LANES
    tail = row
    row += left * (full + 1)
    return full, left, offsets, tail, row


def halves(value):
    high = value.astype(jnp.bfloat16)
    low = (value - high.astype(jnp.float32)).astype(jnp.bfloat16)
    return high, low


def product(left_high, left_low, right_high, right_low):
    def one(a, b):
        return lax.dot_general(a, b, (((1,), (1,)), ((), ())), preferred_element_type=jnp.float32)

    return one(left_high, right_high) + (one(left_high, right_low) + one(left_low, right_high))


def pack_gram(high_ref, low_ref, out_ref, base, width):
    full, left, offsets, tail, _ = triangle(width)
    for block in range(full):
        rows = (block + 1) * LANES
        mine = pl.ds(block * LANES, LANES)
        out_ref[pl.ds(base + offsets[block], rows), :] = product(
            high_ref[pl.ds(0, rows), :], low_ref[pl.ds(0, rows), :], high_ref[mine, :], low_ref[mine, :]
        )
    last = pl.ds(full * LANES, left)
    strip = product(high_ref[last, :], low_ref[last, :], high_ref[...], low_ref[...])
    for block in range(full):
        out_ref[pl.ds(base + tail + block * left, left), :] = strip[:, block * LANES : (block + 1) * LANES]
    corner = pl.ds(base + tail + full * left, left)
    out_ref[corner, :] = jnp.zeros((left, LANES), jnp.float32)
    out_ref[corner, 0:left] = strip[:, full * LANES :]


def gram_kernel(field_ref, basis_ref, packed_ref, core_ref, field_high, field_low, core_high, core_low):
    first, second = field_ref.shape
    rows_one = triangle(first)[-1]
    rows_two = triangle(second)[-1]
    high, low = halves(field_ref[...])
    field_high[...] = high
    field_low[...] = low
    basis_high, basis_low = halves(basis_ref[...].T)

    def one(a, b):
        return jnp.dot(a, b, preferred_element_type=jnp.float32)

    core = one(basis_high, high) + (one(basis_high, low) + one(basis_low, high))
    core_ref[...] = core
    high, low = halves(core.T)
    core_high[...] = high
    core_low[...] = low
    pack_gram(field_high, field_low, packed_ref, 0, first)
    pack_gram(core_high, core_low, packed_ref, rows_one, second)
    filled = rows_one + rows_two
    spare = packed_ref.shape[0] - filled
    if spare:
        packed_ref[pl.ds(filled, spare), :] = jnp.zeros((spare, LANES), jnp.float32)


def unpack(packed_ref, base, out_ref, width, scale):
    full, left, offsets, tail, _ = triangle(width)
    for block in range(full):
        columns = pl.ds(block * LANES, LANES)
        for row in range(block + 1):
            tile = packed_ref[pl.ds(base + offsets[block] + row * LANES, LANES), :] * scale
            out_ref[pl.ds(row * LANES, LANES), columns] = tile
            if row < block:
                out_ref[columns, pl.ds(row * LANES, LANES)] = tile.T
        tile = packed_ref[pl.ds(base + tail + block * left, left), :] * scale
        out_ref[pl.ds(full * LANES, left), columns] = tile
        out_ref[columns, pl.ds(full * LANES, left)] = tile.T
    corner = packed_ref[pl.ds(base + tail + full * left, left), :] * scale
    out_ref[pl.ds(full * LANES, left), pl.ds(full * LANES, left)] = corner[:, 0:left]


def unpack_kernel(scale_one, scale_two, owner_ref, packed_ref, one_ref, two_ref, whole):
    first = whole.shape[0]
    second = two_ref.shape[0]
    rows = one_ref.shape[0]
    unpack(packed_ref, 0, whole, first, scale_one)
    start = pl.multiple_of(owner_ref[0] * rows, 8)
    one_ref[...] = whole[pl.ds(start, rows), :]
    unpack(packed_ref, triangle(first)[-1], two_ref, second, scale_two)


def scatter_sum(value, axis, count):
    rows = value.shape[0] // count
    parts = lax.all_to_all(value.reshape(count, rows, LANES), axis, 0, 0, tiled=True)
    return jnp.sum(parts, axis=0)


def gather(value, axis, count):
    copies = jnp.broadcast_to(value[None], (count,) + value.shape)
    return lax.all_to_all(copies, axis, 0, 0, tiled=True)


def local(sizes, tensor, basis):
    gx, gy, gz, gc = sizes
    slices_here, rows_here, second = tensor.shape
    first = rows_here * gx
    rank = basis.shape[1]
    slices_all = slices_here * gy * gz * gc
    used = triangle(first)[-1] + triangle(second)[-1]
    unit = 8 * gx * gy * gc
    packed_rows = -(-used // unit) * unit
    vmem = pl.BlockSpec(memory_space=pltpu.VMEM)

    whole_basis = gather(basis, "x", gx).reshape(first, rank)
    field = lax.all_to_all(tensor, "x", 0, 0, tiled=True).reshape(first, second)
    packed, core = pl.pallas_call(
        gram_kernel,
        out_shape=(
            jax.ShapeDtypeStruct((packed_rows, LANES), jnp.float32),
            jax.ShapeDtypeStruct((rank, second), jnp.float32),
        ),
        in_specs=[vmem, vmem],
        out_specs=(vmem, vmem),
        scratch_shapes=[
            pltpu.VMEM((first, second), jnp.bfloat16),
            pltpu.VMEM((first, second), jnp.bfloat16),
            pltpu.VMEM((second, rank), jnp.bfloat16),
            pltpu.VMEM((second, rank), jnp.bfloat16),
        ],
        name="local_grams",
    )(field, whole_basis)
    core_parts = lax.all_to_all(core.reshape(gx, rank // gx, second), "x", 0, 0, tiled=True)
    core_out = jnp.transpose(core_parts, (1, 0, 2))

    part = scatter_sum(packed, "c", gc)
    part = scatter_sum(part, "x", gx)
    part = scatter_sum(part, "y", gy)
    part = jnp.sum(gather(part, "z", gz), axis=0)
    part = gather(part, "y", gy).reshape(-1, LANES)
    part = gather(part, "x", gx).reshape(-1, LANES)
    whole = gather(part, "c", gc).reshape(-1, LANES)

    gram_one, gram_two = pl.pallas_call(
        functools.partial(unpack_kernel, 1.0 / (slices_all * second), 1.0 / (slices_all * rank)),
        out_shape=(
            jax.ShapeDtypeStruct((rows_here, first), jnp.float32),
            jax.ShapeDtypeStruct((second, second), jnp.float32),
        ),
        in_specs=[pl.BlockSpec(memory_space=pltpu.SMEM), vmem],
        out_specs=(vmem, vmem),
        scratch_shapes=[pltpu.VMEM((first, first), jnp.float32)],
        name="mirror",
    )(lax.axis_index("x").astype(jnp.int32).reshape(1), whole)
    return gram_one, core_out, gram_two


def solution(mesh):
    gx, rest = mesh.devices.shape
    sizes = (gx, 8, rest // 16, 2)
    fine = Mesh(mesh.devices.reshape(sizes), ("x", "y", "z", "c"))
    spread = ("y", "z", "c")
    in_specs = (P(spread, "x", None), P("x", None))
    out_specs = (P("x", None), P("x", spread, None), P())
    return jax.shard_map(
        functools.partial(local, sizes), mesh=fine, in_specs=in_specs, out_specs=out_specs, check_vma=False
    )
```

```python
import functools

import jax
import jax.numpy as jnp
from jax import lax
from jax.experimental import pallas as pl
from jax.experimental.pallas import tpu as pltpu
from jax.sharding import Mesh, PartitionSpec as P

LANES = 128
FOLD = LANES // 2
VMEM = pl.BlockSpec(memory_space=pltpu.VMEM)
SMEM = pl.BlockSpec(memory_space=pltpu.SMEM)
ROOM = pltpu.CompilerParams(vmem_limit_bytes=24 << 20)


class Layout:
    def __init__(self, width, unit):
        self.width = width
        self.full = width // LANES
        self.left = width - self.full * LANES
        self.above = [0] * self.full
        row = 0
        for block in range(1, self.full):
            self.above[block] = row
            row += block * LANES
        self.strip = row
        row += self.left * (self.full + 1)
        split = -(-self.full // 2)
        self.fold = [(block // split, row + (block % split) * 3 * FOLD) for block in range(self.full)]
        self.used = [row + split * 3 * FOLD, row + (self.full - split) * 3 * FOLD]
        self.rows = -(-self.used[0] // unit) * unit


def halves(value):
    high = value.astype(jnp.bfloat16)
    low = (value - high.astype(jnp.float32)).astype(jnp.bfloat16)
    return high, low


def dot(a, b):
    return jnp.dot(a, b, preferred_element_type=jnp.float32)


def dot_rows(a, b):
    return lax.dot_general(a, b, (((1,), (1,)), ((), ())), preferred_element_type=jnp.float32)


def product(high, low, left, right):
    lh, ll, rh, rl = high[left, :], low[left, :], high[right, :], low[right, :]
    return dot_rows(lh, rh) + (dot_rows(lh, rl) + dot_rows(ll, rh))


def lane_below(rows):
    return lax.broadcasted_iota(jnp.int32, (rows, LANES), 1) < FOLD


def pack_gram(layout, high, low, packed, half):
    full, left = layout.full, layout.left
    for block in range(full):
        mine = pl.ds(block * LANES, LANES)
        tiles = product(high, low, pl.ds(0, (block + 1) * LANES), mine)
        above = block * LANES
        if above:
            packed[half, pl.ds(layout.above[block], above), :] = tiles[:above]
        into, row = layout.fold[block]
        packed[into, pl.ds(row + half * FOLD, FOLD), :] = tiles[above : above + FOLD]
        lower = tiles[above + FOLD :]
        corner = pl.ds(row + 2 * FOLD, FOLD)
        if half == 0:
            packed[into, corner, :] = pltpu.roll(lower, FOLD, 1)
        else:
            packed[into, corner, :] = jnp.where(lane_below(FOLD), packed[into, corner, :], lower)
    last = product(high, low, pl.ds(full * LANES, left), pl.ds(0, layout.width))
    for block in range(full):
        packed[half, pl.ds(layout.strip + block * left, left), :] = last[:, block * LANES : (block + 1) * LANES]
    corner = pl.ds(layout.strip + full * left, left)
    packed[half, corner, :] = jnp.zeros((left, LANES), jnp.float32)
    packed[half, corner, 0:left] = last[:, full * LANES :]
    spare = layout.rows - layout.used[half]
    if spare:
        packed[half, pl.ds(layout.used[half], spare), :] = jnp.zeros((spare, LANES), jnp.float32)


def dense_rows(rows, width):
    full = width // LANES
    left = width - full * LANES
    beside = LANES // left
    group = -(-rows // (8 * beside)) * 8
    return full, left, beside, group, rows * (full + 1) + group


def dense_kernel(field_ref, basis_ref, out_ref):
    _, rows, width = field_ref.shape
    full, left, beside, group, _ = dense_rows(rows, width)
    for block in range(full):
        out_ref[0, pl.ds(block * rows, rows), :] = field_ref[0, :, block * LANES : (block + 1) * LANES]
    out_ref[0, pl.ds(full * rows, rows), :] = basis_ref[...]
    base = (full + 1) * rows
    for part in range(beside):
        some = min(group, rows - part * group)
        piece = field_ref[0, pl.ds(part * group, some), full * LANES : width]
        out_ref[0, pl.ds(base, some), part * left : (part + 1) * left] = piece
        if some < group:
            rest = pl.ds(base + some, group - some)
            out_ref[0, rest, part * left : (part + 1) * left] = jnp.zeros((group - some, left), jnp.float32)


def gram_kernel(
    layout, mine_ref, dense_ref, keep_ref, send_ref, core_ref,
    field, basis, field_high, field_low, core_high, core_low, packed,
):
    blocks = dense_ref.shape[0]
    first, width = field.shape
    rows = first // blocks
    full, left, beside, group, _ = dense_rows(rows, width)
    for owner in range(blocks):
        for block in range(full):
            field[pl.ds(owner * rows, rows), block * LANES : (block + 1) * LANES] = dense_ref[
                owner, pl.ds(block * rows, rows), :
            ]
        basis[pl.ds(owner * rows, rows), :] = dense_ref[owner, pl.ds(full * rows, rows), :]
        base = (full + 1) * rows
        for part in range(beside):
            some = min(group, rows - part * group)
            field[pl.ds(owner * rows + part * group, some), full * LANES : width] = dense_ref[
                owner, pl.ds(base, some), part * left : (part + 1) * left
            ]
    high, low = halves(field[...])
    field_high[...] = high
    field_low[...] = low
    basis_high, basis_low = halves(basis[...].T)
    core = dot(basis_high, high) + (dot(basis_high, low) + dot(basis_low, high))
    core_ref[...] = core
    high, low = halves(core.T)
    core_high[...] = high
    core_low[...] = low
    pack_gram(layout, field_high, field_low, packed, 0)
    pack_gram(layout, core_high, core_low, packed, 1)
    mine = mine_ref[0]
    keep_ref[...] = packed[mine]
    send_ref[...] = packed[1 - mine]


def unpack(layout, packed, half, out_ref, scale):
    full, left = layout.full, layout.left
    for block in range(full):
        columns = pl.ds(block * LANES, LANES)
        for row in range(block):
            there = pl.ds(row * LANES, LANES)
            tile = packed[half, pl.ds(layout.above[block] + row * LANES, LANES), :] * scale
            out_ref[there, columns] = tile
            out_ref[columns, there] = tile.T
        into, row = layout.fold[block]
        upper = packed[into, pl.ds(row + half * FOLD, FOLD), :] * scale
        lower = packed[into, pl.ds(row + 2 * FOLD, FOLD), :] * scale
        if half == 0:
            lower = pltpu.roll(lower, FOLD, 1)
        turned = jnp.concatenate([upper, upper], axis=0).T[FOLD:]
        out_ref[pl.ds(block * LANES, FOLD), columns] = upper
        out_ref[pl.ds(block * LANES + FOLD, FOLD), columns] = jnp.where(lane_below(FOLD), turned, lower)
        tile = packed[half, pl.ds(layout.strip + block * left, left), :] * scale
        out_ref[pl.ds(full * LANES, left), columns] = tile
        out_ref[columns, pl.ds(full * LANES, left)] = tile.T
    corner = packed[half, pl.ds(layout.strip + full * left, left), :] * scale
    out_ref[pl.ds(full * LANES, left), pl.ds(full * LANES, left)] = corner[:, 0:left]


def unpack_kernel(layout, scale_one, scale_two, place_ref, own_ref, other_ref, one_ref, two_ref, packed, whole):
    rows = one_ref.shape[0]
    mine = place_ref[1]
    packed[mine] = own_ref[...]
    packed[1 - mine] = other_ref[...]
    unpack(layout, packed, 0, whole, scale_one)
    one_ref[...] = whole[pl.ds(pl.multiple_of(place_ref[0] * rows, 8), rows), :]
    unpack(layout, packed, 1, two_ref, scale_two)


def exchange(parts, axis):
    return lax.all_to_all(parts, axis, 0, 0, tiled=True)


def copies(value, count):
    return jnp.broadcast_to(value[None], (count,) + value.shape)


def local(sizes, tensor, basis):
    gx, gy, gz, gc = sizes
    slices_here, rows_here, second = tensor.shape
    first = rows_here * gx
    rank = basis.shape[1]
    slices_all = slices_here * gy * gz * gc
    plane = gy * gz
    layout = Layout(first, 8 * gx * plane)
    dense = dense_rows(rows_here, second)[-1]
    swap = [(i, gc - 1 - i) for i in range(gc)]
    place = jnp.stack([lax.axis_index("x"), lax.axis_index("c")]).astype(jnp.int32)

    blocks = pl.pallas_call(
        dense_kernel,
        grid=(slices_here,),
        out_shape=jax.ShapeDtypeStruct((slices_here, dense, LANES), jnp.float32),
        in_specs=[
            pl.BlockSpec((1, rows_here, second), lambda k: (k, 0, 0)),
            pl.BlockSpec((rows_here, rank), lambda k: (0, 0)),
        ],
        out_specs=pl.BlockSpec((1, dense, LANES), lambda k: (k, 0, 0)),
        name="dense_blocks",
    )(tensor, basis)
    blocks = exchange(blocks, "x")
    f32, bf16 = jnp.float32, jnp.bfloat16
    half_shape = jax.ShapeDtypeStruct((layout.rows, LANES), f32)
    keep, send, core = pl.pallas_call(
        functools.partial(gram_kernel, layout),
        out_shape=(half_shape, half_shape, jax.ShapeDtypeStruct((rank, second), f32)),
        in_specs=[SMEM, VMEM],
        out_specs=(VMEM, VMEM, VMEM),
        scratch_shapes=[
            pltpu.VMEM((first, second), f32),
            pltpu.VMEM((first, rank), f32),
            pltpu.VMEM((first, second), bf16),
            pltpu.VMEM((first, second), bf16),
            pltpu.VMEM((second, rank), bf16),
            pltpu.VMEM((second, rank), bf16),
            pltpu.VMEM((2, layout.rows, LANES), f32),
        ],
        compiler_params=ROOM,
        name="local_grams",
    )(place[1:], blocks)

    core_parts = exchange(core.reshape(gx, rank // gx, second), "x")
    came = lax.ppermute(send, "c", swap)
    came, core_parts = lax.optimization_barrier((came, core_parts))
    core_out = jnp.transpose(core_parts, (1, 0, 2))

    part = exchange((keep + came).reshape(gx, -1, LANES), "x")
    part = jnp.sum(part, axis=0)
    part = exchange(part.reshape(plane, -1, LANES), ("y", "z"))
    part = exchange(copies(jnp.sum(part, axis=0), plane), ("y", "z")).reshape(-1, LANES)
    own = exchange(copies(part, gx), "x").reshape(-1, LANES)
    other = lax.ppermute(own, "c", swap)

    gram_one, gram_two = pl.pallas_call(
        functools.partial(unpack_kernel, layout, 1.0 / (slices_all * second), 1.0 / (slices_all * rank)),
        out_shape=(
            jax.ShapeDtypeStruct((rows_here, first), f32),
            jax.ShapeDtypeStruct((second, second), f32),
        ),
        in_specs=[SMEM, VMEM, VMEM],
        out_specs=(VMEM, VMEM),
        scratch_shapes=[pltpu.VMEM((2, layout.rows, LANES), f32), pltpu.VMEM((first, first), f32)],
        compiler_params=ROOM,
        name="mirror",
    )(place, own, other)
    return gram_one, core_out, gram_two


def solution(mesh):
    gx, rest = mesh.devices.shape
    sizes = (gx, 8, rest // 16, 2)
    fine = Mesh(mesh.devices.reshape(sizes), ("x", "y", "z", "c"))
    spread = ("y", "z", "c")
    in_specs = (P(spread, "x", None), P("x", None))
    out_specs = (P("x", None), P("x", spread, None), P())
    return jax.shard_map(
        functools.partial(local, sizes), mesh=fine, in_specs=in_specs, out_specs=out_specs, check_vma=False
    )
```

```python
import functools

import jax
import jax.numpy as jnp
from jax import lax
from jax.experimental import pallas as pl
from jax.experimental.pallas import tpu as pltpu
from jax.sharding import Mesh, PartitionSpec as P

LANES = 128
FOLD = LANES // 2
VMEM = pl.BlockSpec(memory_space=pltpu.VMEM)
SMEM = pl.BlockSpec(memory_space=pltpu.SMEM)
ROOM = pltpu.CompilerParams(vmem_limit_bytes=24 << 20)


class Layout:
    def __init__(self, width, unit):
        self.width = width
        self.full = width // LANES
        self.left = width - self.full * LANES
        self.above = [0] * self.full
        row = 0
        for block in range(1, self.full):
            self.above[block] = row
            row += block * LANES
        self.strip = row
        row += self.left * (self.full + 1)
        split = -(-self.full // 2)
        self.fold = [(block // split, row + (block % split) * 3 * FOLD) for block in range(self.full)]
        self.used = [row + split * 3 * FOLD, row + (self.full - split) * 3 * FOLD]
        self.rows = -(-self.used[0] // unit) * unit


def halves(value):
    high = value.astype(jnp.bfloat16)
    low = (value - high.astype(jnp.float32)).astype(jnp.bfloat16)
    return high, low


def dot(a, b):
    return jnp.dot(a, b, preferred_element_type=jnp.float32)


def dot_rows(a, b):
    return lax.dot_general(a, b, (((1,), (1,)), ((), ())), preferred_element_type=jnp.float32)


def product(high, low, left, right):
    lh, ll, rh, rl = high[left, :], low[left, :], high[right, :], low[right, :]
    return dot_rows(lh, rh) + (dot_rows(lh, rl) + dot_rows(ll, rh))


def lane_below(rows):
    return lax.broadcasted_iota(jnp.int32, (rows, LANES), 1) < FOLD


def pack_gram(layout, high, low, packed, half):
    full, left = layout.full, layout.left
    for block in range(full):
        mine = pl.ds(block * LANES, LANES)
        tiles = product(high, low, pl.ds(0, (block + 1) * LANES), mine)
        above = block * LANES
        if above:
            packed[half, pl.ds(layout.above[block], above), :] = tiles[:above]
        into, row = layout.fold[block]
        packed[into, pl.ds(row + half * FOLD, FOLD), :] = tiles[above : above + FOLD]
        lower = tiles[above + FOLD :]
        corner = pl.ds(row + 2 * FOLD, FOLD)
        if half == 0:
            packed[into, corner, :] = pltpu.roll(lower, FOLD, 1)
        else:
            packed[into, corner, :] = jnp.where(lane_below(FOLD), packed[into, corner, :], lower)
    last = product(high, low, pl.ds(full * LANES, left), pl.ds(0, layout.width))
    for block in range(full):
        packed[half, pl.ds(layout.strip + block * left, left), :] = last[:, block * LANES : (block + 1) * LANES]
    corner = pl.ds(layout.strip + full * left, left)
    packed[half, corner, :] = jnp.zeros((left, LANES), jnp.float32)
    packed[half, corner, 0:left] = last[:, full * LANES :]
    spare = layout.rows - layout.used[half]
    if spare:
        packed[half, pl.ds(layout.used[half], spare), :] = jnp.zeros((spare, LANES), jnp.float32)


def dense_rows(rows, width):
    full = width // LANES
    left = width - full * LANES
    beside = LANES // left
    group = -(-rows // (8 * beside)) * 8
    return full, left, beside, group, rows * (full + 1) + group


def dense_kernel(field_ref, basis_ref, out_ref, dense, tail, arrived, left_for):
    blocks, rows, width = field_ref.shape
    full, left, beside, group, _ = dense_rows(rows, width)
    moves = []
    for block in range(blocks):
        last = field_ref.at[block, :, pl.ds(full * LANES, left)]
        mine = [pltpu.make_async_copy(last, tail.at[block], arrived.at[block, full + 1])]
        for part in range(full + 1):
            source = basis_ref if part == full else field_ref.at[block, :, pl.ds(part * LANES, LANES)]
            into = dense.at[block, pl.ds(part * rows, rows), :]
            mine.append(pltpu.make_async_copy(source, into, arrived.at[block, part]))
        for move in mine:
            move.start()
        moves.append(mine)
    base = (full + 1) * rows
    done = []
    for block in range(blocks):
        for move in moves[block]:
            move.wait()
        for part in range(beside):
            some = min(group, rows - part * group)
            lanes = slice(part * left, (part + 1) * left)
            dense[block, pl.ds(base, some), lanes] = tail[block, pl.ds(part * group, some), :]
            if some < group:
                dense[block, pl.ds(base + some, group - some), lanes] = jnp.zeros((group - some, left), jnp.float32)
        move = pltpu.make_async_copy(dense.at[block], out_ref.at[block], left_for.at[block])
        move.start()
        done.append(move)
    for move in done:
        move.wait()


def gram_kernel(
    layout, place_ref, dense_ref, keep_ref, send_ref, core_ref,
    field, basis, field_high, field_low, core_high, core_low, packed,
):
    blocks = dense_ref.shape[0]
    first, width = field.shape
    rows = first // blocks
    full, left, beside, group, _ = dense_rows(rows, width)
    for owner in range(blocks):
        for block in range(full):
            field[pl.ds(owner * rows, rows), block * LANES : (block + 1) * LANES] = dense_ref[
                owner, pl.ds(block * rows, rows), :
            ]
        basis[pl.ds(owner * rows, rows), :] = dense_ref[owner, pl.ds(full * rows, rows), :]
        base = (full + 1) * rows
        for part in range(beside):
            some = min(group, rows - part * group)
            field[pl.ds(owner * rows + part * group, some), full * LANES : width] = dense_ref[
                owner, pl.ds(base, some), part * left : (part + 1) * left
            ]
    high, low = halves(field[...])
    field_high[...] = high
    field_low[...] = low
    basis_high, basis_low = halves(basis[...].T)
    core = dot(basis_high, high) + (dot(basis_high, low) + dot(basis_low, high))
    owners, tiles, owned, _ = core_ref.shape
    for owner in range(owners):
        for tile in range(tiles):
            lanes = min(LANES, width - tile * LANES)
            piece = core[owner * owned : (owner + 1) * owned, tile * LANES : tile * LANES + lanes]
            if lanes < LANES:
                core_ref[owner, tile] = jnp.zeros((owned, LANES), jnp.float32)
            core_ref[owner, tile, :, 0:lanes] = piece
    high, low = halves(core.T)
    core_high[...] = high
    core_low[...] = low
    pack_gram(layout, field_high, field_low, packed, 0)
    pack_gram(layout, core_high, core_low, packed, 1)
    mine = place_ref[1]
    keep_ref[...] = packed[mine]
    send_ref[...] = packed[1 - mine]


def unpack(layout, packed, half, out_ref, scale):
    full, left = layout.full, layout.left
    for block in range(full):
        columns = pl.ds(block * LANES, LANES)
        for row in range(block):
            there = pl.ds(row * LANES, LANES)
            tile = packed[half, pl.ds(layout.above[block] + row * LANES, LANES), :] * scale
            out_ref[there, columns] = tile
            out_ref[columns, there] = tile.T
        into, row = layout.fold[block]
        upper = packed[into, pl.ds(row + half * FOLD, FOLD), :] * scale
        lower = packed[into, pl.ds(row + 2 * FOLD, FOLD), :] * scale
        if half == 0:
            lower = pltpu.roll(lower, FOLD, 1)
        turned = jnp.concatenate([upper, upper], axis=0).T[FOLD:]
        out_ref[pl.ds(block * LANES, FOLD), columns] = upper
        out_ref[pl.ds(block * LANES + FOLD, FOLD), columns] = jnp.where(lane_below(FOLD), turned, lower)
        tile = packed[half, pl.ds(layout.strip + block * left, left), :] * scale
        out_ref[pl.ds(full * LANES, left), columns] = tile
        out_ref[columns, pl.ds(full * LANES, left)] = tile.T
    corner = packed[half, pl.ds(layout.strip + full * left, left), :] * scale
    out_ref[pl.ds(full * LANES, left), pl.ds(full * LANES, left)] = corner[:, 0:left]


def unpack_kernel(layout, scale_one, scale_two, place_ref, own_ref, other_ref, one_ref, two_ref, packed, whole):
    rows = one_ref.shape[0]
    mine = place_ref[1]
    packed[mine] = own_ref[...]
    packed[1 - mine] = other_ref[...]
    unpack(layout, packed, 0, whole, scale_one)
    one_ref[...] = whole[pl.ds(pl.multiple_of(place_ref[0] * rows, 8), rows), :]
    unpack(layout, packed, 1, two_ref, scale_two)


def exchange(parts, axis):
    return lax.all_to_all(parts, axis, 0, 0, tiled=True)


def copies(value, count):
    return jnp.broadcast_to(value[None], (count,) + value.shape)


def local(sizes, tensor, basis):
    gx, gy, gz, gc = sizes
    slices_here, rows_here, second = tensor.shape
    first = rows_here * gx
    rank = basis.shape[1]
    slices_all = slices_here * gy * gz * gc
    plane = gy * gz
    layout = Layout(first, 8 * gx * plane)
    dense = dense_rows(rows_here, second)[-1]
    swap = [(i, gc - 1 - i) for i in range(gc)]
    place = jnp.stack([lax.axis_index("x"), lax.axis_index("c")]).astype(jnp.int32)

    outside = pl.BlockSpec(memory_space=pl.ANY)
    full, left = dense_rows(rows_here, second)[:2]
    blocks = pl.pallas_call(
        dense_kernel,
        out_shape=jax.ShapeDtypeStruct((slices_here, dense, LANES), jnp.float32),
        in_specs=[outside, outside],
        out_specs=outside,
        scratch_shapes=[
            pltpu.VMEM((slices_here, dense, LANES), jnp.float32),
            pltpu.VMEM((slices_here, rows_here, left), jnp.float32),
            pltpu.SemaphoreType.DMA((slices_here, full + 2)),
            pltpu.SemaphoreType.DMA((slices_here,)),
        ],
        name="dense_blocks",
    )(tensor, basis)
    blocks, place = lax.optimization_barrier((blocks, place))
    blocks = exchange(blocks, "x")
    f32, bf16 = jnp.float32, jnp.bfloat16
    half_shape = jax.ShapeDtypeStruct((layout.rows, LANES), f32)
    keep, send, core = pl.pallas_call(
        functools.partial(gram_kernel, layout),
        out_shape=(half_shape, half_shape, jax.ShapeDtypeStruct((gx, full + 1, rank // gx, LANES), f32)),
        in_specs=[SMEM, VMEM],
        out_specs=(VMEM, VMEM, VMEM),
        scratch_shapes=[
            pltpu.VMEM((first, second), f32),
            pltpu.VMEM((first, rank), f32),
            pltpu.VMEM((first, second), bf16),
            pltpu.VMEM((first, second), bf16),
            pltpu.VMEM((second, rank), bf16),
            pltpu.VMEM((second, rank), bf16),
            pltpu.VMEM((2, layout.rows, LANES), f32),
        ],
        compiler_params=ROOM,
        name="local_grams",
    )(place, blocks)

    came = lax.ppermute(send, "c", swap)
    sums = (keep + came).reshape(gx, -1, LANES)
    some = sums.shape[1]
    parts = exchange(jnp.concatenate([sums, core.reshape(gx, -1, LANES)], axis=1), "x")
    part = jnp.sum(parts[:, :some], axis=0)
    core_out = parts[:, some:].reshape(gx, full + 1, rank // gx, LANES)
    core_out = jnp.transpose(core_out, (2, 0, 1, 3)).reshape(rank // gx, gx, -1)[:, :, :second]
    part = exchange(part.reshape(plane, -1, LANES), ("y", "z"))
    part = exchange(copies(jnp.sum(part, axis=0), plane), ("y", "z")).reshape(-1, LANES)
    own = exchange(copies(part, gx), "x").reshape(-1, LANES)
    other = lax.ppermute(own, "c", swap)

    gram_one, gram_two = pl.pallas_call(
        functools.partial(unpack_kernel, layout, 1.0 / (slices_all * second), 1.0 / (slices_all * rank)),
        out_shape=(
            jax.ShapeDtypeStruct((rows_here, first), f32),
            jax.ShapeDtypeStruct((second, second), f32),
        ),
        in_specs=[SMEM, VMEM, VMEM],
        out_specs=(VMEM, VMEM),
        scratch_shapes=[pltpu.VMEM((2, layout.rows, LANES), f32), pltpu.VMEM((first, first), f32)],
        compiler_params=ROOM,
        name="mirror",
    )(place, own, other)
    return gram_one, core_out, gram_two


def solution(mesh):
    gx, rest = mesh.devices.shape
    sizes = (gx, 8, rest // 16, 2)
    fine = Mesh(mesh.devices.reshape(sizes), ("x", "y", "z", "c"))
    spread = ("y", "z", "c")
    in_specs = (P(spread, "x", None), P("x", None))
    out_specs = (P("x", None), P("x", spread, None), P())
    return jax.shard_map(
        functools.partial(local, sizes), mesh=fine, in_specs=in_specs, out_specs=out_specs, check_vma=False
    )
```

```python
import functools

import jax
import jax.numpy as jnp
from jax import lax
from jax.experimental import pallas as pl
from jax.experimental.pallas import tpu as pltpu
from jax.sharding import Mesh, PartitionSpec as P

LANES = 128
FOLD = LANES // 2
VMEM = pl.BlockSpec(memory_space=pltpu.VMEM)
SMEM = pl.BlockSpec(memory_space=pltpu.SMEM)
ROOM = pltpu.CompilerParams(vmem_limit_bytes=24 << 20)


class Layout:
    def __init__(self, width, unit):
        self.width = width
        self.full = width // LANES
        self.left = width - self.full * LANES
        self.above = [0] * self.full
        row = 0
        for block in range(1, self.full):
            self.above[block] = row
            row += block * LANES
        self.strip = row
        row += self.left * (self.full + 1)
        split = -(-self.full // 2)
        self.fold = [(block // split, row + (block % split) * 3 * FOLD) for block in range(self.full)]
        self.used = [row + split * 3 * FOLD, row + (self.full - split) * 3 * FOLD]
        self.rows = -(-self.used[0] // unit) * unit


def halves(value):
    high = value.astype(jnp.bfloat16)
    low = (value - high.astype(jnp.float32)).astype(jnp.bfloat16)
    return high, low


def dot(a, b):
    return jnp.dot(a, b, preferred_element_type=jnp.float32)


def dot_rows(a, b):
    return lax.dot_general(a, b, (((1,), (1,)), ((), ())), preferred_element_type=jnp.float32)


def lane_below(rows):
    return lax.broadcasted_iota(jnp.int32, (rows, LANES), 1) < FOLD


def pack_gram(layout, product, packed, half):
    full, left, width = layout.full, layout.left, layout.width
    for start in range(0, width, 2 * LANES):
        columns = min(2 * LANES, width - start)
        last = start + columns == width
        group = product(width if last else start + columns, start, columns)
        for block in range(start // LANES, min(full, (start + columns) // LANES)):
            inside = slice(block * LANES - start, (block + 1) * LANES - start)
            above = block * LANES
            if above:
                packed[half, pl.ds(layout.above[block], above), :] = group[:above, inside]
            into, row = layout.fold[block]
            packed[into, pl.ds(row + half * FOLD, FOLD), :] = group[above : above + FOLD, inside]
            lower = group[above + FOLD : above + LANES, inside]
            corner = pl.ds(row + 2 * FOLD, FOLD)
            if half == 0:
                packed[into, corner, :] = pltpu.roll(lower, FOLD, 1)
            else:
                packed[into, corner, :] = jnp.where(lane_below(FOLD), packed[into, corner, :], lower)
        if last:
            strip = group[:, full * LANES - start :]
            for block in range(full):
                piece = strip[block * LANES : (block + 1) * LANES].T
                packed[half, pl.ds(layout.strip + block * left, left), :] = piece
            corner = pl.ds(layout.strip + full * left, left)
            packed[half, corner, :] = jnp.zeros((left, LANES), jnp.float32)
            packed[half, corner, 0:left] = strip[full * LANES :]
    spare = layout.rows - layout.used[half]
    if spare:
        packed[half, pl.ds(layout.used[half], spare), :] = jnp.zeros((spare, LANES), jnp.float32)


def dense_rows(rows, width):
    full = width // LANES
    left = width - full * LANES
    beside = LANES // left
    group = -(-rows // (8 * beside)) * 8
    return full, left, beside, group, rows * (full + 1) + group


def dense_kernel(field_ref, basis_ref, out_ref):
    blocks, rows, width = field_ref.shape
    full, left, beside, group, _ = dense_rows(rows, width)
    base = (full + 1) * rows
    for block in range(blocks):
        for part in range(full):
            out_ref[block, pl.ds(part * rows, rows), :] = field_ref[block, :, part * LANES : (part + 1) * LANES]
        out_ref[block, pl.ds(full * rows, rows), :] = basis_ref[...]
        for part in range(beside):
            some = min(group, rows - part * group)
            lanes = slice(part * left, (part + 1) * left)
            piece = field_ref[block, pl.ds(part * group, some), full * LANES : width]
            out_ref[block, pl.ds(base, some), lanes] = piece
            if some < group:
                out_ref[block, pl.ds(base + some, group - some), lanes] = jnp.zeros((group - some, left), jnp.float32)


def core_kernel(dense_ref, high_ref, low_ref, core_ref, field, basis):
    blocks = dense_ref.shape[0]
    first, width = field.shape
    rows = first // blocks
    full, left, beside, group, _ = dense_rows(rows, width)
    base = (full + 1) * rows
    for owner in range(blocks):
        own = owner * rows
        for part in range(full):
            field[pl.ds(own, rows), part * LANES : (part + 1) * LANES] = dense_ref[owner, pl.ds(part * rows, rows), :]
        basis[pl.ds(own, rows), :] = dense_ref[owner, pl.ds(full * rows, rows), :]
        for part in range(beside):
            some = min(group, rows - part * group)
            piece = dense_ref[owner, pl.ds(base, some), part * left : (part + 1) * left]
            field[pl.ds(own + part * group, some), full * LANES : width] = piece
    high, low = halves(field[...])
    high_ref[...] = high
    low_ref[...] = low
    basis_high, basis_low = halves(basis[...].T)
    core_ref[...] = dot(basis_high, high) + (dot(basis_high, low) + dot(basis_low, high))


def gram_kernel(layout, place_ref, high_ref, low_ref, core_ref, keep_ref, send_ref, left_side, right_side, packed):
    rank = core_ref.shape[0]
    high, low = halves(core_ref[...].T)
    left_side[:, 0:rank] = high
    left_side[:, rank : 2 * rank] = low
    right_side[:, 0:rank] = high
    right_side[:, rank : 2 * rank] = high

    def field_product(rows, start, columns):
        lh, ll = high_ref[pl.ds(0, rows), :], low_ref[pl.ds(0, rows), :]
        rh, rl = high_ref[pl.ds(start, columns), :], low_ref[pl.ds(start, columns), :]
        return dot_rows(lh, rh) + (dot_rows(lh, rl) + dot_rows(ll, rh))

    def core_product(rows, start, columns):
        here, there = pl.ds(0, rows), pl.ds(start, columns)
        both = dot_rows(left_side[here, :], right_side[there, :])
        return both + dot_rows(left_side[here, 0:rank], left_side[there, rank : 2 * rank])

    pack_gram(layout, field_product, packed, 0)
    pack_gram(layout, core_product, packed, 1)
    mine = place_ref[1]
    keep_ref[...] = packed[mine]
    send_ref[...] = packed[1 - mine]


def unpack(layout, packed, half, out_ref, scale):
    full, left = layout.full, layout.left
    for block in range(full):
        columns = pl.ds(block * LANES, LANES)
        for row in range(block):
            there = pl.ds(row * LANES, LANES)
            tile = packed[half, pl.ds(layout.above[block] + row * LANES, LANES), :] * scale
            out_ref[there, columns] = tile
            out_ref[columns, there] = tile.T
        into, row = layout.fold[block]
        upper = packed[into, pl.ds(row + half * FOLD, FOLD), :] * scale
        lower = packed[into, pl.ds(row + 2 * FOLD, FOLD), :] * scale
        if half == 0:
            lower = pltpu.roll(lower, FOLD, 1)
        turned = jnp.concatenate([upper, upper], axis=0).T[FOLD:]
        out_ref[pl.ds(block * LANES, FOLD), columns] = upper
        out_ref[pl.ds(block * LANES + FOLD, FOLD), columns] = jnp.where(lane_below(FOLD), turned, lower)
        tile = packed[half, pl.ds(layout.strip + block * left, left), :] * scale
        out_ref[pl.ds(full * LANES, left), columns] = tile
        out_ref[columns, pl.ds(full * LANES, left)] = tile.T
    corner = packed[half, pl.ds(layout.strip + full * left, left), :] * scale
    out_ref[pl.ds(full * LANES, left), pl.ds(full * LANES, left)] = corner[:, 0:left]


def unpack_kernel(layout, scale_one, scale_two, place_ref, own_ref, other_ref, one_ref, two_ref, packed, whole):
    rows = one_ref.shape[0]
    mine = place_ref[1]
    packed[mine] = own_ref[...]
    packed[1 - mine] = other_ref[...]
    unpack(layout, packed, 0, whole, scale_one)
    one_ref[...] = whole[pl.ds(pl.multiple_of(place_ref[0] * rows, 8), rows), :]
    unpack(layout, packed, 1, two_ref, scale_two)


def exchange(parts, axis):
    return lax.all_to_all(parts, axis, 0, 0, tiled=True)


def copies(value, count):
    return jnp.broadcast_to(value[None], (count,) + value.shape)


def cost(flops, moved):
    return pl.CostEstimate(flops=flops, transcendentals=0, bytes_accessed=moved)


def scatter_sum(value, axes, count):
    return jnp.sum(exchange(value.reshape(count, -1, LANES), axes), axis=0)


def gather(value, axes, count):
    return exchange(copies(value, count), axes).reshape(-1, LANES)


def local(sizes, tensor, basis):
    gx = sizes["x"]
    slices_here, rows_here, second = tensor.shape
    first = rows_here * gx
    rank = basis.shape[1]
    near, far = ("x", "zl"), ("y", "zh")
    near_count, far_count = gx * sizes["zl"], sizes["y"] * sizes["zh"]
    slices_all = slices_here * sizes["y"] * sizes["zh"] * sizes["zl"] * sizes["c"]
    layout = Layout(first, 8 * near_count * far_count)
    dense = dense_rows(rows_here, second)[-1]
    swap = [(i, sizes["c"] - 1 - i) for i in range(sizes["c"])]
    place = jnp.stack([lax.axis_index("x"), lax.axis_index("c")]).astype(jnp.int32)
    f32, bf16 = jnp.float32, jnp.bfloat16

    blocks = pl.pallas_call(
        dense_kernel,
        out_shape=jax.ShapeDtypeStruct((slices_here, dense, LANES), f32),
        in_specs=[VMEM, VMEM],
        out_specs=VMEM,
        compiler_params=ROOM,
        name="dense_blocks",
    )(tensor, basis)
    blocks, place = lax.optimization_barrier((blocks, place))
    blocks = exchange(blocks, "x")
    high, low, core = pl.pallas_call(
        core_kernel,
        out_shape=(
            jax.ShapeDtypeStruct((first, second), bf16),
            jax.ShapeDtypeStruct((first, second), bf16),
            jax.ShapeDtypeStruct((rank, second), f32),
        ),
        in_specs=[VMEM],
        out_specs=(VMEM, VMEM, VMEM),
        scratch_shapes=[pltpu.VMEM((first, second), f32), pltpu.VMEM((first, rank), f32)],
        compiler_params=ROOM,
        cost_estimate=cost(6 * rank * first * second, 8 * first * second),
        name="core_of_slice",
    )(blocks)
    core_parts = exchange(core.reshape(gx, rank // gx, second), "x")
    half_shape = jax.ShapeDtypeStruct((layout.rows, LANES), f32)
    keep, send = pl.pallas_call(
        functools.partial(gram_kernel, layout),
        out_shape=(half_shape, half_shape),
        in_specs=[SMEM, VMEM, VMEM, VMEM],
        out_specs=(VMEM, VMEM),
        scratch_shapes=[
            pltpu.VMEM((second, 2 * rank), bf16),
            pltpu.VMEM((second, 2 * rank), bf16),
            pltpu.VMEM((2, layout.rows, LANES), f32),
        ],
        compiler_params=ROOM,
        cost_estimate=cost(4 * first * first * second, 12 * first * second),
        name="local_grams",
    )(place, high, low, core)

    send, core_parts = lax.optimization_barrier((send, core_parts))
    came = lax.ppermute(send, "c", swap)
    core_out = jnp.transpose(core_parts, (1, 0, 2))
    part = scatter_sum(scatter_sum(keep + came, near, near_count), far, far_count)
    own = gather(gather(part, far, far_count), near, near_count)
    other = lax.ppermute(own, "c", swap)

    gram_one, gram_two = pl.pallas_call(
        functools.partial(unpack_kernel, layout, 1.0 / (slices_all * second), 1.0 / (slices_all * rank)),
        out_shape=(
            jax.ShapeDtypeStruct((rows_here, first), f32),
            jax.ShapeDtypeStruct((second, second), f32),
        ),
        in_specs=[SMEM, VMEM, VMEM],
        out_specs=(VMEM, VMEM),
        scratch_shapes=[pltpu.VMEM((2, layout.rows, LANES), f32), pltpu.VMEM((first, first), f32)],
        compiler_params=ROOM,
        name="mirror",
    )(place, own, other)
    return gram_one, core_out, gram_two


def solution(mesh):
    gx, rest = mesh.devices.shape
    sizes = {"x": gx, "y": 8, "zh": rest // 32, "zl": 2, "c": 2}
    fine = Mesh(mesh.devices.reshape(tuple(sizes.values())), tuple(sizes))
    spread = ("y", "zh", "zl", "c")
    in_specs = (P(spread, "x", None), P("x", None))
    out_specs = (P("x", None), P("x", spread, None), P())
    return jax.shard_map(
        functools.partial(local, sizes), mesh=fine, in_specs=in_specs, out_specs=out_specs, check_vma=False
    )
```

```python
import functools

import jax
import jax.numpy as jnp
from jax import lax
from jax.experimental import pallas as pl
from jax.experimental.pallas import tpu as pltpu
from jax.sharding import Mesh, PartitionSpec as P

LANES = 128
FOLD = LANES // 2
VMEM = pl.BlockSpec(memory_space=pltpu.VMEM)
SMEM = pl.BlockSpec(memory_space=pltpu.SMEM)
ROOM = pltpu.CompilerParams(vmem_limit_bytes=24 << 20)


class Layout:
    def __init__(self, width, unit):
        self.width = width
        self.full = width // LANES
        self.left = width - self.full * LANES
        self.above = [0] * self.full
        row = 0
        for block in range(1, self.full):
            self.above[block] = row
            row += block * LANES
        self.strip = row
        row += self.left * (self.full + 1)
        split = -(-self.full // 2)
        self.fold = [(block // split, row + (block % split) * 3 * FOLD) for block in range(self.full)]
        self.used = [row + split * 3 * FOLD, row + (self.full - split) * 3 * FOLD]
        self.rows = -(-self.used[0] // unit) * unit


def halves(value):
    high = value.astype(jnp.bfloat16)
    low = (value - high.astype(jnp.float32)).astype(jnp.bfloat16)
    return high, low


def dot(a, b):
    return jnp.dot(a, b, preferred_element_type=jnp.float32)


def dot_rows(a, b):
    return lax.dot_general(a, b, (((1,), (1,)), ((), ())), preferred_element_type=jnp.float32)


def lane_below(rows):
    return lax.broadcasted_iota(jnp.int32, (rows, LANES), 1) < FOLD


def pack_gram(layout, product, packed, half):
    full, left, width = layout.full, layout.left, layout.width
    for start in range(0, width, 2 * LANES):
        columns = min(2 * LANES, width - start)
        last = start + columns == width
        group = product(width if last else start + columns, start, columns)
        for block in range(start // LANES, min(full, (start + columns) // LANES)):
            inside = slice(block * LANES - start, (block + 1) * LANES - start)
            above = block * LANES
            if above:
                packed[half, pl.ds(layout.above[block], above), :] = group[:above, inside]
            into, row = layout.fold[block]
            packed[into, pl.ds(row + half * FOLD, FOLD), :] = group[above : above + FOLD, inside]
            lower = group[above + FOLD : above + LANES, inside]
            corner = pl.ds(row + 2 * FOLD, FOLD)
            if half == 0:
                packed[into, corner, :] = pltpu.roll(lower, FOLD, 1)
            else:
                packed[into, corner, :] = jnp.where(lane_below(FOLD), packed[into, corner, :], lower)
        if last:
            strip = group[:, full * LANES - start :]
            for block in range(full):
                piece = strip[block * LANES : (block + 1) * LANES].T
                packed[half, pl.ds(layout.strip + block * left, left), :] = piece
            corner = pl.ds(layout.strip + full * left, left)
            packed[half, corner, :] = jnp.zeros((left, LANES), jnp.float32)
            packed[half, corner, 0:left] = strip[full * LANES :]
    spare = layout.rows - layout.used[half]
    if spare:
        packed[half, pl.ds(layout.used[half], spare), :] = jnp.zeros((spare, LANES), jnp.float32)


def dense_rows(rows, width):
    full = width // LANES
    left = width - full * LANES
    beside = LANES // left
    group = -(-rows // (8 * beside)) * 8
    return full, left, beside, group, rows * (full + 1) + group


def dense_kernel(field_ref, basis_ref, out_ref):
    blocks, rows, width = field_ref.shape
    full, left, beside, group, _ = dense_rows(rows, width)
    base = (full + 1) * rows
    for block in range(blocks):
        for part in range(full):
            out_ref[block, pl.ds(part * rows, rows), :] = field_ref[block, :, part * LANES : (part + 1) * LANES]
        out_ref[block, pl.ds(full * rows, rows), :] = basis_ref[...]
        for part in range(beside):
            some = min(group, rows - part * group)
            lanes = slice(part * left, (part + 1) * left)
            piece = field_ref[block, pl.ds(part * group, some), full * LANES : width]
            out_ref[block, pl.ds(base, some), lanes] = piece
            if some < group:
                out_ref[block, pl.ds(base + some, group - some), lanes] = jnp.zeros((group - some, left), jnp.float32)


def gram_kernel(
    layout, place_ref, dense_ref, keep_ref, send_ref, core_ref,
    field, basis, field_high, field_low, left_side, right_side, packed,
):
    blocks = dense_ref.shape[0]
    first, width = field.shape
    rank = basis.shape[1]
    rows = first // blocks
    full, left, beside, group, _ = dense_rows(rows, width)
    base = (full + 1) * rows
    for owner in range(blocks):
        own = owner * rows
        for part in range(full):
            field[pl.ds(own, rows), part * LANES : (part + 1) * LANES] = dense_ref[owner, pl.ds(part * rows, rows), :]
        basis[pl.ds(own, rows), :] = dense_ref[owner, pl.ds(full * rows, rows), :]
        for part in range(beside):
            some = min(group, rows - part * group)
            piece = dense_ref[owner, pl.ds(base, some), part * left : (part + 1) * left]
            field[pl.ds(own + part * group, some), full * LANES : width] = piece
    high, low = halves(field[...])
    field_high[...] = high
    field_low[...] = low
    basis_high, basis_low = halves(basis[...].T)
    core = dot(basis_high, high) + (dot(basis_high, low) + dot(basis_low, high))
    core_ref[...] = core
    high, low = halves(core.T)
    left_side[:, 0:rank] = high
    left_side[:, rank : 2 * rank] = low
    right_side[:, 0:rank] = high
    right_side[:, rank : 2 * rank] = high

    def field_product(rows, start, columns):
        lh, ll = field_high[pl.ds(0, rows), :], field_low[pl.ds(0, rows), :]
        rh, rl = field_high[pl.ds(start, columns), :], field_low[pl.ds(start, columns), :]
        return dot_rows(lh, rh) + (dot_rows(lh, rl) + dot_rows(ll, rh))

    def core_product(rows, start, columns):
        here, there = pl.ds(0, rows), pl.ds(start, columns)
        both = dot_rows(left_side[here, :], right_side[there, :])
        return both + dot_rows(left_side[here, 0:rank], left_side[there, rank : 2 * rank])

    pack_gram(layout, field_product, packed, 0)
    pack_gram(layout, core_product, packed, 1)
    mine = place_ref[1]
    keep_ref[...] = packed[mine]
    send_ref[...] = packed[1 - mine]


def parts_kernel(place_ref, core_ref, after_ref, *out_refs):
    owned = out_refs[0].shape[0]
    for step, out_ref in enumerate(out_refs):
        owner = lax.rem(place_ref[0] + step, len(out_refs))
        out_ref[...] = core_ref[pl.ds(pl.multiple_of(owner * owned, 8), owned), :]


def rows_kernel(place_ref, *refs):
    came, (out_ref, ordered) = refs[:-2], refs[-2:]
    count = len(came)
    for step, ref in enumerate(came):
        ordered[lax.rem(place_ref[0] + count - step, count)] = ref[...]
    for owner in range(count):
        out_ref[:, owner, :] = ordered[owner]


def unpack(layout, packed, half, out_ref, scale):
    full, left = layout.full, layout.left
    for block in range(full):
        columns = pl.ds(block * LANES, LANES)
        for row in range(block):
            there = pl.ds(row * LANES, LANES)
            tile = packed[half, pl.ds(layout.above[block] + row * LANES, LANES), :] * scale
            out_ref[there, columns] = tile
            out_ref[columns, there] = tile.T
        into, row = layout.fold[block]
        upper = packed[into, pl.ds(row + half * FOLD, FOLD), :] * scale
        lower = packed[into, pl.ds(row + 2 * FOLD, FOLD), :] * scale
        if half == 0:
            lower = pltpu.roll(lower, FOLD, 1)
        turned = jnp.concatenate([upper, upper], axis=0).T[FOLD:]
        out_ref[pl.ds(block * LANES, FOLD), columns] = upper
        out_ref[pl.ds(block * LANES + FOLD, FOLD), columns] = jnp.where(lane_below(FOLD), turned, lower)
        tile = packed[half, pl.ds(layout.strip + block * left, left), :] * scale
        out_ref[pl.ds(full * LANES, left), columns] = tile
        out_ref[columns, pl.ds(full * LANES, left)] = tile.T
    corner = packed[half, pl.ds(layout.strip + full * left, left), :] * scale
    out_ref[pl.ds(full * LANES, left), pl.ds(full * LANES, left)] = corner[:, 0:left]


def unpack_kernel(layout, scale_one, scale_two, place_ref, own_ref, other_ref, one_ref, two_ref, packed, whole):
    rows = one_ref.shape[0]
    mine = place_ref[1]
    packed[mine] = own_ref[...]
    packed[1 - mine] = other_ref[...]
    unpack(layout, packed, 0, whole, scale_one)
    one_ref[...] = whole[pl.ds(pl.multiple_of(place_ref[0] * rows, 8), rows), :]
    unpack(layout, packed, 1, two_ref, scale_two)


def exchange(parts, axis):
    return lax.all_to_all(parts, axis, 0, 0, tiled=True)


def copies(value, count):
    return jnp.broadcast_to(value[None], (count,) + value.shape)


def cost(flops, moved):
    return pl.CostEstimate(flops=flops, transcendentals=0, bytes_accessed=moved)


def scatter_sum(value, axes, count):
    return jnp.sum(exchange(value.reshape(count, -1, LANES), axes), axis=0)


def gather(value, axes, count):
    return exchange(copies(value, count), axes).reshape(-1, LANES)


def local(sizes, tensor, basis):
    gx = sizes["x"]
    slices_here, rows_here, second = tensor.shape
    first = rows_here * gx
    rank = basis.shape[1]
    near, far = ("x", "zl"), ("y", "zh")
    near_count, far_count = gx * sizes["zl"], sizes["y"] * sizes["zh"]
    slices_all = slices_here * sizes["y"] * sizes["zh"] * sizes["zl"] * sizes["c"]
    layout = Layout(first, 8 * near_count * far_count)
    dense = dense_rows(rows_here, second)[-1]
    swap = [(i, sizes["c"] - 1 - i) for i in range(sizes["c"])]
    place = jnp.stack([lax.axis_index("x"), lax.axis_index("c")]).astype(jnp.int32)
    f32, bf16 = jnp.float32, jnp.bfloat16

    blocks = pl.pallas_call(
        dense_kernel,
        out_shape=jax.ShapeDtypeStruct((slices_here, dense, LANES), f32),
        in_specs=[VMEM, VMEM],
        out_specs=VMEM,
        compiler_params=ROOM,
        name="dense_blocks",
    )(tensor, basis)
    blocks, place = lax.optimization_barrier((blocks, place))
    blocks = exchange(blocks, "x")
    half_shape = jax.ShapeDtypeStruct((layout.rows, LANES), f32)
    keep, send, core = pl.pallas_call(
        functools.partial(gram_kernel, layout),
        out_shape=(half_shape, half_shape, jax.ShapeDtypeStruct((rank, second), f32)),
        in_specs=[SMEM, VMEM],
        out_specs=(VMEM, VMEM, VMEM),
        scratch_shapes=[
            pltpu.VMEM((first, second), f32),
            pltpu.VMEM((first, rank), f32),
            pltpu.VMEM((first, second), bf16),
            pltpu.VMEM((first, second), bf16),
            pltpu.VMEM((second, 2 * rank), bf16),
            pltpu.VMEM((second, 2 * rank), bf16),
            pltpu.VMEM((2, layout.rows, LANES), f32),
        ],
        compiler_params=ROOM,
        cost_estimate=cost(5 * first * first * second, 12 * first * second),
        name="local_grams",
    )(place, blocks)

    came = lax.ppermute(send, "c", swap)
    part = scatter_sum(keep + came, near, near_count)
    owned = rank // gx
    core_parts = pl.pallas_call(
        parts_kernel,
        out_shape=[jax.ShapeDtypeStruct((owned, second), f32)] * gx,
        in_specs=[SMEM, VMEM, VMEM],
        out_specs=[VMEM] * gx,
        compiler_params=ROOM,
        cost_estimate=cost(rank * second, 8 * rank * second),
        name="core_parts",
    )(place, core, part[:8])
    came_core = [core_parts[0]]
    for step in range(1, gx):
        shift = [(i, (i + step) % gx) for i in range(gx)]
        came_core.append(lax.ppermute(core_parts[step], "x", shift))
    part = scatter_sum(part, far, far_count)
    part, *came_core = lax.optimization_barrier((part, *came_core))
    core_out = pl.pallas_call(
        rows_kernel,
        out_shape=jax.ShapeDtypeStruct((owned, gx, second), f32),
        in_specs=[SMEM] + [VMEM] * gx,
        out_specs=VMEM,
        scratch_shapes=[pltpu.VMEM((gx, owned, second), f32)],
        compiler_params=ROOM,
        cost_estimate=cost(rank * second, 8 * rank * second),
        name="core_rows",
    )(place, *came_core)
    own = gather(gather(part, far, far_count), near, near_count)
    other = lax.ppermute(own, "c", swap)

    gram_one, gram_two = pl.pallas_call(
        functools.partial(unpack_kernel, layout, 1.0 / (slices_all * second), 1.0 / (slices_all * rank)),
        out_shape=(
            jax.ShapeDtypeStruct((rows_here, first), f32),
            jax.ShapeDtypeStruct((second, second), f32),
        ),
        in_specs=[SMEM, VMEM, VMEM],
        out_specs=(VMEM, VMEM),
        scratch_shapes=[pltpu.VMEM((2, layout.rows, LANES), f32), pltpu.VMEM((first, first), f32)],
        compiler_params=ROOM,
        name="mirror",
    )(place, own, other)
    return gram_one, core_out, gram_two


def solution(mesh):
    gx, rest = mesh.devices.shape
    sizes = {"x": gx, "y": 8, "zh": rest // 32, "zl": 2, "c": 2}
    fine = Mesh(mesh.devices.reshape(tuple(sizes.values())), tuple(sizes))
    spread = ("y", "zh", "zl", "c")
    in_specs = (P(spread, "x", None), P("x", None))
    out_specs = (P("x", None), P("x", spread, None), P())
    return jax.shard_map(
        functools.partial(local, sizes), mesh=fine, in_specs=in_specs, out_specs=out_specs, check_vma=False
    )
```

```python
import functools

import jax
import jax.numpy as jnp
from jax import lax
from jax.experimental import pallas as pl
from jax.experimental.pallas import tpu as pltpu
from jax.sharding import Mesh, PartitionSpec as P

LANES = 128
FOLD = LANES // 2
VMEM = pl.BlockSpec(memory_space=pltpu.VMEM)
SMEM = pl.BlockSpec(memory_space=pltpu.SMEM)
ROOM = pltpu.CompilerParams(vmem_limit_bytes=24 << 20)


class Layout:
    def __init__(self, width, unit):
        self.width = width
        self.full = width // LANES
        self.left = width - self.full * LANES
        self.above = [0] * self.full
        row = 0
        for block in range(1, self.full):
            self.above[block] = row
            row += block * LANES
        self.strip = row
        row += self.left * (self.full + 1)
        split = -(-self.full // 2)
        self.fold = [(block // split, row + (block % split) * 3 * FOLD) for block in range(self.full)]
        self.used = [row + split * 3 * FOLD, row + (self.full - split) * 3 * FOLD]
        self.rows = -(-self.used[0] // unit) * unit


def halves(value):
    high = value.astype(jnp.bfloat16)
    low = (value - high.astype(jnp.float32)).astype(jnp.bfloat16)
    return high, low


def dot(a, b):
    return jnp.dot(a, b, preferred_element_type=jnp.float32)


def dot_rows(a, b):
    return lax.dot_general(a, b, (((1,), (1,)), ((), ())), preferred_element_type=jnp.float32)


def lane_below(rows):
    return lax.broadcasted_iota(jnp.int32, (rows, LANES), 1) < FOLD


def pack_gram(layout, product, packed, half):
    full, left, width = layout.full, layout.left, layout.width
    for start in range(0, width, 2 * LANES):
        columns = min(2 * LANES, width - start)
        last = start + columns == width
        group = product(width if last else start + columns, start, columns)
        for block in range(start // LANES, min(full, (start + columns) // LANES)):
            inside = slice(block * LANES - start, (block + 1) * LANES - start)
            above = block * LANES
            if above:
                packed[half, pl.ds(layout.above[block], above), :] = group[:above, inside]
            into, row = layout.fold[block]
            packed[into, pl.ds(row + half * FOLD, FOLD), :] = group[above : above + FOLD, inside]
            lower = group[above + FOLD : above + LANES, inside]
            corner = pl.ds(row + 2 * FOLD, FOLD)
            if half == 0:
                packed[into, corner, :] = pltpu.roll(lower, FOLD, 1)
            else:
                packed[into, corner, :] = jnp.where(lane_below(FOLD), packed[into, corner, :], lower)
        if last:
            strip = group[:, full * LANES - start :]
            for block in range(full):
                piece = strip[block * LANES : (block + 1) * LANES].T
                packed[half, pl.ds(layout.strip + block * left, left), :] = piece
            corner = pl.ds(layout.strip + full * left, left)
            packed[half, corner, :] = jnp.zeros((left, LANES), jnp.float32)
            packed[half, corner, 0:left] = strip[full * LANES :]
    spare = layout.rows - layout.used[half]
    if spare:
        packed[half, pl.ds(layout.used[half], spare), :] = jnp.zeros((spare, LANES), jnp.float32)


def dense_rows(rows, width):
    full = width // LANES
    left = width - full * LANES
    beside = LANES // left
    group = -(-rows // (8 * beside)) * 8
    return full, left, beside, group, rows * (full + 1) + group


def dense_kernel(field_ref, basis_ref, out_ref):
    blocks, rows, width = field_ref.shape
    full, left, beside, group, _ = dense_rows(rows, width)
    base = (full + 1) * rows
    for block in range(blocks):
        for part in range(full):
            out_ref[block, pl.ds(part * rows, rows), :] = field_ref[block, :, part * LANES : (part + 1) * LANES]
        out_ref[block, pl.ds(full * rows, rows), :] = basis_ref[...]
        for part in range(beside):
            some = min(group, rows - part * group)
            lanes = slice(part * left, (part + 1) * left)
            piece = field_ref[block, pl.ds(part * group, some), full * LANES : width]
            out_ref[block, pl.ds(base, some), lanes] = piece
            if some < group:
                out_ref[block, pl.ds(base + some, group - some), lanes] = jnp.zeros((group - some, left), jnp.float32)


def gram_kernel(
    layout, place_ref, dense_ref, keep_ref, send_ref, core_ref,
    field, basis, field_high, field_low, left_side, right_side, packed,
):
    blocks = dense_ref.shape[0]
    first, width = field.shape
    rank = basis.shape[1]
    rows = first // blocks
    full, left, beside, group, _ = dense_rows(rows, width)
    base = (full + 1) * rows
    for owner in range(blocks):
        own = owner * rows
        for part in range(full):
            field[pl.ds(own, rows), part * LANES : (part + 1) * LANES] = dense_ref[owner, pl.ds(part * rows, rows), :]
        basis[pl.ds(own, rows), :] = dense_ref[owner, pl.ds(full * rows, rows), :]
        for part in range(beside):
            some = min(group, rows - part * group)
            piece = dense_ref[owner, pl.ds(base, some), part * left : (part + 1) * left]
            field[pl.ds(own + part * group, some), full * LANES : width] = piece
    high, low = halves(field[...])
    field_high[...] = high
    field_low[...] = low
    basis_high, basis_low = halves(basis[...].T)
    core = dot(basis_high, high) + (dot(basis_high, low) + dot(basis_low, high))
    core_ref[...] = core
    high, low = halves(core.T)
    left_side[:, 0:rank] = high
    left_side[:, rank : 2 * rank] = low
    right_side[:, 0:rank] = high
    right_side[:, rank : 2 * rank] = high

    def field_product(rows, start, columns):
        lh, ll = field_high[pl.ds(0, rows), :], field_low[pl.ds(0, rows), :]
        rh, rl = field_high[pl.ds(start, columns), :], field_low[pl.ds(start, columns), :]
        return dot_rows(lh, rh) + (dot_rows(lh, rl) + dot_rows(ll, rh))

    def core_product(rows, start, columns):
        here, there = pl.ds(0, rows), pl.ds(start, columns)
        both = dot_rows(left_side[here, :], right_side[there, :])
        return both + dot_rows(left_side[here, 0:rank], left_side[there, rank : 2 * rank])

    pack_gram(layout, field_product, packed, 0)
    pack_gram(layout, core_product, packed, 1)
    mine = place_ref[1]
    keep_ref[...] = packed[mine]
    send_ref[...] = packed[1 - mine]


def parts_kernel(place_ref, core_ref, after_ref, *out_refs):
    owned = out_refs[0].shape[0]
    for step, out_ref in enumerate(out_refs):
        owner = lax.rem(place_ref[0] + step, len(out_refs))
        out_ref[...] = core_ref[pl.ds(pl.multiple_of(owner * owned, 8), owned), :]


def rows_kernel(place_ref, *refs):
    came, (out_ref, ordered) = refs[:-2], refs[-2:]
    count = len(came)
    for step, ref in enumerate(came):
        ordered[lax.rem(place_ref[0] + count - step, count)] = ref[...]
    for owner in range(count):
        out_ref[:, owner, :] = ordered[owner]


def unpack(layout, packed, half, out_ref, scale):
    full, left = layout.full, layout.left
    for block in range(full):
        columns = pl.ds(block * LANES, LANES)
        for row in range(block):
            there = pl.ds(row * LANES, LANES)
            tile = packed[half, pl.ds(layout.above[block] + row * LANES, LANES), :] * scale
            out_ref[there, columns] = tile
            out_ref[columns, there] = tile.T
        into, row = layout.fold[block]
        upper = packed[into, pl.ds(row + half * FOLD, FOLD), :] * scale
        lower = packed[into, pl.ds(row + 2 * FOLD, FOLD), :] * scale
        if half == 0:
            lower = pltpu.roll(lower, FOLD, 1)
        turned = jnp.concatenate([upper, upper], axis=0).T[FOLD:]
        out_ref[pl.ds(block * LANES, FOLD), columns] = upper
        out_ref[pl.ds(block * LANES + FOLD, FOLD), columns] = jnp.where(lane_below(FOLD), turned, lower)
        tile = packed[half, pl.ds(layout.strip + block * left, left), :] * scale
        out_ref[pl.ds(full * LANES, left), columns] = tile
        out_ref[columns, pl.ds(full * LANES, left)] = tile.T
    corner = packed[half, pl.ds(layout.strip + full * left, left), :] * scale
    out_ref[pl.ds(full * LANES, left), pl.ds(full * LANES, left)] = corner[:, 0:left]


def unpack_kernel(layout, scale_one, scale_two, place_ref, own_ref, other_ref, one_ref, two_ref, packed, whole):
    rows = one_ref.shape[0]
    mine = place_ref[1]
    packed[mine] = own_ref[...]
    packed[1 - mine] = other_ref[...]
    unpack(layout, packed, 0, whole, scale_one)
    one_ref[...] = whole[pl.ds(pl.multiple_of(place_ref[0] * rows, 8), rows), :]
    unpack(layout, packed, 1, two_ref, scale_two)


def exchange(parts, axis):
    return lax.all_to_all(parts, axis, 0, 0, tiled=True)


def copies(value, count):
    return jnp.broadcast_to(value[None], (count,) + value.shape)


def cost(flops, moved):
    return pl.CostEstimate(flops=flops, transcendentals=0, bytes_accessed=moved)


def scatter_sum(value, axes, count):
    return jnp.sum(exchange(value.reshape(count, -1, LANES), axes), axis=0)


def gather(value, axes, count):
    return exchange(copies(value, count), axes).reshape(-1, LANES)


def local(sizes, tensor, basis):
    gx = sizes["x"]
    slices_here, rows_here, second = tensor.shape
    first = rows_here * gx
    rank = basis.shape[1]
    near, far = ("x", "zl"), ("y", "zh")
    near_count, far_count = gx * sizes["zl"], sizes["y"] * sizes["zh"]
    slices_all = slices_here * sizes["y"] * sizes["zh"] * sizes["zl"] * sizes["c"]
    layout = Layout(first, 8 * near_count * far_count)
    dense = dense_rows(rows_here, second)[-1]
    swap = [(i, sizes["c"] - 1 - i) for i in range(sizes["c"])]
    place = jnp.stack([lax.axis_index("x"), lax.axis_index("c")]).astype(jnp.int32)
    f32, bf16 = jnp.float32, jnp.bfloat16

    blocks = pl.pallas_call(
        dense_kernel,
        out_shape=jax.ShapeDtypeStruct((slices_here, dense, LANES), f32),
        in_specs=[VMEM, VMEM],
        out_specs=VMEM,
        compiler_params=ROOM,
        name="dense_blocks",
    )(tensor, basis)
    blocks, place = lax.optimization_barrier((blocks, place))
    blocks = exchange(blocks, "x")
    half_shape = jax.ShapeDtypeStruct((layout.rows, LANES), f32)
    keep, send, core = pl.pallas_call(
        functools.partial(gram_kernel, layout),
        out_shape=(half_shape, half_shape, jax.ShapeDtypeStruct((rank, second), f32)),
        in_specs=[SMEM, VMEM],
        out_specs=(VMEM, VMEM, VMEM),
        scratch_shapes=[
            pltpu.VMEM((first, second), f32),
            pltpu.VMEM((first, rank), f32),
            pltpu.VMEM((first, second), bf16),
            pltpu.VMEM((first, second), bf16),
            pltpu.VMEM((second, 2 * rank), bf16),
            pltpu.VMEM((second, 2 * rank), bf16),
            pltpu.VMEM((2, layout.rows, LANES), f32),
        ],
        compiler_params=ROOM,
        cost_estimate=cost(5 * first * first * second, 12 * first * second),
        name="local_grams",
    )(place, blocks)

    came = lax.ppermute(send, "c", swap)
    sums = keep + came
    owned = rank // gx
    core_parts = pl.pallas_call(
        parts_kernel,
        out_shape=[jax.ShapeDtypeStruct((owned, second), f32)] * gx,
        in_specs=[SMEM, VMEM, pl.BlockSpec(memory_space=pl.ANY)],
        out_specs=[VMEM] * gx,
        compiler_params=ROOM,
        cost_estimate=cost(rank * second, 8 * rank * second),
        name="core_parts",
    )(place, core, came)
    came_core = [core_parts[0]]
    for step in range(1, gx):
        shift = [(i, (i + step) % gx) for i in range(gx)]
        came_core.append(lax.ppermute(core_parts[step], "x", shift))
    part = exchange(sums.reshape(near_count, -1, LANES), near)
    part, *came_core = lax.optimization_barrier((part, *came_core))
    part = scatter_sum(jnp.sum(part, axis=0), far, far_count)
    core_out = pl.pallas_call(
        rows_kernel,
        out_shape=jax.ShapeDtypeStruct((owned, gx, second), f32),
        in_specs=[SMEM] + [VMEM] * gx,
        out_specs=VMEM,
        scratch_shapes=[pltpu.VMEM((gx, owned, second), f32)],
        compiler_params=ROOM,
        cost_estimate=cost(rank * second, 8 * rank * second),
        name="core_rows",
    )(place, *came_core)
    own = gather(gather(part, far, far_count), near, near_count)
    other = lax.ppermute(own, "c", swap)

    gram_one, gram_two = pl.pallas_call(
        functools.partial(unpack_kernel, layout, 1.0 / (slices_all * second), 1.0 / (slices_all * rank)),
        out_shape=(
            jax.ShapeDtypeStruct((rows_here, first), f32),
            jax.ShapeDtypeStruct((second, second), f32),
        ),
        in_specs=[SMEM, VMEM, VMEM],
        out_specs=(VMEM, VMEM),
        scratch_shapes=[pltpu.VMEM((2, layout.rows, LANES), f32), pltpu.VMEM((first, first), f32)],
        compiler_params=ROOM,
        name="mirror",
    )(place, own, other)
    return gram_one, core_out, gram_two


def solution(mesh):
    gx, rest = mesh.devices.shape
    sizes = {"x": gx, "y": 8, "zh": rest // 32, "zl": 2, "c": 2}
    fine = Mesh(mesh.devices.reshape(tuple(sizes.values())), tuple(sizes))
    spread = ("y", "zh", "zl", "c")
    in_specs = (P(spread, "x", None), P("x", None))
    out_specs = (P("x", None), P("x", spread, None), P())
    return jax.shard_map(
        functools.partial(local, sizes), mesh=fine, in_specs=in_specs, out_specs=out_specs, check_vma=False
    )
```

```python
import functools

import jax
import jax.numpy as jnp
import numpy as np
from jax import lax
from jax.experimental import pallas as pl
from jax.experimental.pallas import tpu as pltpu
from jax.sharding import Mesh, PartitionSpec as P

LANES = 128
FOLD = LANES // 2
VMEM = pl.BlockSpec(memory_space=pltpu.VMEM)
SMEM = pl.BlockSpec(memory_space=pltpu.SMEM)
ROOM = pltpu.CompilerParams(vmem_limit_bytes=24 << 20)


class Layout:
    def __init__(self, width, unit):
        self.width = width
        self.full = width // LANES
        self.left = width - self.full * LANES
        self.above = [0] * self.full
        row = 0
        for block in range(1, self.full):
            self.above[block] = row
            row += block * LANES
        self.strip = row
        row += self.left * (self.full + 1)
        split = -(-self.full // 2)
        self.fold = [(block // split, row + (block % split) * 3 * FOLD) for block in range(self.full)]
        self.used = [row + split * 3 * FOLD, row + (self.full - split) * 3 * FOLD]
        self.rows = -(-self.used[0] // unit) * unit


def halves(value):
    high = value.astype(jnp.bfloat16)
    low = (value - high.astype(jnp.float32)).astype(jnp.bfloat16)
    return high, low


def dot(a, b):
    return jnp.dot(a, b, preferred_element_type=jnp.float32)


def dot_rows(a, b):
    return lax.dot_general(a, b, (((1,), (1,)), ((), ())), preferred_element_type=jnp.float32)


def lane_below(rows):
    return lax.broadcasted_iota(jnp.int32, (rows, LANES), 1) < FOLD


def pack_gram(layout, product, packed, half):
    full, left, width = layout.full, layout.left, layout.width
    for start in range(0, width, 2 * LANES):
        columns = min(2 * LANES, width - start)
        last = start + columns == width
        group = product(width if last else start + columns, start, columns)
        for block in range(start // LANES, min(full, (start + columns) // LANES)):
            inside = slice(block * LANES - start, (block + 1) * LANES - start)
            above = block * LANES
            if above:
                packed[half, pl.ds(layout.above[block], above), :] = group[:above, inside]
            into, row = layout.fold[block]
            packed[into, pl.ds(row + half * FOLD, FOLD), :] = group[above : above + FOLD, inside]
            lower = group[above + FOLD : above + LANES, inside]
            corner = pl.ds(row + 2 * FOLD, FOLD)
            if half == 0:
                packed[into, corner, :] = pltpu.roll(lower, FOLD, 1)
            else:
                packed[into, corner, :] = jnp.where(lane_below(FOLD), packed[into, corner, :], lower)
        if last:
            strip = group[:, full * LANES - start :]
            for block in range(full):
                piece = strip[block * LANES : (block + 1) * LANES].T
                packed[half, pl.ds(layout.strip + block * left, left), :] = piece
            corner = pl.ds(layout.strip + full * left, left)
            packed[half, corner, :] = jnp.zeros((left, LANES), jnp.float32)
            packed[half, corner, 0:left] = strip[full * LANES :]
    spare = layout.rows - layout.used[half]
    if spare:
        packed[half, pl.ds(layout.used[half], spare), :] = jnp.zeros((spare, LANES), jnp.float32)


def dense_rows(rows, width):
    full = width // LANES
    left = width - full * LANES
    beside = LANES // left
    group = -(-rows // (8 * beside)) * 8
    return full, left, beside, group, rows * (full + 1) + group


def dense_kernel(field_ref, basis_ref, out_ref):
    blocks, rows, width = field_ref.shape
    full, left, beside, group, _ = dense_rows(rows, width)
    base = (full + 1) * rows
    for block in range(blocks):
        for part in range(full):
            out_ref[block, pl.ds(part * rows, rows), :] = field_ref[block, :, part * LANES : (part + 1) * LANES]
        out_ref[block, pl.ds(full * rows, rows), :] = basis_ref[...]
        for part in range(beside):
            some = min(group, rows - part * group)
            lanes = slice(part * left, (part + 1) * left)
            piece = field_ref[block, pl.ds(part * group, some), full * LANES : width]
            out_ref[block, pl.ds(base, some), lanes] = piece
            if some < group:
                out_ref[block, pl.ds(base + some, group - some), lanes] = jnp.zeros((group - some, left), jnp.float32)


def gram_kernel(
    layout, place_ref, dense_ref, keep_ref, send_ref, core_ref,
    field, basis, field_high, field_low, left_side, right_side, packed,
):
    blocks = dense_ref.shape[0]
    first, width = field.shape
    rank = basis.shape[1]
    rows = first // blocks
    full, left, beside, group, _ = dense_rows(rows, width)
    base = (full + 1) * rows
    for owner in range(blocks):
        own = owner * rows
        for part in range(full):
            field[pl.ds(own, rows), part * LANES : (part + 1) * LANES] = dense_ref[owner, pl.ds(part * rows, rows), :]
        basis[pl.ds(own, rows), :] = dense_ref[owner, pl.ds(full * rows, rows), :]
        for part in range(beside):
            some = min(group, rows - part * group)
            piece = dense_ref[owner, pl.ds(base, some), part * left : (part + 1) * left]
            field[pl.ds(own + part * group, some), full * LANES : width] = piece
    high, low = halves(field[...])
    field_high[...] = high
    field_low[...] = low
    basis_high, basis_low = halves(basis[...].T)
    core = dot(basis_high, high) + (dot(basis_high, low) + dot(basis_low, high))
    core_ref[...] = core
    high, low = halves(core.T)
    left_side[:, 0:rank] = high
    left_side[:, rank : 2 * rank] = low
    right_side[:, 0:rank] = high
    right_side[:, rank : 2 * rank] = high

    def field_product(rows, start, columns):
        lh, ll = field_high[pl.ds(0, rows), :], field_low[pl.ds(0, rows), :]
        rh, rl = field_high[pl.ds(start, columns), :], field_low[pl.ds(start, columns), :]
        return dot_rows(lh, rh) + (dot_rows(lh, rl) + dot_rows(ll, rh))

    def core_product(rows, start, columns):
        here, there = pl.ds(0, rows), pl.ds(start, columns)
        both = dot_rows(left_side[here, :], right_side[there, :])
        return both + dot_rows(left_side[here, 0:rank], left_side[there, rank : 2 * rank])

    pack_gram(layout, field_product, packed, 0)
    pack_gram(layout, core_product, packed, 1)
    mine = place_ref[1]
    keep_ref[...] = packed[mine]
    send_ref[...] = packed[1 - mine]


def parts_kernel(place_ref, core_ref, after_ref, *out_refs):
    owned = out_refs[0].shape[0]
    for step, out_ref in enumerate(out_refs):
        owner = lax.rem(place_ref[0] + step, len(out_refs))
        out_ref[...] = core_ref[pl.ds(pl.multiple_of(owner * owned, 8), owned), :]


def rows_kernel(place_ref, *refs):
    came, (out_ref, ordered) = refs[:-2], refs[-2:]
    count = len(came)
    for step, ref in enumerate(came):
        ordered[lax.rem(place_ref[0] + count - step, count)] = ref[...]
    for owner in range(count):
        out_ref[:, owner, :] = ordered[owner]


def unpack(layout, packed, half, out_ref, scale):
    full, left = layout.full, layout.left
    for block in range(full):
        columns = pl.ds(block * LANES, LANES)
        for row in range(block):
            there = pl.ds(row * LANES, LANES)
            tile = packed[half, pl.ds(layout.above[block] + row * LANES, LANES), :] * scale
            out_ref[there, columns] = tile
            out_ref[columns, there] = tile.T
        into, row = layout.fold[block]
        upper = packed[into, pl.ds(row + half * FOLD, FOLD), :] * scale
        lower = packed[into, pl.ds(row + 2 * FOLD, FOLD), :] * scale
        if half == 0:
            lower = pltpu.roll(lower, FOLD, 1)
        turned = jnp.concatenate([upper, upper], axis=0).T[FOLD:]
        out_ref[pl.ds(block * LANES, FOLD), columns] = upper
        out_ref[pl.ds(block * LANES + FOLD, FOLD), columns] = jnp.where(lane_below(FOLD), turned, lower)
        tile = packed[half, pl.ds(layout.strip + block * left, left), :] * scale
        out_ref[pl.ds(full * LANES, left), columns] = tile
        out_ref[columns, pl.ds(full * LANES, left)] = tile.T
    corner = packed[half, pl.ds(layout.strip + full * left, left), :] * scale
    out_ref[pl.ds(full * LANES, left), pl.ds(full * LANES, left)] = corner[:, 0:left]


def unpack_kernel(layout, scale_one, scale_two, place_ref, own_ref, other_ref, one_ref, two_ref, packed, whole):
    rows = one_ref.shape[0]
    mine = place_ref[1]
    packed[mine] = own_ref[...]
    packed[1 - mine] = other_ref[...]
    unpack(layout, packed, 0, whole, scale_one)
    one_ref[...] = whole[pl.ds(pl.multiple_of(place_ref[0] * rows, 8), rows), :]
    unpack(layout, packed, 1, two_ref, scale_two)


def exchange(parts, axes, groups=None):
    return lax.all_to_all(parts, axes, 0, 0, axis_index_groups=groups, tiled=True)


def copies(value, count):
    return jnp.broadcast_to(value[None], (count,) + value.shape)


def cost(flops, moved):
    return pl.CostEstimate(flops=flops, transcendentals=0, bytes_accessed=moved)


def both_groups(sizes):
    shape = tuple(sizes.values())
    index = np.arange(np.prod(shape)).reshape(shape)
    near = [index[:, a, b, d, e, 0] for a, b, d, e in np.ndindex(shape[1:5])]
    near += [index[a, b, :, d, :, 1] for a, b, d in np.ndindex(shape[0], shape[1], shape[3])]
    far = [index[a, ..., 0] for a in range(shape[0])]
    far += [index[:, :, b, :, e, 1] for b, e in np.ndindex(shape[2], shape[4])]
    return [[group.reshape(-1).tolist() for group in groups] for groups in (near, far)]


def local(sizes, tensor, basis):
    gx = sizes["x"]
    slices_here, rows_here, second = tensor.shape
    first = rows_here * gx
    rank = basis.shape[1]
    axes = tuple(sizes)
    near, far = both_groups(sizes)
    near_count, far_count = len(near[0]), len(far[0])
    slices_all = slices_here * near_count * far_count // gx * sizes["c"]
    layout = Layout(first, 8 * near_count * far_count)
    dense = dense_rows(rows_here, second)[-1]
    swap = [(i, sizes["c"] - 1 - i) for i in range(sizes["c"])]
    place = jnp.stack([lax.axis_index("x"), lax.axis_index("c")]).astype(jnp.int32)
    f32, bf16 = jnp.float32, jnp.bfloat16

    blocks = pl.pallas_call(
        dense_kernel,
        out_shape=jax.ShapeDtypeStruct((slices_here, dense, LANES), f32),
        in_specs=[VMEM, VMEM],
        out_specs=VMEM,
        compiler_params=ROOM,
        name="dense_blocks",
    )(tensor, basis)
    blocks, place = lax.optimization_barrier((blocks, place))
    blocks = exchange(blocks, "x")
    half_shape = jax.ShapeDtypeStruct((layout.rows, LANES), f32)
    keep, send, core = pl.pallas_call(
        functools.partial(gram_kernel, layout),
        out_shape=(half_shape, half_shape, jax.ShapeDtypeStruct((rank, second), f32)),
        in_specs=[SMEM, VMEM],
        out_specs=(VMEM, VMEM, VMEM),
        scratch_shapes=[
            pltpu.VMEM((first, second), f32),
            pltpu.VMEM((first, rank), f32),
            pltpu.VMEM((first, second), bf16),
            pltpu.VMEM((first, second), bf16),
            pltpu.VMEM((second, 2 * rank), bf16),
            pltpu.VMEM((second, 2 * rank), bf16),
            pltpu.VMEM((2, layout.rows, LANES), f32),
        ],
        compiler_params=ROOM,
        cost_estimate=cost(5 * first * first * second, 12 * first * second),
        name="local_grams",
    )(place, blocks)

    came = lax.ppermute(send, "c", swap)
    sums = keep + came
    owned = rank // gx
    core_parts = pl.pallas_call(
        parts_kernel,
        out_shape=[jax.ShapeDtypeStruct((owned, second), f32)] * gx,
        in_specs=[SMEM, VMEM, pl.BlockSpec(memory_space=pl.ANY)],
        out_specs=[VMEM] * gx,
        compiler_params=ROOM,
        cost_estimate=cost(rank * second, 8 * rank * second),
        name="core_parts",
    )(place, core, came)
    came_core = [core_parts[0]]
    for step in range(1, gx):
        shift = [(i, (i + step) % gx) for i in range(gx)]
        came_core.append(lax.ppermute(core_parts[step], "x", shift))
    part = exchange(sums.reshape(near_count, -1, LANES), axes, near)
    part, *came_core = lax.optimization_barrier((part, *came_core))
    part = exchange(jnp.sum(part, axis=0).reshape(far_count, -1, LANES), axes, far)
    core_out = pl.pallas_call(
        rows_kernel,
        out_shape=jax.ShapeDtypeStruct((owned, gx, second), f32),
        in_specs=[SMEM] + [VMEM] * gx,
        out_specs=VMEM,
        scratch_shapes=[pltpu.VMEM((gx, owned, second), f32)],
        compiler_params=ROOM,
        cost_estimate=cost(rank * second, 8 * rank * second),
        name="core_rows",
    )(place, *came_core)
    part = exchange(copies(jnp.sum(part, axis=0), far_count), axes, far).reshape(-1, LANES)
    own = exchange(copies(part, near_count), axes, near).reshape(-1, LANES)
    other = lax.ppermute(own, "c", swap)

    gram_one, gram_two = pl.pallas_call(
        functools.partial(unpack_kernel, layout, 1.0 / (slices_all * second), 1.0 / (slices_all * rank)),
        out_shape=(
            jax.ShapeDtypeStruct((rows_here, first), f32),
            jax.ShapeDtypeStruct((second, second), f32),
        ),
        in_specs=[SMEM, VMEM, VMEM],
        out_specs=(VMEM, VMEM),
        scratch_shapes=[pltpu.VMEM((2, layout.rows, LANES), f32), pltpu.VMEM((first, first), f32)],
        compiler_params=ROOM,
        name="mirror",
    )(place, own, other)
    return gram_one, core_out, gram_two


def solution(mesh):
    gx, rest = mesh.devices.shape
    sizes = {"x": gx, "yh": 4, "yl": 2, "zh": rest // 32, "zl": 2, "c": 2}
    fine = Mesh(mesh.devices.reshape(tuple(sizes.values())), tuple(sizes))
    spread = ("yh", "yl", "zh", "zl", "c")
    in_specs = (P(spread, "x", None), P("x", None))
    out_specs = (P("x", None), P("x", spread, None), P())
    return jax.shard_map(
        functools.partial(local, sizes), mesh=fine, in_specs=in_specs, out_specs=out_specs, check_vma=False
    )
```

```python
import functools

import jax
import jax.numpy as jnp
import numpy as np
from jax import lax
from jax.experimental import pallas as pl
from jax.experimental.pallas import tpu as pltpu
from jax.sharding import Mesh, PartitionSpec as P

LANES = 128
FOLD = LANES // 2
VMEM = pl.BlockSpec(memory_space=pltpu.VMEM)
SMEM = pl.BlockSpec(memory_space=pltpu.SMEM)
ROOM = pltpu.CompilerParams(vmem_limit_bytes=24 << 20)


class Layout:
    def __init__(self, width, unit):
        self.width = width
        self.full = width // LANES
        self.left = width - self.full * LANES
        self.above = [0] * self.full
        row = 0
        for block in range(1, self.full):
            self.above[block] = row
            row += block * LANES
        self.strip = row
        row += self.left * (self.full + 1)
        split = -(-self.full // 2)
        self.fold = [(block // split, row + (block % split) * 3 * FOLD) for block in range(self.full)]
        self.used = [row + split * 3 * FOLD, row + (self.full - split) * 3 * FOLD]
        self.rows = -(-self.used[0] // unit) * unit


def halves(value):
    high = value.astype(jnp.bfloat16)
    low = (value - high.astype(jnp.float32)).astype(jnp.bfloat16)
    return high, low


def dot(a, b):
    return jnp.dot(a, b, preferred_element_type=jnp.float32)


def dot_rows(a, b):
    return lax.dot_general(a, b, (((1,), (1,)), ((), ())), preferred_element_type=jnp.float32)


def lane_below(rows):
    return lax.broadcasted_iota(jnp.int32, (rows, LANES), 1) < FOLD


def pack_gram(layout, product, packed, half):
    full, left, width = layout.full, layout.left, layout.width
    for start in range(0, width, 2 * LANES):
        columns = min(2 * LANES, width - start)
        last = start + columns == width
        group = product(width if last else start + columns, start, columns)
        for block in range(start // LANES, min(full, (start + columns) // LANES)):
            inside = slice(block * LANES - start, (block + 1) * LANES - start)
            above = block * LANES
            if above:
                packed[half, pl.ds(layout.above[block], above), :] = group[:above, inside]
            into, row = layout.fold[block]
            packed[into, pl.ds(row + half * FOLD, FOLD), :] = group[above : above + FOLD, inside]
            lower = group[above + FOLD : above + LANES, inside]
            corner = pl.ds(row + 2 * FOLD, FOLD)
            if half == 0:
                packed[into, corner, :] = pltpu.roll(lower, FOLD, 1)
            else:
                packed[into, corner, :] = jnp.where(lane_below(FOLD), packed[into, corner, :], lower)
        if last:
            strip = group[:, full * LANES - start :]
            for block in range(full):
                piece = strip[block * LANES : (block + 1) * LANES].T
                packed[half, pl.ds(layout.strip + block * left, left), :] = piece
            corner = pl.ds(layout.strip + full * left, left)
            packed[half, corner, :] = jnp.zeros((left, LANES), jnp.float32)
            packed[half, corner, 0:left] = strip[full * LANES :]
    spare = layout.rows - layout.used[half]
    if spare:
        packed[half, pl.ds(layout.used[half], spare), :] = jnp.zeros((spare, LANES), jnp.float32)


def dense_rows(rows, width):
    full = width // LANES
    left = width - full * LANES
    beside = LANES // left
    group = -(-rows // (8 * beside)) * 8
    return full, left, beside, group, rows * (full + 1) + group


def dense_kernel(field_ref, basis_ref, out_ref):
    blocks, rows, width = field_ref.shape
    full, left, beside, group, _ = dense_rows(rows, width)
    base = (full + 1) * rows
    for block in range(blocks):
        for part in range(full):
            out_ref[block, pl.ds(part * rows, rows), :] = field_ref[block, :, part * LANES : (part + 1) * LANES]
        out_ref[block, pl.ds(full * rows, rows), :] = basis_ref[...]
        for part in range(beside):
            some = min(group, rows - part * group)
            lanes = slice(part * left, (part + 1) * left)
            piece = field_ref[block, pl.ds(part * group, some), full * LANES : width]
            out_ref[block, pl.ds(base, some), lanes] = piece
            if some < group:
                out_ref[block, pl.ds(base + some, group - some), lanes] = jnp.zeros((group - some, left), jnp.float32)


def gram_kernel(
    layout, place_ref, dense_ref, keep_ref, send_ref, core_ref,
    field, basis, field_high, field_low, left_side, right_side, packed,
):
    blocks = dense_ref.shape[0]
    first, width = field.shape
    rank = basis.shape[1]
    rows = first // blocks
    full, left, beside, group, _ = dense_rows(rows, width)
    base = (full + 1) * rows
    for owner in range(blocks):
        own = owner * rows
        for part in range(full):
            field[pl.ds(own, rows), part * LANES : (part + 1) * LANES] = dense_ref[owner, pl.ds(part * rows, rows), :]
        basis[pl.ds(own, rows), :] = dense_ref[owner, pl.ds(full * rows, rows), :]
        for part in range(beside):
            some = min(group, rows - part * group)
            piece = dense_ref[owner, pl.ds(base, some), part * left : (part + 1) * left]
            field[pl.ds(own + part * group, some), full * LANES : width] = piece
    high, low = halves(field[...])
    field_high[...] = high
    field_low[...] = low
    basis_high, basis_low = halves(basis[...].T)
    core = dot(basis_high, high) + (dot(basis_high, low) + dot(basis_low, high))
    core_ref[...] = core
    high, low = halves(core.T)
    left_side[:, 0:rank] = high
    left_side[:, rank : 2 * rank] = low
    right_side[:, 0:rank] = high
    right_side[:, rank : 2 * rank] = high

    def field_product(rows, start, columns):
        lh, ll = field_high[pl.ds(0, rows), :], field_low[pl.ds(0, rows), :]
        rh, rl = field_high[pl.ds(start, columns), :], field_low[pl.ds(start, columns), :]
        return dot_rows(lh, rh) + (dot_rows(lh, rl) + dot_rows(ll, rh))

    def core_product(rows, start, columns):
        here, there = pl.ds(0, rows), pl.ds(start, columns)
        both = dot_rows(left_side[here, :], right_side[there, :])
        return both + dot_rows(left_side[here, 0:rank], left_side[there, rank : 2 * rank])

    pack_gram(layout, field_product, packed, 0)
    pack_gram(layout, core_product, packed, 1)
    mine = place_ref[1]
    keep_ref[...] = packed[mine]
    send_ref[...] = packed[1 - mine]


def parts_kernel(place_ref, core_ref, after_ref, *out_refs):
    owned = out_refs[0].shape[0]
    for step, out_ref in enumerate(out_refs):
        owner = lax.rem(place_ref[0] + step, len(out_refs))
        out_ref[...] = core_ref[pl.ds(pl.multiple_of(owner * owned, 8), owned), :]


def rows_kernel(place_ref, *refs):
    came, (out_ref, ordered) = refs[:-2], refs[-2:]
    count = len(came)
    for step, ref in enumerate(came):
        ordered[lax.rem(place_ref[0] + count - step, count)] = ref[...]
    for owner in range(count):
        out_ref[:, owner, :] = ordered[owner]


def unpack(layout, packed, half, out_ref, scale):
    full, left = layout.full, layout.left
    for block in range(full):
        columns = pl.ds(block * LANES, LANES)
        for row in range(block):
            there = pl.ds(row * LANES, LANES)
            tile = packed[half, pl.ds(layout.above[block] + row * LANES, LANES), :] * scale
            out_ref[there, columns] = tile
            out_ref[columns, there] = tile.T
        into, row = layout.fold[block]
        upper = packed[into, pl.ds(row + half * FOLD, FOLD), :] * scale
        lower = packed[into, pl.ds(row + 2 * FOLD, FOLD), :] * scale
        if half == 0:
            lower = pltpu.roll(lower, FOLD, 1)
        turned = jnp.concatenate([upper, upper], axis=0).T[FOLD:]
        out_ref[pl.ds(block * LANES, FOLD), columns] = upper
        out_ref[pl.ds(block * LANES + FOLD, FOLD), columns] = jnp.where(lane_below(FOLD), turned, lower)
        tile = packed[half, pl.ds(layout.strip + block * left, left), :] * scale
        out_ref[pl.ds(full * LANES, left), columns] = tile
        out_ref[columns, pl.ds(full * LANES, left)] = tile.T
    corner = packed[half, pl.ds(layout.strip + full * left, left), :] * scale
    out_ref[pl.ds(full * LANES, left), pl.ds(full * LANES, left)] = corner[:, 0:left]


def unpack_kernel(layout, scale_one, scale_two, place_ref, own_ref, other_ref, one_ref, two_ref, packed, whole):
    rows = one_ref.shape[0]
    mine = place_ref[1]
    packed[mine] = own_ref[...]
    packed[1 - mine] = other_ref[...]
    unpack(layout, packed, 0, whole, scale_one)
    one_ref[...] = whole[pl.ds(pl.multiple_of(place_ref[0] * rows, 8), rows), :]
    unpack(layout, packed, 1, two_ref, scale_two)


def exchange(parts, axes, groups=None):
    return lax.all_to_all(parts, axes, 0, 0, axis_index_groups=groups, tiled=True)


def copies(value, count):
    return jnp.broadcast_to(value[None], (count,) + value.shape)


def cost(flops, moved):
    return pl.CostEstimate(flops=flops, transcendentals=0, bytes_accessed=moved)


def both_groups(sizes):
    shape = tuple(sizes.values())
    index = np.arange(np.prod(shape)).reshape(shape)
    near = [index[:, b, d, :, 0] for b, d in np.ndindex(shape[1], shape[2])]
    near += [index[a, :, d, e, 1] for a, d, e in np.ndindex(shape[0], shape[2], shape[3])]
    far = [index[a, :, :, e, 0] for a, e in np.ndindex(shape[0], shape[3])]
    far += [index[:, b, :, :, 1] for b in range(shape[1])]
    return [[group.reshape(-1).tolist() for group in groups] for groups in (near, far)]


def local(sizes, tensor, basis):
    gx = sizes["x"]
    slices_here, rows_here, second = tensor.shape
    first = rows_here * gx
    rank = basis.shape[1]
    axes = tuple(sizes)
    near, far = both_groups(sizes)
    near_count, far_count = len(near[0]), len(far[0])
    slices_all = slices_here * near_count * far_count // gx * sizes["c"]
    layout = Layout(first, 8 * near_count * far_count)
    dense = dense_rows(rows_here, second)[-1]
    swap = [(i, sizes["c"] - 1 - i) for i in range(sizes["c"])]
    place = jnp.stack([lax.axis_index("x"), lax.axis_index("c")]).astype(jnp.int32)
    f32, bf16 = jnp.float32, jnp.bfloat16

    blocks = pl.pallas_call(
        dense_kernel,
        out_shape=jax.ShapeDtypeStruct((slices_here, dense, LANES), f32),
        in_specs=[VMEM, VMEM],
        out_specs=VMEM,
        compiler_params=ROOM,
        name="dense_blocks",
    )(tensor, basis)
    blocks, place = lax.optimization_barrier((blocks, place))
    blocks = exchange(blocks, "x")
    half_shape = jax.ShapeDtypeStruct((layout.rows, LANES), f32)
    keep, send, core = pl.pallas_call(
        functools.partial(gram_kernel, layout),
        out_shape=(half_shape, half_shape, jax.ShapeDtypeStruct((rank, second), f32)),
        in_specs=[SMEM, VMEM],
        out_specs=(VMEM, VMEM, VMEM),
        scratch_shapes=[
            pltpu.VMEM((first, second), f32),
            pltpu.VMEM((first, rank), f32),
            pltpu.VMEM((first, second), bf16),
            pltpu.VMEM((first, second), bf16),
            pltpu.VMEM((second, 2 * rank), bf16),
            pltpu.VMEM((second, 2 * rank), bf16),
            pltpu.VMEM((2, layout.rows, LANES), f32),
        ],
        compiler_params=ROOM,
        cost_estimate=cost(5 * first * first * second, 12 * first * second),
        name="local_grams",
    )(place, blocks)

    came = lax.ppermute(send, "c", swap)
    sums = keep + came
    owned = rank // gx
    core_parts = pl.pallas_call(
        parts_kernel,
        out_shape=[jax.ShapeDtypeStruct((owned, second), f32)] * gx,
        in_specs=[SMEM, VMEM, pl.BlockSpec(memory_space=pl.ANY)],
        out_specs=[VMEM] * gx,
        compiler_params=ROOM,
        cost_estimate=cost(rank * second, 8 * rank * second),
        name="core_parts",
    )(place, core, came)
    came_core = [core_parts[0]]
    for step in range(1, gx):
        shift = [(i, (i + step) % gx) for i in range(gx)]
        came_core.append(lax.ppermute(core_parts[step], "x", shift))
    part = exchange(sums.reshape(near_count, -1, LANES), axes, near)
    part, *came_core = lax.optimization_barrier((part, *came_core))
    part = exchange(jnp.sum(part, axis=0).reshape(far_count, -1, LANES), axes, far)
    core_out = pl.pallas_call(
        rows_kernel,
        out_shape=jax.ShapeDtypeStruct((owned, gx, second), f32),
        in_specs=[SMEM] + [VMEM] * gx,
        out_specs=VMEM,
        scratch_shapes=[pltpu.VMEM((gx, owned, second), f32)],
        compiler_params=ROOM,
        cost_estimate=cost(rank * second, 8 * rank * second),
        name="core_rows",
    )(place, *came_core)
    part = exchange(copies(jnp.sum(part, axis=0), far_count), axes, far).reshape(-1, LANES)
    own = exchange(copies(part, near_count), axes, near).reshape(-1, LANES)
    other = lax.ppermute(own, "c", swap)

    gram_one, gram_two = pl.pallas_call(
        functools.partial(unpack_kernel, layout, 1.0 / (slices_all * second), 1.0 / (slices_all * rank)),
        out_shape=(
            jax.ShapeDtypeStruct((rows_here, first), f32),
            jax.ShapeDtypeStruct((second, second), f32),
        ),
        in_specs=[SMEM, VMEM, VMEM],
        out_specs=(VMEM, VMEM),
        scratch_shapes=[pltpu.VMEM((2, layout.rows, LANES), f32), pltpu.VMEM((first, first), f32)],
        compiler_params=ROOM,
        name="mirror",
    )(place, own, other)
    return gram_one, core_out, gram_two


def solution(mesh):
    gx, rest = mesh.devices.shape
    sizes = {"x": gx, "y": 8, "zh": rest // 32, "zl": 2, "c": 2}
    fine = Mesh(mesh.devices.reshape(tuple(sizes.values())), tuple(sizes))
    spread = ("y", "zh", "zl", "c")
    in_specs = (P(spread, "x", None), P("x", None))
    out_specs = (P("x", None), P("x", spread, None), P())
    return jax.shard_map(
        functools.partial(local, sizes), mesh=fine, in_specs=in_specs, out_specs=out_specs, check_vma=False
    )
```

```python
import functools

import jax
import jax.numpy as jnp
import numpy as np
from jax import lax
from jax.experimental import pallas as pl
from jax.experimental.pallas import tpu as pltpu
from jax.sharding import Mesh, PartitionSpec as P

LANES = 128
FOLD = LANES // 2
VMEM = pl.BlockSpec(memory_space=pltpu.VMEM)
SMEM = pl.BlockSpec(memory_space=pltpu.SMEM)
ROOM = pltpu.CompilerParams(vmem_limit_bytes=24 << 20)


class Layout:
    def __init__(self, width, unit):
        self.width = width
        self.full = width // LANES
        self.left = width - self.full * LANES
        self.above = [0] * self.full
        row = 0
        for block in range(1, self.full):
            self.above[block] = row
            row += block * LANES
        self.strip = row
        row += self.left * (self.full + 1)
        split = -(-self.full // 2)
        self.fold = [(block // split, row + (block % split) * 3 * FOLD) for block in range(self.full)]
        self.used = [row + split * 3 * FOLD, row + (self.full - split) * 3 * FOLD]
        self.rows = -(-self.used[0] // unit) * unit


def halves(value):
    high = value.astype(jnp.bfloat16)
    low = (value - high.astype(jnp.float32)).astype(jnp.bfloat16)
    return high, low


def dot(a, b):
    return jnp.dot(a, b, preferred_element_type=jnp.float32)


def dot_rows(a, b):
    return lax.dot_general(a, b, (((1,), (1,)), ((), ())), preferred_element_type=jnp.float32)


def lane_below(rows):
    return lax.broadcasted_iota(jnp.int32, (rows, LANES), 1) < FOLD


def pack_gram(layout, product, packed, half):
    full, left, width = layout.full, layout.left, layout.width
    for start in range(0, width, 2 * LANES):
        columns = min(2 * LANES, width - start)
        last = start + columns == width
        group = product(width if last else start + columns, start, columns)
        for block in range(start // LANES, min(full, (start + columns) // LANES)):
            inside = slice(block * LANES - start, (block + 1) * LANES - start)
            above = block * LANES
            if above:
                packed[half, pl.ds(layout.above[block], above), :] = group[:above, inside]
            into, row = layout.fold[block]
            packed[into, pl.ds(row + half * FOLD, FOLD), :] = group[above : above + FOLD, inside]
            lower = group[above + FOLD : above + LANES, inside]
            corner = pl.ds(row + 2 * FOLD, FOLD)
            if half == 0:
                packed[into, corner, :] = pltpu.roll(lower, FOLD, 1)
            else:
                packed[into, corner, :] = jnp.where(lane_below(FOLD), packed[into, corner, :], lower)
        if last:
            strip = group[:, full * LANES - start :]
            for block in range(full):
                piece = strip[block * LANES : (block + 1) * LANES].T
                packed[half, pl.ds(layout.strip + block * left, left), :] = piece
            corner = pl.ds(layout.strip + full * left, left)
            packed[half, corner, :] = jnp.zeros((left, LANES), jnp.float32)
            packed[half, corner, 0:left] = strip[full * LANES :]
    spare = layout.rows - layout.used[half]
    if spare:
        packed[half, pl.ds(layout.used[half], spare), :] = jnp.zeros((spare, LANES), jnp.float32)


def dense_rows(rows, width):
    full = width // LANES
    left = width - full * LANES
    beside = LANES // left
    group = -(-rows // (8 * beside)) * 8
    return full, left, beside, group, rows * (full + 1) + group


def dense_kernel(field_ref, basis_ref, out_ref):
    blocks, rows, width = field_ref.shape
    full, left, beside, group, _ = dense_rows(rows, width)
    base = (full + 1) * rows
    for block in range(blocks):
        for part in range(full):
            out_ref[block, pl.ds(part * rows, rows), :] = field_ref[block, :, part * LANES : (part + 1) * LANES]
        out_ref[block, pl.ds(full * rows, rows), :] = basis_ref[...]
        for part in range(beside):
            some = min(group, rows - part * group)
            lanes = slice(part * left, (part + 1) * left)
            piece = field_ref[block, pl.ds(part * group, some), full * LANES : width]
            out_ref[block, pl.ds(base, some), lanes] = piece
            if some < group:
                out_ref[block, pl.ds(base + some, group - some), lanes] = jnp.zeros((group - some, left), jnp.float32)


def gram_kernel(
    layout, place_ref, dense_ref, keep_ref, send_ref, core_ref,
    field, basis, field_high, field_low, left_side, right_side, packed,
):
    blocks = dense_ref.shape[0]
    first, width = field.shape
    rank = basis.shape[1]
    rows = first // blocks
    full, left, beside, group, _ = dense_rows(rows, width)
    base = (full + 1) * rows
    for owner in range(blocks):
        own = owner * rows
        for part in range(full):
            field[pl.ds(own, rows), part * LANES : (part + 1) * LANES] = dense_ref[owner, pl.ds(part * rows, rows), :]
        basis[pl.ds(own, rows), :] = dense_ref[owner, pl.ds(full * rows, rows), :]
        for part in range(beside):
            some = min(group, rows - part * group)
            piece = dense_ref[owner, pl.ds(base, some), part * left : (part + 1) * left]
            field[pl.ds(own + part * group, some), full * LANES : width] = piece
    high, low = halves(field[...])
    field_high[...] = high
    field_low[...] = low
    basis_high, basis_low = halves(basis[...].T)
    core = dot(basis_high, high) + (dot(basis_high, low) + dot(basis_low, high))
    core_ref[...] = core
    high, low = halves(core.T)
    left_side[:, 0:rank] = high
    left_side[:, rank : 2 * rank] = low
    right_side[:, 0:rank] = high
    right_side[:, rank : 2 * rank] = high

    def field_product(rows, start, columns):
        lh, ll = field_high[pl.ds(0, rows), :], field_low[pl.ds(0, rows), :]
        rh, rl = field_high[pl.ds(start, columns), :], field_low[pl.ds(start, columns), :]
        return dot_rows(lh, rh) + (dot_rows(lh, rl) + dot_rows(ll, rh))

    def core_product(rows, start, columns):
        here, there = pl.ds(0, rows), pl.ds(start, columns)
        both = dot_rows(left_side[here, :], right_side[there, :])
        return both + dot_rows(left_side[here, 0:rank], left_side[there, rank : 2 * rank])

    pack_gram(layout, field_product, packed, 0)
    pack_gram(layout, core_product, packed, 1)
    mine = place_ref[1]
    keep_ref[...] = packed[mine]
    send_ref[...] = packed[1 - mine]


def parts_kernel(place_ref, core_ref, after_ref, *out_refs):
    owned = out_refs[0].shape[0]
    for step, out_ref in enumerate(out_refs):
        owner = lax.rem(place_ref[0] + step, len(out_refs))
        out_ref[...] = core_ref[pl.ds(pl.multiple_of(owner * owned, 8), owned), :]


def rows_kernel(place_ref, *refs):
    came, (out_ref, ordered) = refs[:-2], refs[-2:]
    count = len(came)
    for step, ref in enumerate(came):
        ordered[lax.rem(place_ref[0] + count - step, count)] = ref[...]
    for owner in range(count):
        out_ref[:, owner, :] = ordered[owner]


def unpack(layout, packed, half, out_ref, scale):
    full, left = layout.full, layout.left
    for block in range(full):
        columns = pl.ds(block * LANES, LANES)
        for row in range(block):
            there = pl.ds(row * LANES, LANES)
            tile = packed[half, pl.ds(layout.above[block] + row * LANES, LANES), :] * scale
            out_ref[there, columns] = tile
            out_ref[columns, there] = tile.T
        into, row = layout.fold[block]
        upper = packed[into, pl.ds(row + half * FOLD, FOLD), :] * scale
        lower = packed[into, pl.ds(row + 2 * FOLD, FOLD), :] * scale
        if half == 0:
            lower = pltpu.roll(lower, FOLD, 1)
        turned = jnp.concatenate([upper, upper], axis=0).T[FOLD:]
        out_ref[pl.ds(block * LANES, FOLD), columns] = upper
        out_ref[pl.ds(block * LANES + FOLD, FOLD), columns] = jnp.where(lane_below(FOLD), turned, lower)
        tile = packed[half, pl.ds(layout.strip + block * left, left), :] * scale
        out_ref[pl.ds(full * LANES, left), columns] = tile
        out_ref[columns, pl.ds(full * LANES, left)] = tile.T
    corner = packed[half, pl.ds(layout.strip + full * left, left), :] * scale
    out_ref[pl.ds(full * LANES, left), pl.ds(full * LANES, left)] = corner[:, 0:left]


def unpack_kernel(layout, scale_one, scale_two, place_ref, own_ref, other_ref, one_ref, two_ref, packed, whole):
    rows = one_ref.shape[0]
    mine = place_ref[1]
    packed[mine] = own_ref[...]
    packed[1 - mine] = other_ref[...]
    unpack(layout, packed, 0, whole, scale_one)
    one_ref[...] = whole[pl.ds(pl.multiple_of(place_ref[0] * rows, 8), rows), :]
    unpack(layout, packed, 1, two_ref, scale_two)


def exchange(parts, axes, groups=None):
    return lax.all_to_all(parts, axes, 0, 0, axis_index_groups=groups, tiled=True)


def copies(value, count):
    return jnp.broadcast_to(value[None], (count,) + value.shape)


def cost(flops, moved):
    return pl.CostEstimate(flops=flops, transcendentals=0, bytes_accessed=moved)


def both_groups(sizes):
    shape = tuple(sizes.values())
    index = np.arange(np.prod(shape)).reshape(shape)
    near, far = [], []
    for core in range(shape[3]):
        places = np.roll(index[..., core], core - 1, axis=(0, 1, 2))
        places = places.reshape(shape[0] // 2, 2, shape[1] // 2, 2, shape[2] // 2, 2)
        near += [places[a, :, b, :, d, :] for a, b, d in np.ndindex(places.shape[::2])]
        far += [places[:, a, :, b, :, d] for a, b, d in np.ndindex(2, 2, 2)]
    return [[group.reshape(-1).tolist() for group in groups] for groups in (near, far)]


def local(sizes, tensor, basis):
    gx = sizes["x"]
    slices_here, rows_here, second = tensor.shape
    first = rows_here * gx
    rank = basis.shape[1]
    axes = tuple(sizes)
    near, far = both_groups(sizes)
    near_count, far_count = len(near[0]), len(far[0])
    slices_all = slices_here * near_count * far_count // gx * sizes["c"]
    layout = Layout(first, 8 * near_count * far_count)
    dense = dense_rows(rows_here, second)[-1]
    swap = [(i, sizes["c"] - 1 - i) for i in range(sizes["c"])]
    place = jnp.stack([lax.axis_index("x"), lax.axis_index("c")]).astype(jnp.int32)
    f32, bf16 = jnp.float32, jnp.bfloat16

    blocks = pl.pallas_call(
        dense_kernel,
        out_shape=jax.ShapeDtypeStruct((slices_here, dense, LANES), f32),
        in_specs=[VMEM, VMEM],
        out_specs=VMEM,
        compiler_params=ROOM,
        name="dense_blocks",
    )(tensor, basis)
    blocks, place = lax.optimization_barrier((blocks, place))
    blocks = exchange(blocks, "x")
    half_shape = jax.ShapeDtypeStruct((layout.rows, LANES), f32)
    keep, send, core = pl.pallas_call(
        functools.partial(gram_kernel, layout),
        out_shape=(half_shape, half_shape, jax.ShapeDtypeStruct((rank, second), f32)),
        in_specs=[SMEM, VMEM],
        out_specs=(VMEM, VMEM, VMEM),
        scratch_shapes=[
            pltpu.VMEM((first, second), f32),
            pltpu.VMEM((first, rank), f32),
            pltpu.VMEM((first, second), bf16),
            pltpu.VMEM((first, second), bf16),
            pltpu.VMEM((second, 2 * rank), bf16),
            pltpu.VMEM((second, 2 * rank), bf16),
            pltpu.VMEM((2, layout.rows, LANES), f32),
        ],
        compiler_params=ROOM,
        cost_estimate=cost(5 * first * first * second, 12 * first * second),
        name="local_grams",
    )(place, blocks)

    came = lax.ppermute(send, "c", swap)
    sums = keep + came
    owned = rank // gx
    core_parts = pl.pallas_call(
        parts_kernel,
        out_shape=[jax.ShapeDtypeStruct((owned, second), f32)] * gx,
        in_specs=[SMEM, VMEM, pl.BlockSpec(memory_space=pl.ANY)],
        out_specs=[VMEM] * gx,
        compiler_params=ROOM,
        cost_estimate=cost(rank * second, 8 * rank * second),
        name="core_parts",
    )(place, core, came)
    came_core = [core_parts[0]]
    for step in range(1, gx):
        shift = [(i, (i + step) % gx) for i in range(gx)]
        came_core.append(lax.ppermute(core_parts[step], "x", shift))
    part = exchange(sums.reshape(near_count, -1, LANES), axes, near)
    part, *came_core = lax.optimization_barrier((part, *came_core))
    part = exchange(jnp.sum(part, axis=0).reshape(far_count, -1, LANES), axes, far)
    core_out = pl.pallas_call(
        rows_kernel,
        out_shape=jax.ShapeDtypeStruct((owned, gx, second), f32),
        in_specs=[SMEM] + [VMEM] * gx,
        out_specs=VMEM,
        scratch_shapes=[pltpu.VMEM((gx, owned, second), f32)],
        compiler_params=ROOM,
        cost_estimate=cost(rank * second, 8 * rank * second),
        name="core_rows",
    )(place, *came_core)
    part = exchange(copies(jnp.sum(part, axis=0), far_count), axes, far).reshape(-1, LANES)
    own = exchange(copies(part, near_count), axes, near).reshape(-1, LANES)
    other = lax.ppermute(own, "c", swap)

    gram_one, gram_two = pl.pallas_call(
        functools.partial(unpack_kernel, layout, 1.0 / (slices_all * second), 1.0 / (slices_all * rank)),
        out_shape=(
            jax.ShapeDtypeStruct((rows_here, first), f32),
            jax.ShapeDtypeStruct((second, second), f32),
        ),
        in_specs=[SMEM, VMEM, VMEM],
        out_specs=(VMEM, VMEM),
        scratch_shapes=[pltpu.VMEM((2, layout.rows, LANES), f32), pltpu.VMEM((first, first), f32)],
        compiler_params=ROOM,
        name="mirror",
    )(place, own, other)
    return gram_one, core_out, gram_two


def solution(mesh):
    gx, rest = mesh.devices.shape
    sizes = {"x": gx, "y": 8, "z": rest // 16, "c": 2}
    fine = Mesh(mesh.devices.reshape(tuple(sizes.values())), tuple(sizes))
    spread = ("y", "z", "c")
    in_specs = (P(spread, "x", None), P("x", None))
    out_specs = (P("x", None), P("x", spread, None), P())
    return jax.shard_map(
        functools.partial(local, sizes), mesh=fine, in_specs=in_specs, out_specs=out_specs, check_vma=False
    )
```

```python
import functools

import jax
import jax.numpy as jnp
import numpy as np
from jax import lax
from jax.experimental import pallas as pl
from jax.experimental.pallas import tpu as pltpu
from jax.sharding import Mesh, PartitionSpec as P

LANES = 128
FOLD = LANES // 2
VMEM = pl.BlockSpec(memory_space=pltpu.VMEM)
ANY = pl.BlockSpec(memory_space=pl.ANY)
ROOM = pltpu.CompilerParams(vmem_limit_bytes=24 << 20)


class Layout:
    def __init__(self, width, unit):
        self.width = width
        self.full = width // LANES
        self.left = width - self.full * LANES
        self.above = [0] * self.full
        row = 0
        for block in range(1, self.full):
            self.above[block] = row
            row += block * LANES
        self.strip = row
        row += self.left * (self.full + 1)
        split = -(-self.full // 2)
        self.fold = [(block // split, row + (block % split) * 3 * FOLD) for block in range(self.full)]
        self.used = [row + split * 3 * FOLD, row + (self.full - split) * 3 * FOLD]
        self.rows = -(-self.used[0] // unit) * unit


def halves(value):
    high = value.astype(jnp.bfloat16)
    low = (value - high.astype(jnp.float32)).astype(jnp.bfloat16)
    return high, low


def dot(a, b):
    return jnp.dot(a, b, preferred_element_type=jnp.float32)


def dot_rows(a, b):
    return lax.dot_general(a, b, (((1,), (1,)), ((), ())), preferred_element_type=jnp.float32)


def lane_below(rows):
    return lax.broadcasted_iota(jnp.int32, (rows, LANES), 1) < FOLD


def pack_gram(layout, product, packed, half):
    full, left, width = layout.full, layout.left, layout.width
    for start in range(0, width, 2 * LANES):
        columns = min(2 * LANES, width - start)
        last = start + columns == width
        group = product(width if last else start + columns, start, columns)
        for block in range(start // LANES, min(full, (start + columns) // LANES)):
            inside = slice(block * LANES - start, (block + 1) * LANES - start)
            above = block * LANES
            if above:
                packed[half, pl.ds(layout.above[block], above), :] = group[:above, inside]
            into, row = layout.fold[block]
            packed[into, pl.ds(row + half * FOLD, FOLD), :] = group[above : above + FOLD, inside]
            lower = group[above + FOLD : above + LANES, inside]
            corner = pl.ds(row + 2 * FOLD, FOLD)
            if half == 0:
                packed[into, corner, :] = pltpu.roll(lower, FOLD, 1)
            else:
                packed[into, corner, :] = jnp.where(lane_below(FOLD), packed[into, corner, :], lower)
        if last:
            strip = group[:, full * LANES - start :]
            for block in range(full):
                piece = strip[block * LANES : (block + 1) * LANES].T
                packed[half, pl.ds(layout.strip + block * left, left), :] = piece
            corner = pl.ds(layout.strip + full * left, left)
            packed[half, corner, :] = jnp.zeros((left, LANES), jnp.float32)
            packed[half, corner, 0:left] = strip[full * LANES :]
    spare = layout.rows - layout.used[half]
    if spare:
        packed[half, pl.ds(layout.used[half], spare), :] = jnp.zeros((spare, LANES), jnp.float32)


def dense_rows(rows, width):
    full = width // LANES
    left = width - full * LANES
    beside = LANES // left
    group = -(-rows // (8 * beside)) * 8
    return full, left, beside, group, rows * (full + 1) + group


def dense_kernel(field_ref, basis_ref, out_ref):
    blocks, rows, width = field_ref.shape
    full, left, beside, group, _ = dense_rows(rows, width)
    base = (full + 1) * rows
    for block in range(blocks):
        for part in range(full):
            out_ref[block, pl.ds(part * rows, rows), :] = field_ref[block, :, part * LANES : (part + 1) * LANES]
        out_ref[block, pl.ds(full * rows, rows), :] = basis_ref[...]
        for part in range(beside):
            some = min(group, rows - part * group)
            lanes = slice(part * left, (part + 1) * left)
            piece = field_ref[block, pl.ds(part * group, some), full * LANES : width]
            out_ref[block, pl.ds(base, some), lanes] = piece
            if some < group:
                out_ref[block, pl.ds(base + some, group - some), lanes] = jnp.zeros((group - some, left), jnp.float32)


def gram_kernel(
    layout, dense_ref, keep_ref, send_ref, core_ref,
    field, basis, field_high, field_low, left_side, right_side, packed,
):
    blocks = dense_ref.shape[0]
    first, width = field.shape
    rank = basis.shape[1]
    rows = first // blocks
    full, left, beside, group, _ = dense_rows(rows, width)
    base = (full + 1) * rows
    for owner in range(blocks):
        own = owner * rows
        for part in range(full):
            field[pl.ds(own, rows), part * LANES : (part + 1) * LANES] = dense_ref[owner, pl.ds(part * rows, rows), :]
        basis[pl.ds(own, rows), :] = dense_ref[owner, pl.ds(full * rows, rows), :]
        for part in range(beside):
            some = min(group, rows - part * group)
            piece = dense_ref[owner, pl.ds(base, some), part * left : (part + 1) * left]
            field[pl.ds(own + part * group, some), full * LANES : width] = piece
    high, low = halves(field[...])
    field_high[...] = high
    field_low[...] = low
    basis_high, basis_low = halves(basis[...].T)
    core = dot(basis_high, high) + (dot(basis_high, low) + dot(basis_low, high))
    core_ref[...] = core
    high, low = halves(core.T)
    left_side[:, 0:rank] = high
    left_side[:, rank : 2 * rank] = low
    right_side[:, 0:rank] = high
    right_side[:, rank : 2 * rank] = high

    def field_product(rows, start, columns):
        lh, ll = field_high[pl.ds(0, rows), :], field_low[pl.ds(0, rows), :]
        rh, rl = field_high[pl.ds(start, columns), :], field_low[pl.ds(start, columns), :]
        return dot_rows(lh, rh) + (dot_rows(lh, rl) + dot_rows(ll, rh))

    def core_product(rows, start, columns):
        here, there = pl.ds(0, rows), pl.ds(start, columns)
        both = dot_rows(left_side[here, :], right_side[there, :])
        return both + dot_rows(left_side[here, 0:rank], left_side[there, rank : 2 * rank])

    pack_gram(layout, field_product, packed, 0)
    pack_gram(layout, core_product, packed, 1)
    mine = lax.axis_index("c")
    keep_ref[...] = packed[mine]
    send_ref[...] = packed[1 - mine]


def parts_kernel(core_ref, after_ref, *out_refs):
    owned = out_refs[0].shape[0]
    for step, out_ref in enumerate(out_refs):
        owner = lax.rem(lax.axis_index("x") + step, len(out_refs))
        out_ref[...] = core_ref[pl.ds(pl.multiple_of(owner * owned, 8), owned), :]


def rows_kernel(*refs):
    came, (out_ref, ordered) = refs[:-2], refs[-2:]
    count = len(came)
    for step, ref in enumerate(came):
        ordered[lax.rem(lax.axis_index("x") + count - step, count)] = ref[...]
    for owner in range(count):
        out_ref[:, owner, :] = ordered[owner]


def unpack_rows(layout, packed, half, block, out_ref, scale):
    full, left = layout.full, layout.left
    last = pl.ds(full * LANES, left)
    if block == full:
        for column in range(full):
            piece = packed[half, pl.ds(layout.strip + column * left, left), :]
            out_ref[last, pl.ds(column * LANES, LANES)] = piece * scale
        corner = packed[half, pl.ds(layout.strip + full * left, left), :] * scale
        out_ref[last, last] = corner[:, 0:left]
        return
    rows = pl.ds(block * LANES, LANES)
    for column in range(full):
        columns = pl.ds(column * LANES, LANES)
        if column > block:
            out_ref[rows, columns] = packed[half, pl.ds(layout.above[column] + block * LANES, LANES), :] * scale
        elif column < block:
            tile = packed[half, pl.ds(layout.above[block] + column * LANES, LANES), :] * scale
            out_ref[rows, columns] = tile.T
        else:
            into, row = layout.fold[block]
            upper = packed[into, pl.ds(row + half * FOLD, FOLD), :] * scale
            lower = packed[into, pl.ds(row + 2 * FOLD, FOLD), :] * scale
            if half == 0:
                lower = pltpu.roll(lower, FOLD, 1)
            turned = jnp.concatenate([upper, upper], axis=0).T[FOLD:]
            out_ref[pl.ds(block * LANES, FOLD), columns] = upper
            out_ref[pl.ds(block * LANES + FOLD, FOLD), columns] = jnp.where(lane_below(FOLD), turned, lower)
    piece = packed[half, pl.ds(layout.strip + block * left, left), :] * scale
    out_ref[rows, last] = piece.T


def unpack_kernel(
    layout, scale_one, scale_two, own_ref, other_ref, one_ref, two_ref, packed, whole_one, whole_two, sent
):
    width = layout.width
    mine = lax.axis_index("c")
    packed[mine] = own_ref[...]
    packed[1 - mine] = other_ref[...]
    moves = []
    for block in range(layout.full + 1):
        unpack_rows(layout, packed, 1, block, whole_two, scale_two)
        rows = pl.ds(block * LANES, min(LANES, width - block * LANES))
        move = pltpu.make_async_copy(whole_two.at[rows, :], two_ref.at[rows, :], sent.at[block])
        move.start()
        moves.append(move)
    place = lax.axis_index("x")
    owned = one_ref.shape[0]
    for owner in range(width // owned):

        @pl.when(place == owner)
        def _():
            for block in range(owner * owned // LANES, ((owner + 1) * owned - 1) // LANES + 1):
                unpack_rows(layout, packed, 0, block, whole_one, scale_one)

    rows = pl.ds(pl.multiple_of(place * owned, 8), owned)
    move = pltpu.make_async_copy(whole_one.at[rows, :], one_ref, sent.at[layout.full + 1])
    move.start()
    moves.append(move)
    for move in moves:
        move.wait()


def exchange(parts, axes, groups=None):
    return lax.all_to_all(parts, axes, 0, 0, axis_index_groups=groups, tiled=True)


def copies(value, count):
    return jnp.broadcast_to(value[None], (count,) + value.shape)


def cost(flops, moved):
    return pl.CostEstimate(flops=flops, transcendentals=0, bytes_accessed=moved)


def both_groups(sizes):
    shape = tuple(sizes.values())
    index = np.arange(np.prod(shape)).reshape(shape)
    near = [index[:, b, d, :, 0] for b, d in np.ndindex(shape[1], shape[2])]
    near += [index[a, :, d, e, 1] for a, d, e in np.ndindex(shape[0], shape[2], shape[3])]
    far = [index[a, :, :, e, 0] for a, e in np.ndindex(shape[0], shape[3])]
    far += [index[:, b, :, :, 1] for b in range(shape[1])]
    return [[group.reshape(-1).tolist() for group in groups] for groups in (near, far)]


def local(sizes, tensor, basis):
    gx = sizes["x"]
    slices_here, rows_here, second = tensor.shape
    first = rows_here * gx
    rank = basis.shape[1]
    axes = tuple(sizes)
    near, far = both_groups(sizes)
    near_count, far_count = len(near[0]), len(far[0])
    slices_all = slices_here * near_count * far_count // gx * sizes["c"]
    layout = Layout(first, 8 * near_count * far_count)
    dense = dense_rows(rows_here, second)[-1]
    swap = [(i, sizes["c"] - 1 - i) for i in range(sizes["c"])]
    f32, bf16 = jnp.float32, jnp.bfloat16

    blocks = pl.pallas_call(
        dense_kernel,
        out_shape=jax.ShapeDtypeStruct((slices_here, dense, LANES), f32),
        in_specs=[VMEM, VMEM],
        out_specs=VMEM,
        compiler_params=ROOM,
        name="dense_blocks",
    )(tensor, basis)
    blocks = exchange(blocks, "x")
    half_shape = jax.ShapeDtypeStruct((layout.rows, LANES), f32)
    keep, send, core = pl.pallas_call(
        functools.partial(gram_kernel, layout),
        out_shape=(half_shape, half_shape, jax.ShapeDtypeStruct((rank, second), f32)),
        in_specs=[VMEM],
        out_specs=(VMEM, VMEM, VMEM),
        scratch_shapes=[
            pltpu.VMEM((first, second), f32),
            pltpu.VMEM((first, rank), f32),
            pltpu.VMEM((first, second), bf16),
            pltpu.VMEM((first, second), bf16),
            pltpu.VMEM((second, 2 * rank), bf16),
            pltpu.VMEM((second, 2 * rank), bf16),
            pltpu.VMEM((2, layout.rows, LANES), f32),
        ],
        compiler_params=ROOM,
        cost_estimate=cost(5 * first * first * second, 12 * first * second),
        name="local_grams",
    )(blocks)

    came = lax.ppermute(send, "c", swap)
    sums = keep + came
    owned = rank // gx
    core_parts = pl.pallas_call(
        parts_kernel,
        out_shape=[jax.ShapeDtypeStruct((owned, second), f32)] * gx,
        in_specs=[VMEM, ANY],
        out_specs=[VMEM] * gx,
        compiler_params=ROOM,
        cost_estimate=cost(rank * second, 8 * rank * second),
        name="core_parts",
    )(core, came)
    came_core = [core_parts[0]]
    for step in range(1, gx):
        shift = [(i, (i + step) % gx) for i in range(gx)]
        came_core.append(lax.ppermute(core_parts[step], "x", shift))
    part = exchange(sums.reshape(near_count, -1, LANES), axes, near)
    part, *came_core = lax.optimization_barrier((part, *came_core))
    part = exchange(jnp.sum(part, axis=0).reshape(far_count, -1, LANES), axes, far)
    core_out = pl.pallas_call(
        rows_kernel,
        out_shape=jax.ShapeDtypeStruct((owned, gx, second), f32),
        in_specs=[VMEM] * gx,
        out_specs=VMEM,
        scratch_shapes=[pltpu.VMEM((gx, owned, second), f32)],
        compiler_params=ROOM,
        cost_estimate=cost(rank * second, 8 * rank * second),
        name="core_rows",
    )(*came_core)
    part = exchange(copies(jnp.sum(part, axis=0), far_count), axes, far).reshape(-1, LANES)
    own = exchange(copies(part, near_count), axes, near).reshape(-1, LANES)
    other = lax.ppermute(own, "c", swap)

    gram_one, gram_two = pl.pallas_call(
        functools.partial(unpack_kernel, layout, 1.0 / (slices_all * second), 1.0 / (slices_all * rank)),
        out_shape=(
            jax.ShapeDtypeStruct((rows_here, first), f32),
            jax.ShapeDtypeStruct((second, second), f32),
        ),
        in_specs=[VMEM, VMEM],
        out_specs=(ANY, ANY),
        scratch_shapes=[
            pltpu.VMEM((2, layout.rows, LANES), f32),
            pltpu.VMEM((first, first), f32),
            pltpu.VMEM((second, second), f32),
            pltpu.SemaphoreType.DMA((layout.full + 2,)),
        ],
        compiler_params=ROOM,
        name="mirror",
    )(own, other)
    return gram_one, core_out, gram_two


def solution(mesh):
    gx, rest = mesh.devices.shape
    sizes = {"x": gx, "y": 8, "zh": rest // 32, "zl": 2, "c": 2}
    fine = Mesh(mesh.devices.reshape(tuple(sizes.values())), tuple(sizes))
    spread = ("y", "zh", "zl", "c")
    in_specs = (P(spread, "x", None), P("x", None))
    out_specs = (P("x", None), P("x", spread, None), P())
    return jax.shard_map(
        functools.partial(local, sizes), mesh=fine, in_specs=in_specs, out_specs=out_specs, check_vma=False
    )
```

```python
import functools

import jax
import jax.numpy as jnp
import numpy as np
from jax import lax
from jax.experimental import pallas as pl
from jax.experimental.pallas import tpu as pltpu
from jax.sharding import Mesh, PartitionSpec as P

LANES = 128
FOLD = LANES // 2
VMEM = pl.BlockSpec(memory_space=pltpu.VMEM)
ANY = pl.BlockSpec(memory_space=pl.ANY)
ROOM = pltpu.CompilerParams(vmem_limit_bytes=24 << 20)


class Layout:
    def __init__(self, width, unit):
        self.width = width
        self.full = width // LANES
        self.left = width - self.full * LANES
        self.above = [0] * self.full
        row = 0
        for block in range(1, self.full):
            self.above[block] = row
            row += block * LANES
        self.strip = row
        row += self.left * (self.full + 1)
        split = -(-self.full // 2)
        self.fold = [(block // split, row + (block % split) * 3 * FOLD) for block in range(self.full)]
        self.used = [row + split * 3 * FOLD, row + (self.full - split) * 3 * FOLD]
        self.rows = -(-self.used[0] // unit) * unit


def halves(value):
    high = value.astype(jnp.bfloat16)
    low = (value - high.astype(jnp.float32)).astype(jnp.bfloat16)
    return high, low


def dot(a, b):
    return jnp.dot(a, b, preferred_element_type=jnp.float32)


def dot_rows(a, b):
    return lax.dot_general(a, b, (((1,), (1,)), ((), ())), preferred_element_type=jnp.float32)


def lane_below(rows):
    return lax.broadcasted_iota(jnp.int32, (rows, LANES), 1) < FOLD


def pack_gram(layout, product, packed, half):
    full, left, width = layout.full, layout.left, layout.width
    for start in range(0, width, 2 * LANES):
        columns = min(2 * LANES, width - start)
        last = start + columns == width
        group = product(width if last else start + columns, start, columns)
        for block in range(start // LANES, min(full, (start + columns) // LANES)):
            inside = slice(block * LANES - start, (block + 1) * LANES - start)
            above = block * LANES
            if above:
                packed[half, pl.ds(layout.above[block], above), :] = group[:above, inside]
            into, row = layout.fold[block]
            packed[into, pl.ds(row + half * FOLD, FOLD), :] = group[above : above + FOLD, inside]
            lower = group[above + FOLD : above + LANES, inside]
            corner = pl.ds(row + 2 * FOLD, FOLD)
            if half == 0:
                packed[into, corner, :] = pltpu.roll(lower, FOLD, 1)
            else:
                packed[into, corner, :] = jnp.where(lane_below(FOLD), packed[into, corner, :], lower)
        if last:
            strip = group[:, full * LANES - start :]
            for block in range(full):
                piece = strip[block * LANES : (block + 1) * LANES].T
                packed[half, pl.ds(layout.strip + block * left, left), :] = piece
            corner = pl.ds(layout.strip + full * left, left)
            packed[half, corner, :] = jnp.zeros((left, LANES), jnp.float32)
            packed[half, corner, 0:left] = strip[full * LANES :]
    spare = layout.rows - layout.used[half]
    if spare:
        packed[half, pl.ds(layout.used[half], spare), :] = jnp.zeros((spare, LANES), jnp.float32)


def dense_rows(rows, width):
    full = width // LANES
    left = width - full * LANES
    beside = LANES // left
    group = -(-rows // (8 * beside)) * 8
    return full, left, beside, group, rows * (full + 1) + group


def dense_kernel(field_ref, basis_ref, out_ref):
    blocks, rows, width = field_ref.shape
    full, left, beside, group, _ = dense_rows(rows, width)
    base = (full + 1) * rows
    for block in range(blocks):
        for part in range(full):
            out_ref[block, pl.ds(part * rows, rows), :] = field_ref[block, :, part * LANES : (part + 1) * LANES]
        out_ref[block, pl.ds(full * rows, rows), :] = basis_ref[...]
        for part in range(beside):
            some = min(group, rows - part * group)
            lanes = slice(part * left, (part + 1) * left)
            piece = field_ref[block, pl.ds(part * group, some), full * LANES : width]
            out_ref[block, pl.ds(base, some), lanes] = piece
            if some < group:
                out_ref[block, pl.ds(base + some, group - some), lanes] = jnp.zeros((group - some, left), jnp.float32)


def gram_kernel(
    layout, dense_ref, keep_ref, send_ref, core_ref,
    field, basis, field_high, field_low, left_side, right_side, packed,
):
    blocks = dense_ref.shape[0]
    first, width = field.shape
    rank = basis.shape[1]
    rows = first // blocks
    full, left, beside, group, _ = dense_rows(rows, width)
    base = (full + 1) * rows
    for owner in range(blocks):
        own = owner * rows
        for part in range(full):
            field[pl.ds(own, rows), part * LANES : (part + 1) * LANES] = dense_ref[owner, pl.ds(part * rows, rows), :]
        basis[pl.ds(own, rows), :] = dense_ref[owner, pl.ds(full * rows, rows), :]
        for part in range(beside):
            some = min(group, rows - part * group)
            piece = dense_ref[owner, pl.ds(base, some), part * left : (part + 1) * left]
            field[pl.ds(own + part * group, some), full * LANES : width] = piece
    high, low = halves(field[...])
    field_high[...] = high
    field_low[...] = low
    basis_high, basis_low = halves(basis[...].T)
    core = dot(basis_high, high) + (dot(basis_high, low) + dot(basis_low, high))
    core_ref[...] = core
    high, low = halves(core.T)
    left_side[:, 0:rank] = high
    left_side[:, rank : 2 * rank] = low
    right_side[:, 0:rank] = high
    right_side[:, rank : 2 * rank] = high

    def field_product(rows, start, columns):
        lh, ll = field_high[pl.ds(0, rows), :], field_low[pl.ds(0, rows), :]
        rh, rl = field_high[pl.ds(start, columns), :], field_low[pl.ds(start, columns), :]
        return dot_rows(lh, rh) + (dot_rows(lh, rl) + dot_rows(ll, rh))

    def core_product(rows, start, columns):
        here, there = pl.ds(0, rows), pl.ds(start, columns)
        both = dot_rows(left_side[here, :], right_side[there, :])
        return both + dot_rows(left_side[here, 0:rank], left_side[there, rank : 2 * rank])

    pack_gram(layout, field_product, packed, 0)
    pack_gram(layout, core_product, packed, 1)
    mine = lax.axis_index("c")
    keep_ref[...] = packed[mine]
    send_ref[...] = packed[1 - mine]


def sum_kernel(keep_ref, came_ref, out_ref, sums, sent):
    count = sent.shape[0]
    some = sums.shape[0] // count
    moves = []
    for step in range(count):
        rows = pl.ds(step * some, some)
        sums[rows, :] = keep_ref[rows, :] + came_ref[rows, :]
        move = pltpu.make_async_copy(sums.at[rows, :], out_ref.at[rows, :], sent.at[step])
        move.start()
        moves.append(move)
    for move in moves:
        move.wait()


def parts_kernel(core_ref, after_ref, *out_refs):
    owned = out_refs[0].shape[0]
    for step, out_ref in enumerate(out_refs):
        owner = lax.rem(lax.axis_index("x") + step, len(out_refs))
        out_ref[...] = core_ref[pl.ds(pl.multiple_of(owner * owned, 8), owned), :]


def rows_kernel(*refs):
    came, (out_ref, ordered) = refs[:-2], refs[-2:]
    count = len(came)
    for step, ref in enumerate(came):
        ordered[lax.rem(lax.axis_index("x") + count - step, count)] = ref[...]
    for owner in range(count):
        out_ref[:, owner, :] = ordered[owner]


def unpack_rows(layout, packed, half, block, out_ref, scale):
    full, left = layout.full, layout.left
    last = pl.ds(full * LANES, left)
    if block == full:
        for column in range(full):
            piece = packed[half, pl.ds(layout.strip + column * left, left), :]
            out_ref[last, pl.ds(column * LANES, LANES)] = piece * scale
        corner = packed[half, pl.ds(layout.strip + full * left, left), :] * scale
        out_ref[last, last] = corner[:, 0:left]
        return
    rows = pl.ds(block * LANES, LANES)
    for column in range(full):
        columns = pl.ds(column * LANES, LANES)
        if column > block:
            out_ref[rows, columns] = packed[half, pl.ds(layout.above[column] + block * LANES, LANES), :] * scale
        elif column < block:
            tile = packed[half, pl.ds(layout.above[block] + column * LANES, LANES), :] * scale
            out_ref[rows, columns] = tile.T
        else:
            into, row = layout.fold[block]
            upper = packed[into, pl.ds(row + half * FOLD, FOLD), :] * scale
            lower = packed[into, pl.ds(row + 2 * FOLD, FOLD), :] * scale
            if half == 0:
                lower = pltpu.roll(lower, FOLD, 1)
            turned = jnp.concatenate([upper, upper], axis=0).T[FOLD:]
            out_ref[pl.ds(block * LANES, FOLD), columns] = upper
            out_ref[pl.ds(block * LANES + FOLD, FOLD), columns] = jnp.where(lane_below(FOLD), turned, lower)
    piece = packed[half, pl.ds(layout.strip + block * left, left), :] * scale
    out_ref[rows, last] = piece.T


def unpack_kernel(
    layout, orders, scale_one, scale_two, own_ref, other_ref, one_ref, two_ref, packed, came, whole_one, whole_two, sent
):
    width = layout.width
    mine = lax.axis_index("c")
    packed[mine] = own_ref[...]
    packed[1 - mine] = other_ref[...]
    for half in range(2):
        chunk = layout.rows // len(orders[half])
        if orders[half] == sorted(orders[half]):
            continue
        came[...] = packed[half]
        for place, source in enumerate(orders[half]):
            packed[half, pl.ds(place * chunk, chunk), :] = came[pl.ds(source * chunk, chunk), :]
    moves = []
    for block in range(layout.full + 1):
        unpack_rows(layout, packed, 1, block, whole_two, scale_two)
        rows = pl.ds(block * LANES, min(LANES, width - block * LANES))
        move = pltpu.make_async_copy(whole_two.at[rows, :], two_ref.at[rows, :], sent.at[block])
        move.start()
        moves.append(move)
    place = lax.axis_index("x")
    owned = one_ref.shape[0]
    for owner in range(width // owned):

        @pl.when(place == owner)
        def _():
            for block in range(owner * owned // LANES, ((owner + 1) * owned - 1) // LANES + 1):
                unpack_rows(layout, packed, 0, block, whole_one, scale_one)

    rows = pl.ds(pl.multiple_of(place * owned, 8), owned)
    move = pltpu.make_async_copy(whole_one.at[rows, :], one_ref, sent.at[layout.full + 1])
    move.start()
    moves.append(move)
    for move in moves:
        move.wait()


def exchange(parts, axes, groups=None):
    return lax.all_to_all(parts, axes, 0, 0, axis_index_groups=groups, tiled=True)


def copies(value, count):
    return jnp.broadcast_to(value[None], (count,) + value.shape)


def cost(flops, moved):
    return pl.CostEstimate(flops=flops, transcendentals=0, bytes_accessed=moved)


def both_groups(sizes):
    shape = tuple(sizes.values())
    index = np.arange(np.prod(shape)).reshape(shape)

    def short(core):
        return [index[:, b, d, :, core] for b, d in np.ndindex(shape[1], shape[2])]

    def rest(core):
        return [index[a, :, :, e, core] for a, e in np.ndindex(shape[0], shape[3])]

    near = short(0) + [index[a, :, d, e, 1] for a, d, e in np.ndindex(shape[0], shape[2], shape[3])]
    far = rest(0) + [index[:, b, :, :, 1] for b in range(shape[1])]
    groups = [near, far, short(0) + short(1), rest(0) + rest(1)]
    chunks = np.arange(np.prod(shape[:4])).reshape(shape[0], shape[3], shape[1], shape[2])
    orders = [sorted(chunks.reshape(-1).tolist()), chunks.transpose(2, 0, 3, 1).reshape(-1).tolist()]
    return [[group.reshape(-1).tolist() for group in part] for part in groups], orders


def local(sizes, tensor, basis):
    gx = sizes["x"]
    slices_here, rows_here, second = tensor.shape
    first = rows_here * gx
    rank = basis.shape[1]
    axes = tuple(sizes)
    (near, far, back_near, back_far), orders = both_groups(sizes)
    near_count, far_count = len(near[0]), len(far[0])
    slices_all = slices_here * near_count * far_count // gx * sizes["c"]
    layout = Layout(first, 8 * near_count * far_count)
    dense = dense_rows(rows_here, second)[-1]
    swap = [(i, sizes["c"] - 1 - i) for i in range(sizes["c"])]
    f32, bf16 = jnp.float32, jnp.bfloat16

    blocks = pl.pallas_call(
        dense_kernel,
        out_shape=jax.ShapeDtypeStruct((slices_here, dense, LANES), f32),
        in_specs=[VMEM, VMEM],
        out_specs=VMEM,
        compiler_params=ROOM,
        name="dense_blocks",
    )(tensor, basis)
    blocks = exchange(blocks, "x")
    half_shape = jax.ShapeDtypeStruct((layout.rows, LANES), f32)
    keep, send, core = pl.pallas_call(
        functools.partial(gram_kernel, layout),
        out_shape=(half_shape, half_shape, jax.ShapeDtypeStruct((rank, second), f32)),
        in_specs=[VMEM],
        out_specs=(VMEM, VMEM, VMEM),
        scratch_shapes=[
            pltpu.VMEM((first, second), f32),
            pltpu.VMEM((first, rank), f32),
            pltpu.VMEM((first, second), bf16),
            pltpu.VMEM((first, second), bf16),
            pltpu.VMEM((second, 2 * rank), bf16),
            pltpu.VMEM((second, 2 * rank), bf16),
            pltpu.VMEM((2, layout.rows, LANES), f32),
        ],
        compiler_params=ROOM,
        cost_estimate=cost(5 * first * first * second, 12 * first * second),
        name="local_grams",
    )(blocks)

    came = lax.ppermute(send, "c", swap)
    sums = pl.pallas_call(
        sum_kernel,
        out_shape=half_shape,
        in_specs=[VMEM, VMEM],
        out_specs=ANY,
        scratch_shapes=[pltpu.VMEM((layout.rows, LANES), f32), pltpu.SemaphoreType.DMA((8,))],
        compiler_params=ROOM,
        name="sum_of_cores",
    )(keep, came)
    owned = rank // gx
    core_parts = pl.pallas_call(
        parts_kernel,
        out_shape=[jax.ShapeDtypeStruct((owned, second), f32)] * gx,
        in_specs=[VMEM, ANY],
        out_specs=[VMEM] * gx,
        compiler_params=ROOM,
        cost_estimate=cost(rank * second, 8 * rank * second),
        name="core_parts",
    )(core, came)
    came_core = [core_parts[0]]
    for step in range(1, gx):
        shift = [(i, (i + step) % gx) for i in range(gx)]
        came_core.append(lax.ppermute(core_parts[step], "x", shift))
    part = exchange(sums.reshape(near_count, -1, LANES), axes, near)
    part, *came_core = lax.optimization_barrier((part, *came_core))
    part = exchange(jnp.sum(part, axis=0).reshape(far_count, -1, LANES), axes, far)
    core_out = pl.pallas_call(
        rows_kernel,
        out_shape=jax.ShapeDtypeStruct((owned, gx, second), f32),
        in_specs=[VMEM] * gx,
        out_specs=VMEM,
        scratch_shapes=[pltpu.VMEM((gx, owned, second), f32)],
        compiler_params=ROOM,
        cost_estimate=cost(rank * second, 8 * rank * second),
        name="core_rows",
    )(*came_core)
    part = exchange(copies(jnp.sum(part, axis=0), far_count), axes, back_far).reshape(-1, LANES)
    own = exchange(copies(part, near_count), axes, back_near).reshape(-1, LANES)
    other = lax.ppermute(own, "c", swap)

    gram_one, gram_two = pl.pallas_call(
        functools.partial(unpack_kernel, layout, orders, 1.0 / (slices_all * second), 1.0 / (slices_all * rank)),
        out_shape=(
            jax.ShapeDtypeStruct((rows_here, first), f32),
            jax.ShapeDtypeStruct((second, second), f32),
        ),
        in_specs=[VMEM, VMEM],
        out_specs=(ANY, ANY),
        scratch_shapes=[
            pltpu.VMEM((2, layout.rows, LANES), f32),
            pltpu.VMEM((layout.rows, LANES), f32),
            pltpu.VMEM((first, first), f32),
            pltpu.VMEM((second, second), f32),
            pltpu.SemaphoreType.DMA((layout.full + 2,)),
        ],
        compiler_params=ROOM,
        name="mirror",
    )(own, other)
    return gram_one, core_out, gram_two


def solution(mesh):
    gx, rest = mesh.devices.shape
    sizes = {"x": gx, "y": 8, "zh": rest // 32, "zl": 2, "c": 2}
    fine = Mesh(mesh.devices.reshape(tuple(sizes.values())), tuple(sizes))
    spread = ("y", "zh", "zl", "c")
    in_specs = (P(spread, "x", None), P("x", None))
    out_specs = (P("x", None), P("x", spread, None), P())
    return jax.shard_map(
        functools.partial(local, sizes), mesh=fine, in_specs=in_specs, out_specs=out_specs, check_vma=False
    )
```

```python
import functools

import jax
import jax.numpy as jnp
import numpy as np
from jax import lax
from jax.experimental import pallas as pl
from jax.experimental.pallas import tpu as pltpu
from jax.sharding import Mesh, PartitionSpec as P

LANES = 128
FOLD = LANES // 2
VMEM = pl.BlockSpec(memory_space=pltpu.VMEM)
ANY = pl.BlockSpec(memory_space=pl.ANY)
ROOM = pltpu.CompilerParams(vmem_limit_bytes=24 << 20)


class Layout:
    def __init__(self, width, unit):
        self.width = width
        self.full = width // LANES
        self.left = width - self.full * LANES
        self.above = [0] * self.full
        row = 0
        for block in range(1, self.full):
            self.above[block] = row
            row += block * LANES
        self.strip = row
        row += self.left * (self.full + 1)
        split = -(-self.full // 2)
        self.fold = [(block // split, row + (block % split) * 3 * FOLD) for block in range(self.full)]
        self.used = [row + split * 3 * FOLD, row + (self.full - split) * 3 * FOLD]
        self.rows = -(-self.used[0] // unit) * unit


def halves(value):
    high = value.astype(jnp.bfloat16)
    low = (value - high.astype(jnp.float32)).astype(jnp.bfloat16)
    return high, low


def dot(a, b):
    return jnp.dot(a, b, preferred_element_type=jnp.float32)


def dot_rows(a, b):
    return lax.dot_general(a, b, (((1,), (1,)), ((), ())), preferred_element_type=jnp.float32)


def lane_below(rows):
    return lax.broadcasted_iota(jnp.int32, (rows, LANES), 1) < FOLD


def pack_gram(layout, product, packed, half):
    full, left, width = layout.full, layout.left, layout.width
    for start in range(0, width, 2 * LANES):
        columns = min(2 * LANES, width - start)
        last = start + columns == width
        group = product(width if last else start + columns, start, columns)
        for block in range(start // LANES, min(full, (start + columns) // LANES)):
            inside = slice(block * LANES - start, (block + 1) * LANES - start)
            above = block * LANES
            if above:
                packed[half, pl.ds(layout.above[block], above), :] = group[:above, inside]
            into, row = layout.fold[block]
            packed[into, pl.ds(row + half * FOLD, FOLD), :] = group[above : above + FOLD, inside]
            lower = group[above + FOLD : above + LANES, inside]
            corner = pl.ds(row + 2 * FOLD, FOLD)
            if half == 0:
                packed[into, corner, :] = pltpu.roll(lower, FOLD, 1)
            else:
                packed[into, corner, :] = jnp.where(lane_below(FOLD), packed[into, corner, :], lower)
        if last:
            strip = group[:, full * LANES - start :]
            for block in range(full):
                piece = strip[block * LANES : (block + 1) * LANES].T
                packed[half, pl.ds(layout.strip + block * left, left), :] = piece
            corner = pl.ds(layout.strip + full * left, left)
            packed[half, corner, :] = jnp.zeros((left, LANES), jnp.float32)
            packed[half, corner, 0:left] = strip[full * LANES :]
    spare = layout.rows - layout.used[half]
    if spare:
        packed[half, pl.ds(layout.used[half], spare), :] = jnp.zeros((spare, LANES), jnp.float32)


def dense_rows(rows, width):
    full = width // LANES
    left = width - full * LANES
    beside = LANES // left
    group = -(-rows // (8 * beside)) * 8
    return full, left, beside, group, rows * (full + 1) + group


def dense_kernel(field_ref, basis_ref, out_ref):
    blocks, rows, width = field_ref.shape
    full, left, beside, group, _ = dense_rows(rows, width)
    base = (full + 1) * rows
    for block in range(blocks):
        for part in range(full):
            out_ref[block, pl.ds(part * rows, rows), :] = field_ref[block, :, part * LANES : (part + 1) * LANES]
        out_ref[block, pl.ds(full * rows, rows), :] = basis_ref[...]
        for part in range(beside):
            some = min(group, rows - part * group)
            lanes = slice(part * left, (part + 1) * left)
            piece = field_ref[block, pl.ds(part * group, some), full * LANES : width]
            out_ref[block, pl.ds(base, some), lanes] = piece
            if some < group:
                out_ref[block, pl.ds(base + some, group - some), lanes] = jnp.zeros((group - some, left), jnp.float32)


def gram_kernel(
    layout, dense_ref, keep_ref, send_ref, core_ref,
    field, basis, field_high, field_low, left_side, right_side, packed,
):
    blocks = dense_ref.shape[0]
    first, width = field.shape
    rank = basis.shape[1]
    rows = first // blocks
    full, left, beside, group, _ = dense_rows(rows, width)
    base = (full + 1) * rows
    for owner in range(blocks):
        own = owner * rows
        for part in range(full):
            field[pl.ds(own, rows), part * LANES : (part + 1) * LANES] = dense_ref[owner, pl.ds(part * rows, rows), :]
        basis[pl.ds(own, rows), :] = dense_ref[owner, pl.ds(full * rows, rows), :]
        for part in range(beside):
            some = min(group, rows - part * group)
            piece = dense_ref[owner, pl.ds(base, some), part * left : (part + 1) * left]
            field[pl.ds(own + part * group, some), full * LANES : width] = piece
    high, low = halves(field[...])
    field_high[...] = high
    field_low[...] = low
    basis_high, basis_low = halves(basis[...].T)
    core = dot(basis_high, high) + (dot(basis_high, low) + dot(basis_low, high))
    core_ref[...] = core
    high, low = halves(core.T)
    left_side[:, 0:rank] = high
    left_side[:, rank : 2 * rank] = low
    right_side[:, 0:rank] = high
    right_side[:, rank : 2 * rank] = high

    def field_product(rows, start, columns):
        lh, ll = field_high[pl.ds(0, rows), :], field_low[pl.ds(0, rows), :]
        rh, rl = field_high[pl.ds(start, columns), :], field_low[pl.ds(start, columns), :]
        return dot_rows(lh, rh) + (dot_rows(lh, rl) + dot_rows(ll, rh))

    def core_product(rows, start, columns):
        here, there = pl.ds(0, rows), pl.ds(start, columns)
        both = dot_rows(left_side[here, :], right_side[there, :])
        return both + dot_rows(left_side[here, 0:rank], left_side[there, rank : 2 * rank])

    pack_gram(layout, field_product, packed, 0)
    pack_gram(layout, core_product, packed, 1)
    mine = lax.axis_index("c")
    keep_ref[...] = packed[mine]
    send_ref[...] = packed[1 - mine]


def sum_kernel(keep_ref, came_ref, out_ref, sums, sent):
    count = sent.shape[0]
    some = sums.shape[0] // count
    moves = []
    for step in range(count):
        rows = pl.ds(step * some, some)
        sums[rows, :] = keep_ref[rows, :] + came_ref[rows, :]
        move = pltpu.make_async_copy(sums.at[rows, :], out_ref.at[rows, :], sent.at[step])
        move.start()
        moves.append(move)
    for move in moves:
        move.wait()


def parts_kernel(steps, owners, core_ref, after_ref, *out_refs):
    owned = out_refs[0].shape[0]
    for step, out_ref in zip(steps, out_refs):
        owner = lax.rem(lax.axis_index("x") + step, owners)
        out_ref[...] = core_ref[pl.ds(pl.multiple_of(owner * owned, 8), owned), :]


def rows_kernel(*refs):
    came, (out_ref, ordered) = refs[:-2], refs[-2:]
    count = len(came)
    for step, ref in enumerate(came):
        ordered[lax.rem(lax.axis_index("x") + count - step, count)] = ref[...]
    for owner in range(count):
        out_ref[:, owner, :] = ordered[owner]


def unpack_rows(layout, packed, half, block, out_ref, scale):
    full, left = layout.full, layout.left
    last = pl.ds(full * LANES, left)
    if block == full:
        for column in range(full):
            piece = packed[half, pl.ds(layout.strip + column * left, left), :]
            out_ref[last, pl.ds(column * LANES, LANES)] = piece * scale
        corner = packed[half, pl.ds(layout.strip + full * left, left), :] * scale
        out_ref[last, last] = corner[:, 0:left]
        return
    rows = pl.ds(block * LANES, LANES)
    for column in range(full):
        columns = pl.ds(column * LANES, LANES)
        if column > block:
            out_ref[rows, columns] = packed[half, pl.ds(layout.above[column] + block * LANES, LANES), :] * scale
        elif column < block:
            tile = packed[half, pl.ds(layout.above[block] + column * LANES, LANES), :] * scale
            out_ref[rows, columns] = tile.T
        else:
            into, row = layout.fold[block]
            upper = packed[into, pl.ds(row + half * FOLD, FOLD), :] * scale
            lower = packed[into, pl.ds(row + 2 * FOLD, FOLD), :] * scale
            if half == 0:
                lower = pltpu.roll(lower, FOLD, 1)
            turned = jnp.concatenate([upper, upper], axis=0).T[FOLD:]
            out_ref[pl.ds(block * LANES, FOLD), columns] = upper
            out_ref[pl.ds(block * LANES + FOLD, FOLD), columns] = jnp.where(lane_below(FOLD), turned, lower)
    piece = packed[half, pl.ds(layout.strip + block * left, left), :] * scale
    out_ref[rows, last] = piece.T


def unpack_kernel(
    layout, orders, scale_one, scale_two, own_ref, other_ref, one_ref, two_ref, packed, came, whole_one, whole_two, sent
):
    width = layout.width
    mine = lax.axis_index("c")
    packed[mine] = own_ref[...]
    packed[1 - mine] = other_ref[...]
    for half in range(2):
        chunk = layout.rows // len(orders[half])
        if orders[half] == sorted(orders[half]):
            continue
        came[...] = packed[half]
        for place, source in enumerate(orders[half]):
            packed[half, pl.ds(place * chunk, chunk), :] = came[pl.ds(source * chunk, chunk), :]
    moves = []
    for block in range(layout.full + 1):
        unpack_rows(layout, packed, 1, block, whole_two, scale_two)
        rows = pl.ds(block * LANES, min(LANES, width - block * LANES))
        move = pltpu.make_async_copy(whole_two.at[rows, :], two_ref.at[rows, :], sent.at[block])
        move.start()
        moves.append(move)
    place = lax.axis_index("x")
    owned = one_ref.shape[0]
    for owner in range(width // owned):

        @pl.when(place == owner)
        def _():
            for block in range(owner * owned // LANES, ((owner + 1) * owned - 1) // LANES + 1):
                unpack_rows(layout, packed, 0, block, whole_one, scale_one)

    rows = pl.ds(pl.multiple_of(place * owned, 8), owned)
    move = pltpu.make_async_copy(whole_one.at[rows, :], one_ref, sent.at[layout.full + 1])
    move.start()
    moves.append(move)
    for move in moves:
        move.wait()


def exchange(parts, axes, groups=None):
    return lax.all_to_all(parts, axes, 0, 0, axis_index_groups=groups, tiled=True)


def copies(value, count):
    return jnp.broadcast_to(value[None], (count,) + value.shape)


def cost(flops, moved):
    return pl.CostEstimate(flops=flops, transcendentals=0, bytes_accessed=moved)


def both_groups(sizes):
    shape = tuple(sizes.values())
    index = np.arange(np.prod(shape)).reshape(shape)

    def short(core):
        return [index[:, b, d, :, core] for b, d in np.ndindex(shape[1], shape[2])]

    def rest(core):
        return [index[a, :, :, e, core] for a, e in np.ndindex(shape[0], shape[3])]

    near = short(0) + [index[a, :, d, e, 1] for a, d, e in np.ndindex(shape[0], shape[2], shape[3])]
    far = rest(0) + [index[:, b, :, :, 1] for b in range(shape[1])]
    groups = [near, far, short(0) + short(1), rest(0) + rest(1)]
    chunks = np.arange(np.prod(shape[:4])).reshape(shape[0], shape[3], shape[1], shape[2])
    orders = [sorted(chunks.reshape(-1).tolist()), chunks.transpose(2, 0, 3, 1).reshape(-1).tolist()]
    return [[group.reshape(-1).tolist() for group in part] for part in groups], orders


def local(sizes, tensor, basis):
    gx = sizes["x"]
    slices_here, rows_here, second = tensor.shape
    first = rows_here * gx
    rank = basis.shape[1]
    axes = tuple(sizes)
    (near, far, back_near, back_far), orders = both_groups(sizes)
    near_count, far_count = len(near[0]), len(far[0])
    slices_all = slices_here * near_count * far_count // gx * sizes["c"]
    layout = Layout(first, 8 * near_count * far_count)
    dense = dense_rows(rows_here, second)[-1]
    swap = [(i, sizes["c"] - 1 - i) for i in range(sizes["c"])]
    f32, bf16 = jnp.float32, jnp.bfloat16

    blocks = pl.pallas_call(
        dense_kernel,
        out_shape=jax.ShapeDtypeStruct((slices_here, dense, LANES), f32),
        in_specs=[VMEM, VMEM],
        out_specs=VMEM,
        compiler_params=ROOM,
        name="dense_blocks",
    )(tensor, basis)
    blocks = exchange(blocks, "x")
    half_shape = jax.ShapeDtypeStruct((layout.rows, LANES), f32)
    keep, send, core = pl.pallas_call(
        functools.partial(gram_kernel, layout),
        out_shape=(half_shape, half_shape, jax.ShapeDtypeStruct((rank, second), f32)),
        in_specs=[VMEM],
        out_specs=(VMEM, VMEM, VMEM),
        scratch_shapes=[
            pltpu.VMEM((first, second), f32),
            pltpu.VMEM((first, rank), f32),
            pltpu.VMEM((first, second), bf16),
            pltpu.VMEM((first, second), bf16),
            pltpu.VMEM((second, 2 * rank), bf16),
            pltpu.VMEM((second, 2 * rank), bf16),
            pltpu.VMEM((2, layout.rows, LANES), f32),
        ],
        compiler_params=ROOM,
        cost_estimate=cost(5 * first * first * second, 12 * first * second),
        name="local_grams",
    )(blocks)

    came = lax.ppermute(send, "c", swap)
    sums = pl.pallas_call(
        sum_kernel,
        out_shape=half_shape,
        in_specs=[VMEM, VMEM],
        out_specs=ANY,
        scratch_shapes=[pltpu.VMEM((layout.rows, LANES), f32), pltpu.SemaphoreType.DMA((8,))],
        compiler_params=ROOM,
        name="sum_of_cores",
    )(keep, came)
    owned = rank // gx
    def parts(steps, after):
        return pl.pallas_call(
            functools.partial(parts_kernel, steps, gx),
            out_shape=[jax.ShapeDtypeStruct((owned, second), f32)] * len(steps),
            in_specs=[VMEM, ANY],
            out_specs=[VMEM] * len(steps),
            compiler_params=ROOM,
            cost_estimate=cost(rank * second, 8 * rank * second),
            name="core_parts",
        )(core, after)

    def along_x(block, step):
        return lax.ppermute(block, "x", [(i, (i + step) % gx) for i in range(gx)])

    early = [step for step in range(gx) if 2 * step != gx]
    late = gx // 2
    blocks_early = parts(early, came)
    came_core = [along_x(block, step) if step else block for step, block in zip(early, blocks_early)]
    part = exchange(sums.reshape(near_count, -1, LANES), axes, near)
    part, *came_core = lax.optimization_barrier((part, *came_core))
    part = jnp.sum(part, axis=0)
    came_late = along_x(parts([late], part)[0], late)
    part = exchange(part.reshape(far_count, -1, LANES), axes, far)
    part, came_late = lax.optimization_barrier((part, came_late))
    came_core = came_core[:late] + [came_late] + came_core[late:]
    core_out = pl.pallas_call(
        rows_kernel,
        out_shape=jax.ShapeDtypeStruct((owned, gx, second), f32),
        in_specs=[VMEM] * gx,
        out_specs=VMEM,
        scratch_shapes=[pltpu.VMEM((gx, owned, second), f32)],
        compiler_params=ROOM,
        cost_estimate=cost(rank * second, 8 * rank * second),
        name="core_rows",
    )(*came_core)
    part = exchange(copies(jnp.sum(part, axis=0), far_count), axes, back_far).reshape(-1, LANES)
    own = exchange(copies(part, near_count), axes, back_near).reshape(-1, LANES)
    other = lax.ppermute(own, "c", swap)

    gram_one, gram_two = pl.pallas_call(
        functools.partial(unpack_kernel, layout, orders, 1.0 / (slices_all * second), 1.0 / (slices_all * rank)),
        out_shape=(
            jax.ShapeDtypeStruct((rows_here, first), f32),
            jax.ShapeDtypeStruct((second, second), f32),
        ),
        in_specs=[VMEM, VMEM],
        out_specs=(ANY, ANY),
        scratch_shapes=[
            pltpu.VMEM((2, layout.rows, LANES), f32),
            pltpu.VMEM((layout.rows, LANES), f32),
            pltpu.VMEM((first, first), f32),
            pltpu.VMEM((second, second), f32),
            pltpu.SemaphoreType.DMA((layout.full + 2,)),
        ],
        compiler_params=ROOM,
        name="mirror",
    )(own, other)
    return gram_one, core_out, gram_two


def solution(mesh):
    gx, rest = mesh.devices.shape
    sizes = {"x": gx, "y": 8, "zh": rest // 32, "zl": 2, "c": 2}
    fine = Mesh(mesh.devices.reshape(tuple(sizes.values())), tuple(sizes))
    spread = ("y", "zh", "zl", "c")
    in_specs = (P(spread, "x", None), P("x", None))
    out_specs = (P("x", None), P("x", spread, None), P())
    return jax.shard_map(
        functools.partial(local, sizes), mesh=fine, in_specs=in_specs, out_specs=out_specs, check_vma=False
    )
```

```python
import functools

import jax
import jax.numpy as jnp
import numpy as np
from jax import lax
from jax.experimental import pallas as pl
from jax.experimental.pallas import tpu as pltpu
from jax.sharding import Mesh, PartitionSpec as P

LANES = 128
FOLD = LANES // 2
VMEM = pl.BlockSpec(memory_space=pltpu.VMEM)
ANY = pl.BlockSpec(memory_space=pl.ANY)
ROOM = pltpu.CompilerParams(vmem_limit_bytes=24 << 20)


class Layout:
    def __init__(self, width, unit):
        self.width = width
        self.full = width // LANES
        self.left = width - self.full * LANES
        self.above = [0] * self.full
        row = 0
        for block in range(1, self.full):
            self.above[block] = row
            row += block * LANES
        self.strip = row
        row += self.left * (self.full + 1)
        split = -(-self.full // 2)
        self.fold = [(block // split, row + (block % split) * 3 * FOLD) for block in range(self.full)]
        self.used = [row + split * 3 * FOLD, row + (self.full - split) * 3 * FOLD]
        self.rows = -(-self.used[0] // unit) * unit


def halves(value):
    high = value.astype(jnp.bfloat16)
    low = (value - high.astype(jnp.float32)).astype(jnp.bfloat16)
    return high, low


def dot(a, b):
    return jnp.dot(a, b, preferred_element_type=jnp.float32)


def dot_rows(a, b):
    return lax.dot_general(a, b, (((1,), (1,)), ((), ())), preferred_element_type=jnp.float32)


def lane_below(rows):
    return lax.broadcasted_iota(jnp.int32, (rows, LANES), 1) < FOLD


def pack_gram(layout, product, packed, half):
    full, left, width = layout.full, layout.left, layout.width
    for start in range(0, width, 2 * LANES):
        columns = min(2 * LANES, width - start)
        last = start + columns == width
        group = product(width if last else start + columns, start, columns)
        for block in range(start // LANES, min(full, (start + columns) // LANES)):
            inside = slice(block * LANES - start, (block + 1) * LANES - start)
            above = block * LANES
            if above:
                packed[half, pl.ds(layout.above[block], above), :] = group[:above, inside]
            into, row = layout.fold[block]
            packed[into, pl.ds(row + half * FOLD, FOLD), :] = group[above : above + FOLD, inside]
            lower = group[above + FOLD : above + LANES, inside]
            corner = pl.ds(row + 2 * FOLD, FOLD)
            if half == 0:
                packed[into, corner, :] = pltpu.roll(lower, FOLD, 1)
            else:
                packed[into, corner, :] = jnp.where(lane_below(FOLD), packed[into, corner, :], lower)
        if last:
            strip = group[:, full * LANES - start :]
            for block in range(full):
                piece = strip[block * LANES : (block + 1) * LANES].T
                packed[half, pl.ds(layout.strip + block * left, left), :] = piece
            corner = pl.ds(layout.strip + full * left, left)
            packed[half, corner, :] = jnp.zeros((left, LANES), jnp.float32)
            packed[half, corner, 0:left] = strip[full * LANES :]
    spare = layout.rows - layout.used[half]
    if spare:
        packed[half, pl.ds(layout.used[half], spare), :] = jnp.zeros((spare, LANES), jnp.float32)


def dense_rows(rows, width):
    full = width // LANES
    left = width - full * LANES
    beside = LANES // left
    group = -(-rows // (8 * beside)) * 8
    return full, left, beside, group, rows * (full + 1) + group


def dense_kernel(field_ref, basis_ref, out_ref):
    blocks, rows, width = field_ref.shape
    full, left, beside, group, _ = dense_rows(rows, width)
    base = (full + 1) * rows
    for block in range(blocks):
        for part in range(full):
            out_ref[block, pl.ds(part * rows, rows), :] = field_ref[block, :, part * LANES : (part + 1) * LANES]
        out_ref[block, pl.ds(full * rows, rows), :] = basis_ref[...]
        for part in range(beside):
            some = min(group, rows - part * group)
            lanes = slice(part * left, (part + 1) * left)
            piece = field_ref[block, pl.ds(part * group, some), full * LANES : width]
            out_ref[block, pl.ds(base, some), lanes] = piece
            if some < group:
                out_ref[block, pl.ds(base + some, group - some), lanes] = jnp.zeros((group - some, left), jnp.float32)


def gram_kernel(
    layout, dense_ref, keep_ref, send_ref, core_ref,
    field, basis, field_high, field_low, left_side, right_side, packed,
):
    blocks = dense_ref.shape[0]
    first, width = field.shape
    rank = basis.shape[1]
    rows = first // blocks
    full, left, beside, group, _ = dense_rows(rows, width)
    base = (full + 1) * rows
    for owner in range(blocks):
        own = owner * rows
        for part in range(full):
            field[pl.ds(own, rows), part * LANES : (part + 1) * LANES] = dense_ref[owner, pl.ds(part * rows, rows), :]
        basis[pl.ds(own, rows), :] = dense_ref[owner, pl.ds(full * rows, rows), :]
        for part in range(beside):
            some = min(group, rows - part * group)
            piece = dense_ref[owner, pl.ds(base, some), part * left : (part + 1) * left]
            field[pl.ds(own + part * group, some), full * LANES : width] = piece
    high, low = halves(field[...])
    field_high[...] = high
    field_low[...] = low
    basis_high, basis_low = halves(basis[...].T)
    core = dot(basis_high, high) + (dot(basis_high, low) + dot(basis_low, high))
    core_ref[...] = core
    high, low = halves(core.T)
    left_side[:, 0:rank] = high
    left_side[:, rank : 2 * rank] = low
    right_side[:, 0:rank] = high
    right_side[:, rank : 2 * rank] = high

    def field_product(rows, start, columns):
        lh, ll = field_high[pl.ds(0, rows), :], field_low[pl.ds(0, rows), :]
        rh, rl = field_high[pl.ds(start, columns), :], field_low[pl.ds(start, columns), :]
        return dot_rows(lh, rh) + (dot_rows(lh, rl) + dot_rows(ll, rh))

    def core_product(rows, start, columns):
        here, there = pl.ds(0, rows), pl.ds(start, columns)
        both = dot_rows(left_side[here, :], right_side[there, :])
        return both + dot_rows(left_side[here, 0:rank], left_side[there, rank : 2 * rank])

    pack_gram(layout, field_product, packed, 0)
    pack_gram(layout, core_product, packed, 1)
    mine = lax.axis_index("c")
    keep_ref[...] = packed[mine]
    send_ref[...] = packed[1 - mine]


def sum_kernel(keep_ref, came_ref, out_ref, sums, sent):
    count = sent.shape[0]
    some = sums.shape[0] // count
    moves = []
    for step in range(count):
        rows = pl.ds(step * some, some)
        sums[rows, :] = keep_ref[rows, :] + came_ref[rows, :]
        move = pltpu.make_async_copy(sums.at[rows, :], out_ref.at[rows, :], sent.at[step])
        move.start()
        moves.append(move)
    for move in moves:
        move.wait()


def parts_kernel(core_ref, after_ref, *out_refs):
    owned = out_refs[0].shape[0]
    for step, out_ref in enumerate(out_refs):
        owner = lax.rem(lax.axis_index("x") + step, len(out_refs))
        out_ref[...] = core_ref[pl.ds(pl.multiple_of(owner * owned, 8), owned), :]


def rows_kernel(*refs):
    came, (out_ref, ordered) = refs[:-2], refs[-2:]
    count = len(came)
    for step, ref in enumerate(came):
        ordered[lax.rem(lax.axis_index("x") + count - step, count)] = ref[...]
    for owner in range(count):
        out_ref[:, owner, :] = ordered[owner]


def unpack_rows(layout, packed, half, block, out_ref, scale):
    full, left = layout.full, layout.left
    last = pl.ds(full * LANES, left)
    if block == full:
        for column in range(full):
            piece = packed[half, pl.ds(layout.strip + column * left, left), :]
            out_ref[last, pl.ds(column * LANES, LANES)] = piece * scale
        corner = packed[half, pl.ds(layout.strip + full * left, left), :] * scale
        out_ref[last, last] = corner[:, 0:left]
        return
    rows = pl.ds(block * LANES, LANES)
    for column in range(full):
        columns = pl.ds(column * LANES, LANES)
        if column > block:
            out_ref[rows, columns] = packed[half, pl.ds(layout.above[column] + block * LANES, LANES), :] * scale
        elif column < block:
            tile = packed[half, pl.ds(layout.above[block] + column * LANES, LANES), :] * scale
            out_ref[rows, columns] = tile.T
        else:
            into, row = layout.fold[block]
            upper = packed[into, pl.ds(row + half * FOLD, FOLD), :] * scale
            lower = packed[into, pl.ds(row + 2 * FOLD, FOLD), :] * scale
            if half == 0:
                lower = pltpu.roll(lower, FOLD, 1)
            turned = jnp.concatenate([upper, upper], axis=0).T[FOLD:]
            out_ref[pl.ds(block * LANES, FOLD), columns] = upper
            out_ref[pl.ds(block * LANES + FOLD, FOLD), columns] = jnp.where(lane_below(FOLD), turned, lower)
    piece = packed[half, pl.ds(layout.strip + block * left, left), :] * scale
    out_ref[rows, last] = piece.T


def unpack_kernel(
    layout, orders, scale_one, scale_two, own_ref, other_ref, one_ref, two_ref, packed, came, whole_one, whole_two, sent
):
    width = layout.width
    mine = lax.axis_index("c")
    packed[mine] = own_ref[...]
    packed[1 - mine] = other_ref[...]
    for half in range(2):
        chunk = layout.rows // len(orders[half])
        if orders[half] == sorted(orders[half]):
            continue
        came[...] = packed[half]
        for place, source in enumerate(orders[half]):
            packed[half, pl.ds(place * chunk, chunk), :] = came[pl.ds(source * chunk, chunk), :]
    moves = []
    for block in range(layout.full + 1):
        unpack_rows(layout, packed, 1, block, whole_two, scale_two)
        rows = pl.ds(block * LANES, min(LANES, width - block * LANES))
        move = pltpu.make_async_copy(whole_two.at[rows, :], two_ref.at[rows, :], sent.at[block])
        move.start()
        moves.append(move)
    place = lax.axis_index("x")
    owned = one_ref.shape[0]
    for owner in range(width // owned):

        @pl.when(place == owner)
        def _():
            for block in range(owner * owned // LANES, ((owner + 1) * owned - 1) // LANES + 1):
                unpack_rows(layout, packed, 0, block, whole_one, scale_one)

    rows = pl.ds(pl.multiple_of(place * owned, 8), owned)
    move = pltpu.make_async_copy(whole_one.at[rows, :], one_ref, sent.at[layout.full + 1])
    move.start()
    moves.append(move)
    for move in moves:
        move.wait()


def exchange(parts, axes, groups=None):
    return lax.all_to_all(parts, axes, 0, 0, axis_index_groups=groups, tiled=True)


def copies(value, count):
    return jnp.broadcast_to(value[None], (count,) + value.shape)


def cost(flops, moved):
    return pl.CostEstimate(flops=flops, transcendentals=0, bytes_accessed=moved)


def both_groups(sizes):
    shape = tuple(sizes.values())
    index = np.arange(np.prod(shape)).reshape(shape)

    def short(core):
        return [index[:, b, d, :, core] for b, d in np.ndindex(shape[1], shape[2])]

    def rest(core):
        return [index[a, :, :, e, core] for a, e in np.ndindex(shape[0], shape[3])]

    near = [index[a, b, :, :, 0] for a, b in np.ndindex(shape[0], shape[1])]
    near += [index[a, :, d, e, 1] for a, d, e in np.ndindex(shape[0], shape[2], shape[3])]
    far = [index[:, :, d, e, 0] for d, e in np.ndindex(shape[2], shape[3])]
    far += [index[:, b, :, :, 1] for b in range(shape[1])]
    groups = [near, far, short(0) + short(1), rest(0) + rest(1)]
    chunks = np.arange(np.prod(shape[:4])).reshape(shape[0], shape[3], shape[1], shape[2])
    orders = [chunks.transpose(order).reshape(-1).tolist() for order in ((3, 1, 0, 2), (2, 0, 3, 1))]
    return [[group.reshape(-1).tolist() for group in part] for part in groups], orders


def local(sizes, tensor, basis):
    gx = sizes["x"]
    slices_here, rows_here, second = tensor.shape
    first = rows_here * gx
    rank = basis.shape[1]
    axes = tuple(sizes)
    (near, far, back_near, back_far), orders = both_groups(sizes)
    near_count, far_count = len(near[0]), len(far[0])
    slices_all = slices_here * near_count * far_count // gx * sizes["c"]
    layout = Layout(first, 8 * near_count * far_count)
    dense = dense_rows(rows_here, second)[-1]
    swap = [(i, sizes["c"] - 1 - i) for i in range(sizes["c"])]
    f32, bf16 = jnp.float32, jnp.bfloat16

    blocks = pl.pallas_call(
        dense_kernel,
        out_shape=jax.ShapeDtypeStruct((slices_here, dense, LANES), f32),
        in_specs=[VMEM, VMEM],
        out_specs=VMEM,
        compiler_params=ROOM,
        name="dense_blocks",
    )(tensor, basis)
    blocks = exchange(blocks, "x")
    half_shape = jax.ShapeDtypeStruct((layout.rows, LANES), f32)
    keep, send, core = pl.pallas_call(
        functools.partial(gram_kernel, layout),
        out_shape=(half_shape, half_shape, jax.ShapeDtypeStruct((rank, second), f32)),
        in_specs=[VMEM],
        out_specs=(VMEM, VMEM, VMEM),
        scratch_shapes=[
            pltpu.VMEM((first, second), f32),
            pltpu.VMEM((first, rank), f32),
            pltpu.VMEM((first, second), bf16),
            pltpu.VMEM((first, second), bf16),
            pltpu.VMEM((second, 2 * rank), bf16),
            pltpu.VMEM((second, 2 * rank), bf16),
            pltpu.VMEM((2, layout.rows, LANES), f32),
        ],
        compiler_params=ROOM,
        cost_estimate=cost(5 * first * first * second, 12 * first * second),
        name="local_grams",
    )(blocks)

    came = lax.ppermute(send, "c", swap)
    sums = pl.pallas_call(
        sum_kernel,
        out_shape=half_shape,
        in_specs=[VMEM, VMEM],
        out_specs=ANY,
        scratch_shapes=[pltpu.VMEM((layout.rows, LANES), f32), pltpu.SemaphoreType.DMA((8,))],
        compiler_params=ROOM,
        name="sum_of_cores",
    )(keep, came)
    owned = rank // gx
    core_parts = pl.pallas_call(
        parts_kernel,
        out_shape=[jax.ShapeDtypeStruct((owned, second), f32)] * gx,
        in_specs=[VMEM, ANY],
        out_specs=[VMEM] * gx,
        compiler_params=ROOM,
        cost_estimate=cost(rank * second, 8 * rank * second),
        name="core_parts",
    )(core, came)
    came_core = [core_parts[0]]
    for step in range(1, gx):
        shift = [(i, (i + step) % gx) for i in range(gx)]
        came_core.append(lax.ppermute(core_parts[step], "x", shift))
    part = exchange(sums.reshape(near_count, -1, LANES), axes, near)
    part, *came_core = lax.optimization_barrier((part, *came_core))
    part = exchange(jnp.sum(part, axis=0).reshape(far_count, -1, LANES), axes, far)
    core_out = pl.pallas_call(
        rows_kernel,
        out_shape=jax.ShapeDtypeStruct((owned, gx, second), f32),
        in_specs=[VMEM] * gx,
        out_specs=VMEM,
        scratch_shapes=[pltpu.VMEM((gx, owned, second), f32)],
        compiler_params=ROOM,
        cost_estimate=cost(rank * second, 8 * rank * second),
        name="core_rows",
    )(*came_core)
    part = exchange(copies(jnp.sum(part, axis=0), far_count), axes, back_far).reshape(-1, LANES)
    own = exchange(copies(part, near_count), axes, back_near).reshape(-1, LANES)
    other = lax.ppermute(own, "c", swap)

    gram_one, gram_two = pl.pallas_call(
        functools.partial(unpack_kernel, layout, orders, 1.0 / (slices_all * second), 1.0 / (slices_all * rank)),
        out_shape=(
            jax.ShapeDtypeStruct((rows_here, first), f32),
            jax.ShapeDtypeStruct((second, second), f32),
        ),
        in_specs=[VMEM, VMEM],
        out_specs=(ANY, ANY),
        scratch_shapes=[
            pltpu.VMEM((2, layout.rows, LANES), f32),
            pltpu.VMEM((layout.rows, LANES), f32),
            pltpu.VMEM((first, first), f32),
            pltpu.VMEM((second, second), f32),
            pltpu.SemaphoreType.DMA((layout.full + 2,)),
        ],
        compiler_params=ROOM,
        name="mirror",
    )(own, other)
    return gram_one, core_out, gram_two


def solution(mesh):
    gx, rest = mesh.devices.shape
    sizes = {"x": gx, "y": 8, "zh": rest // 32, "zl": 2, "c": 2}
    fine = Mesh(mesh.devices.reshape(tuple(sizes.values())), tuple(sizes))
    spread = ("y", "zh", "zl", "c")
    in_specs = (P(spread, "x", None), P("x", None))
    out_specs = (P("x", None), P("x", spread, None), P())
    return jax.shard_map(
        functools.partial(local, sizes), mesh=fine, in_specs=in_specs, out_specs=out_specs, check_vma=False
    )
```

```python
import functools

import jax
import jax.numpy as jnp
import numpy as np
from jax import lax
from jax.experimental import pallas as pl
from jax.experimental.pallas import tpu as pltpu
from jax.sharding import Mesh, PartitionSpec as P

LANES = 128
FOLD = LANES // 2
VMEM = pl.BlockSpec(memory_space=pltpu.VMEM)
ANY = pl.BlockSpec(memory_space=pl.ANY)
ROOM = pltpu.CompilerParams(vmem_limit_bytes=24 << 20)


class Layout:
    def __init__(self, width, unit):
        self.width = width
        self.full = width // LANES
        self.left = width - self.full * LANES
        self.above = [0] * self.full
        row = 0
        for block in range(1, self.full):
            self.above[block] = row
            row += block * LANES
        self.strip = row
        row += self.left * (self.full + 1)
        split = -(-self.full // 2)
        self.fold = [(block // split, row + (block % split) * 3 * FOLD) for block in range(self.full)]
        self.used = [row + split * 3 * FOLD, row + (self.full - split) * 3 * FOLD]
        self.rows = -(-self.used[0] // unit) * unit


def halves(value):
    high = value.astype(jnp.bfloat16)
    low = (value - high.astype(jnp.float32)).astype(jnp.bfloat16)
    return high, low


def dot(a, b):
    return jnp.dot(a, b, preferred_element_type=jnp.float32)


def dot_rows(a, b):
    return lax.dot_general(a, b, (((1,), (1,)), ((), ())), preferred_element_type=jnp.float32)


def lane_below(rows):
    return lax.broadcasted_iota(jnp.int32, (rows, LANES), 1) < FOLD


def pack_gram(layout, product, packed, half):
    full, left, width = layout.full, layout.left, layout.width
    for start in range(0, width, 2 * LANES):
        columns = min(2 * LANES, width - start)
        last = start + columns == width
        group = product(width if last else start + columns, start, columns)
        for block in range(start // LANES, min(full, (start + columns) // LANES)):
            inside = slice(block * LANES - start, (block + 1) * LANES - start)
            above = block * LANES
            if above:
                packed[half, pl.ds(layout.above[block], above), :] = group[:above, inside]
            into, row = layout.fold[block]
            packed[into, pl.ds(row + half * FOLD, FOLD), :] = group[above : above + FOLD, inside]
            lower = group[above + FOLD : above + LANES, inside]
            corner = pl.ds(row + 2 * FOLD, FOLD)
            if half == 0:
                packed[into, corner, :] = pltpu.roll(lower, FOLD, 1)
            else:
                packed[into, corner, :] = jnp.where(lane_below(FOLD), packed[into, corner, :], lower)
        if last:
            strip = group[:, full * LANES - start :]
            for block in range(full):
                piece = strip[block * LANES : (block + 1) * LANES].T
                packed[half, pl.ds(layout.strip + block * left, left), :] = piece
            corner = pl.ds(layout.strip + full * left, left)
            packed[half, corner, :] = jnp.zeros((left, LANES), jnp.float32)
            packed[half, corner, 0:left] = strip[full * LANES :]
    spare = layout.rows - layout.used[half]
    if spare:
        packed[half, pl.ds(layout.used[half], spare), :] = jnp.zeros((spare, LANES), jnp.float32)


def dense_rows(rows, width):
    full = width // LANES
    left = width - full * LANES
    beside = LANES // left
    group = -(-rows // (8 * beside)) * 8
    return full, left, beside, group, rows * (full + 1) + group


def dense_kernel(field_ref, basis_ref, out_ref):
    blocks, rows, width = field_ref.shape
    full, left, beside, group, _ = dense_rows(rows, width)
    base = (full + 1) * rows
    for block in range(blocks):
        for part in range(full):
            out_ref[block, pl.ds(part * rows, rows), :] = field_ref[block, :, part * LANES : (part + 1) * LANES]
        out_ref[block, pl.ds(full * rows, rows), :] = basis_ref[...]
        for part in range(beside):
            some = min(group, rows - part * group)
            lanes = slice(part * left, (part + 1) * left)
            piece = field_ref[block, pl.ds(part * group, some), full * LANES : width]
            out_ref[block, pl.ds(base, some), lanes] = piece
            if some < group:
                out_ref[block, pl.ds(base + some, group - some), lanes] = jnp.zeros((group - some, left), jnp.float32)


def gram_kernel(
    layout, dense_ref, keep_ref, send_ref, core_ref,
    field, basis, field_high, field_low, left_side, right_side, packed,
):
    blocks = dense_ref.shape[0]
    first, width = field.shape
    rank = basis.shape[1]
    rows = first // blocks
    full, left, beside, group, _ = dense_rows(rows, width)
    base = (full + 1) * rows
    for owner in range(blocks):
        own = owner * rows
        for part in range(full):
            field[pl.ds(own, rows), part * LANES : (part + 1) * LANES] = dense_ref[owner, pl.ds(part * rows, rows), :]
        basis[pl.ds(own, rows), :] = dense_ref[owner, pl.ds(full * rows, rows), :]
        for part in range(beside):
            some = min(group, rows - part * group)
            piece = dense_ref[owner, pl.ds(base, some), part * left : (part + 1) * left]
            field[pl.ds(own + part * group, some), full * LANES : width] = piece
    high, low = halves(field[...])
    field_high[...] = high
    field_low[...] = low
    basis_high, basis_low = halves(basis[...].T)
    core = dot(basis_high, high) + (dot(basis_high, low) + dot(basis_low, high))
    core_ref[...] = core
    high, low = halves(core.T)
    left_side[:, 0:rank] = high
    left_side[:, rank : 2 * rank] = low
    right_side[:, 0:rank] = high
    right_side[:, rank : 2 * rank] = high

    def field_product(rows, start, columns):
        lh, ll = field_high[pl.ds(0, rows), :], field_low[pl.ds(0, rows), :]
        rh, rl = field_high[pl.ds(start, columns), :], field_low[pl.ds(start, columns), :]
        return dot_rows(lh, rh) + (dot_rows(lh, rl) + dot_rows(ll, rh))

    def core_product(rows, start, columns):
        here, there = pl.ds(0, rows), pl.ds(start, columns)
        both = dot_rows(left_side[here, :], right_side[there, :])
        return both + dot_rows(left_side[here, 0:rank], left_side[there, rank : 2 * rank])

    pack_gram(layout, field_product, packed, 0)
    pack_gram(layout, core_product, packed, 1)
    mine = lax.axis_index("c")
    keep_ref[...] = packed[mine]
    send_ref[...] = packed[1 - mine]


def sum_kernel(keep_ref, came_ref, out_ref, sums, sent):
    count = sent.shape[0]
    some = sums.shape[0] // count
    moves = []
    for step in range(count):
        rows = pl.ds(step * some, some)
        sums[rows, :] = keep_ref[rows, :] + came_ref[rows, :]
        move = pltpu.make_async_copy(sums.at[rows, :], out_ref.at[rows, :], sent.at[step])
        move.start()
        moves.append(move)
    for move in moves:
        move.wait()


def parts_kernel(core_ref, after_ref, *out_refs):
    owned = out_refs[0].shape[0]
    for step, out_ref in enumerate(out_refs):
        owner = lax.rem(lax.axis_index("x") + step, len(out_refs))
        out_ref[...] = core_ref[pl.ds(pl.multiple_of(owner * owned, 8), owned), :]


def rows_kernel(*refs):
    came, (out_ref, ordered) = refs[:-2], refs[-2:]
    count = len(came)
    for step, ref in enumerate(came):
        ordered[lax.rem(lax.axis_index("x") + count - step, count)] = ref[...]
    for owner in range(count):
        out_ref[:, owner, :] = ordered[owner]


def unpack_rows(layout, packed, half, block, out_ref, scale):
    full, left = layout.full, layout.left
    last = pl.ds(full * LANES, left)
    if block == full:
        for column in range(full):
            piece = packed[half, pl.ds(layout.strip + column * left, left), :]
            out_ref[last, pl.ds(column * LANES, LANES)] = piece * scale
        corner = packed[half, pl.ds(layout.strip + full * left, left), :] * scale
        out_ref[last, last] = corner[:, 0:left]
        return
    rows = pl.ds(block * LANES, LANES)
    for column in range(full):
        columns = pl.ds(column * LANES, LANES)
        if column > block:
            out_ref[rows, columns] = packed[half, pl.ds(layout.above[column] + block * LANES, LANES), :] * scale
        elif column < block:
            tile = packed[half, pl.ds(layout.above[block] + column * LANES, LANES), :] * scale
            out_ref[rows, columns] = tile.T
        else:
            into, row = layout.fold[block]
            upper = packed[into, pl.ds(row + half * FOLD, FOLD), :] * scale
            lower = packed[into, pl.ds(row + 2 * FOLD, FOLD), :] * scale
            if half == 0:
                lower = pltpu.roll(lower, FOLD, 1)
            turned = jnp.concatenate([upper, upper], axis=0).T[FOLD:]
            out_ref[pl.ds(block * LANES, FOLD), columns] = upper
            out_ref[pl.ds(block * LANES + FOLD, FOLD), columns] = jnp.where(lane_below(FOLD), turned, lower)
    piece = packed[half, pl.ds(layout.strip + block * left, left), :] * scale
    out_ref[rows, last] = piece.T


def unpack_kernel(
    layout, orders, scale_one, scale_two, own_ref, other_ref, one_ref, two_ref, packed, came, whole_one, whole_two, sent
):
    width = layout.width
    mine = lax.axis_index("c")
    packed[mine] = own_ref[...]
    packed[1 - mine] = other_ref[...]
    for half in range(2):
        chunk = layout.rows // len(orders[half])
        if orders[half] == sorted(orders[half]):
            continue
        came[...] = packed[half]
        for place, source in enumerate(orders[half]):
            packed[half, pl.ds(place * chunk, chunk), :] = came[pl.ds(source * chunk, chunk), :]
    moves = []
    for block in range(layout.full + 1):
        unpack_rows(layout, packed, 1, block, whole_two, scale_two)
        rows = pl.ds(block * LANES, min(LANES, width - block * LANES))
        move = pltpu.make_async_copy(whole_two.at[rows, :], two_ref.at[rows, :], sent.at[block])
        move.start()
        moves.append(move)
    place = lax.axis_index("x")
    owned = one_ref.shape[0]
    for owner in range(width // owned):

        @pl.when(place == owner)
        def _():
            for block in range(owner * owned // LANES, ((owner + 1) * owned - 1) // LANES + 1):
                unpack_rows(layout, packed, 0, block, whole_one, scale_one)

    rows = pl.ds(pl.multiple_of(place * owned, 8), owned)
    move = pltpu.make_async_copy(whole_one.at[rows, :], one_ref, sent.at[layout.full + 1])
    move.start()
    moves.append(move)
    for move in moves:
        move.wait()


def exchange(parts, axes, groups=None):
    return lax.all_to_all(parts, axes, 0, 0, axis_index_groups=groups, tiled=True)


def copies(value, count):
    return jnp.broadcast_to(value[None], (count,) + value.shape)


def cost(flops, moved):
    return pl.CostEstimate(flops=flops, transcendentals=0, bytes_accessed=moved)


def both_groups(sizes):
    shape = tuple(sizes.values())
    index = np.arange(np.prod(shape)).reshape(shape)

    def short(core):
        return [index[:, b, d, :, core] for b, d in np.ndindex(shape[1], shape[2])]

    def rest(core):
        return [index[a, :, :, e, core] for a, e in np.ndindex(shape[0], shape[3])]

    near = short(0) + [index[a, :, d, e, 1] for a, d, e in np.ndindex(shape[0], shape[2], shape[3])]
    far = rest(0) + [index[:, b, :, :, 1] for b in range(shape[1])]
    groups = [near, far, short(0) + short(1), rest(0) + rest(1)]
    chunks = np.arange(np.prod(shape[:4])).reshape(shape[0], shape[3], shape[1], shape[2])
    orders = [sorted(chunks.reshape(-1).tolist()), chunks.transpose(2, 0, 3, 1).reshape(-1).tolist()]
    return [[group.reshape(-1).tolist() for group in part] for part in groups], orders


def local(sizes, tensor, basis):
    gx = sizes["x"]
    slices_here, rows_here, second = tensor.shape
    first = rows_here * gx
    rank = basis.shape[1]
    axes = tuple(sizes)
    (near, far, back_near, back_far), orders = both_groups(sizes)
    near_count, far_count = len(near[0]), len(far[0])
    slices_all = slices_here * near_count * far_count // gx * sizes["c"]
    layout = Layout(first, 8 * near_count * far_count)
    dense = dense_rows(rows_here, second)[-1]
    swap = [(i, sizes["c"] - 1 - i) for i in range(sizes["c"])]
    f32, bf16 = jnp.float32, jnp.bfloat16

    blocks = pl.pallas_call(
        dense_kernel,
        out_shape=jax.ShapeDtypeStruct((slices_here, dense, LANES), f32),
        in_specs=[VMEM, VMEM],
        out_specs=VMEM,
        compiler_params=ROOM,
        name="dense_blocks",
    )(tensor, basis)
    blocks = exchange(blocks, "x")
    half_shape = jax.ShapeDtypeStruct((layout.rows, LANES), f32)
    keep, send, core = pl.pallas_call(
        functools.partial(gram_kernel, layout),
        out_shape=(half_shape, half_shape, jax.ShapeDtypeStruct((rank, second), f32)),
        in_specs=[VMEM],
        out_specs=(VMEM, VMEM, VMEM),
        scratch_shapes=[
            pltpu.VMEM((first, second), f32),
            pltpu.VMEM((first, rank), f32),
            pltpu.VMEM((first, second), bf16),
            pltpu.VMEM((first, second), bf16),
            pltpu.VMEM((second, 2 * rank), bf16),
            pltpu.VMEM((second, 2 * rank), bf16),
            pltpu.VMEM((2, layout.rows, LANES), f32),
        ],
        compiler_params=ROOM,
        cost_estimate=cost(5 * first * first * second, 12 * first * second),
        name="local_grams",
    )(blocks)

    came = lax.ppermute(send, "c", swap)
    sums = pl.pallas_call(
        sum_kernel,
        out_shape=half_shape,
        in_specs=[VMEM, VMEM],
        out_specs=ANY,
        scratch_shapes=[pltpu.VMEM((layout.rows, LANES), f32), pltpu.SemaphoreType.DMA((8,))],
        compiler_params=ROOM,
        name="sum_of_cores",
    )(keep, came)
    owned = rank // gx
    core_parts = pl.pallas_call(
        parts_kernel,
        out_shape=[jax.ShapeDtypeStruct((owned, second), f32)] * gx,
        in_specs=[VMEM, ANY],
        out_specs=[VMEM] * gx,
        compiler_params=ROOM,
        cost_estimate=cost(rank * second, 8 * rank * second),
        name="core_parts",
    )(core, came)
    came_core = [core_parts[0]] * gx
    for step in sorted(range(1, gx), key=lambda step: min(step, gx - step)):
        shift = [(i, (i + step) % gx) for i in range(gx)]
        came_core[step] = lax.ppermute(core_parts[step], "x", shift)
    part = exchange(sums.reshape(near_count, -1, LANES), axes, near)
    order = sorted(range(gx), key=lambda step: -min(step, gx - step))
    part, *tied = lax.optimization_barrier((part, *[came_core[step] for step in order]))
    came_core = [tied[order.index(step)] for step in range(gx)]
    part = exchange(jnp.sum(part, axis=0).reshape(far_count, -1, LANES), axes, far)
    core_out = pl.pallas_call(
        rows_kernel,
        out_shape=jax.ShapeDtypeStruct((owned, gx, second), f32),
        in_specs=[VMEM] * gx,
        out_specs=VMEM,
        scratch_shapes=[pltpu.VMEM((gx, owned, second), f32)],
        compiler_params=ROOM,
        cost_estimate=cost(rank * second, 8 * rank * second),
        name="core_rows",
    )(*came_core)
    part = exchange(copies(jnp.sum(part, axis=0), far_count), axes, back_far).reshape(-1, LANES)
    own = exchange(copies(part, near_count), axes, back_near).reshape(-1, LANES)
    other = lax.ppermute(own, "c", swap)

    gram_one, gram_two = pl.pallas_call(
        functools.partial(unpack_kernel, layout, orders, 1.0 / (slices_all * second), 1.0 / (slices_all * rank)),
        out_shape=(
            jax.ShapeDtypeStruct((rows_here, first), f32),
            jax.ShapeDtypeStruct((second, second), f32),
        ),
        in_specs=[VMEM, VMEM],
        out_specs=(ANY, ANY),
        scratch_shapes=[
            pltpu.VMEM((2, layout.rows, LANES), f32),
            pltpu.VMEM((layout.rows, LANES), f32),
            pltpu.VMEM((first, first), f32),
            pltpu.VMEM((second, second), f32),
            pltpu.SemaphoreType.DMA((layout.full + 2,)),
        ],
        compiler_params=ROOM,
        name="mirror",
    )(own, other)
    return gram_one, core_out, gram_two


def solution(mesh):
    gx, rest = mesh.devices.shape
    sizes = {"x": gx, "y": 8, "zh": rest // 32, "zl": 2, "c": 2}
    fine = Mesh(mesh.devices.reshape(tuple(sizes.values())), tuple(sizes))
    spread = ("y", "zh", "zl", "c")
    in_specs = (P(spread, "x", None), P("x", None))
    out_specs = (P("x", None), P("x", spread, None), P())
    return jax.shard_map(
        functools.partial(local, sizes), mesh=fine, in_specs=in_specs, out_specs=out_specs, check_vma=False
    )
```
